32 devices in a mesh: dp: 8 (over z, x), mp: 4 (over y, core).
Axes of the slice: x: 2, y: 2, z: 4, core: 2. Of those that a mesh axis runs over, the one named last changes fastest.
Arguments:
- features: bfloat16 [32768, 256], P('dp'), may hold values from -6 to 6
- lengths: int32 [16], P('dp'), may hold values from 64 to 256, as said below
- routes: int32 [512, 1], P('dp'), may hold values from 0 to 7; in each aligned block of 64 rows (0 to 63, 64 to 127, ...) at most 16 rows name the same one
- res_in_weight: bfloat16 [768, 128], replicated, may hold values from -0.21875 to 0.21875
- res_out_weight: bfloat16 [128, 256], replicated, may hold values from -0.5 to 0.5
- down_weight: bfloat16 [4096, 512], P(None, 'mp'), may hold values from -0.09375 to 0.09375
- proj_weight: bfloat16 [512, 256], P('mp'), may hold values from -0.25 to 0.25
- cotangent: bfloat16 [1024, 2048], P('dp', 'mp'), may hold values from -0.25 to 0.25
Outputs:
- packed: bfloat16 [1024, 2048], P('dp', 'mp')
- grad_res_in: float32 [768, 128], replicated
- grad_res_out: float32 [128, 256], replicated
- grad_down: float32 [4096, 512], P(None, 'mp')
- grad_proj: float32 [512, 256], P('mp')
The draws below stay inside these ranges and needn't reach their ends.
Inputs may be any that keep to these rules, and one draw needn't show every extreme that they name: `lengths`: latent frames of each utterance; some utterance has exactly 256 and some exactly 64. `routes`: among the pieces of one index of dp, at most 16 name the same packed shard.
All inputs are finite; a program needn't handle non-finite values.
Results may differ from the reference program's by a relative error of at most 0.014.
Values may be sent and summed in bfloat16 or wider, within the bound.
No kernel may reach another device: no remote copies, remote signals or barrier semaphores. Data moves between devices by JAX's collectives and lax.ppermute only.
A program may use at most 128 MiB of HBM per device.

```python
import math
import jax
import jax.numpy as jnp
import numpy as np
from jax import lax

C_IN = 256
C_HID = 128
C_OUT = 512
LAT = 256
STRIDE = 8
KERNEL = 16
DILATION_SPAN = 9
PIECE = 8
LMAX = 256
UTT_DEV = 2
ROWS_UTT = 2048
UTTS = 16
PIECE_DEV = 64
CAP = 16
PIECES = 512
SLOTS = 128
N_DP = 8
N_MP = 4


def draw_lengths(key, part):
    first_key, second_key, third_key = jax.random.split(key, 3)
    values = jax.random.randint(first_key, (UTTS,), LMAX // 4, LMAX + 1)
    longest = jax.random.randint(second_key, (), 0, UTTS)
    offset = jax.random.randint(third_key, (), 1, UTTS)
    shortest = (longest + offset) % UTTS
    positions = jnp.arange(UTTS)
    values = jnp.where(positions == longest, LMAX, values)
    values = jnp.where(positions == shortest, LMAX // 4, values)
    return values.astype(jnp.int32)


def levels(key, extent, cuts, low, top_value):
    factor_of, own = 1.0, jax.random.fold_in(key, 6)
    for position, blocks in cuts:
        heights = jnp.exp(jax.random.uniform(jax.random.fold_in(own, position), (blocks,), jnp.float32, low / len(cuts), top_value / len(cuts)))
        factor_of = factor_of * jnp.repeat(heights, extent[position] // blocks).reshape([-1 if axis == position else 1 for axis in range(len(extent))])
    return factor_of


def assign_block(key, own, number, rows, count, top, limit, lean):
    order = jax.random.permutation(key, count)
    heavy_load, usual = portions_of(count, rows * top, limit, lean, True), portions_of(count, rows * top, limit, lean, False)
    places = jnp.arange(count)

    def named(sizes, rotation):
        used = int((sizes > 0).sum())
        fixed = max(1, used // 4)
        moved = fixed + (places - fixed + rotation * (used - fixed)) % max(1, count - fixed)
        return jnp.zeros((count,), jnp.int32).at[order[jnp.where(places < fixed, places, moved)]].set(jnp.asarray(sizes, jnp.int32))

    sizes = jnp.where(number % 4 == 0, named(heavy_load, number // 4), named(usual, number - number // 4 - 1))
    mixed = jax.random.permutation(jax.random.fold_in(own, 3), count)
    donor, sink = mixed[0:count // 2 * 2:2], mixed[1:count // 2 * 2:2]
    slack = jnp.minimum(sizes[donor] - 1, limit - sizes[sink]) // 2
    slack = jnp.where((donor == order[0]) | (sink == order[0]) | (sizes[sink] == 0), 0, jnp.maximum(slack, 0))
    moved = jax.random.randint(jax.random.fold_in(own, 4), (count // 2,), 0, 1 << 20) % (slack + 1)
    sizes = sizes.at[donor].add(-moved).at[sink].add(moved)
    members = jnp.searchsorted(jnp.cumsum(sizes), jnp.arange(rows * top), side="right").astype(jnp.int32)
    grid = members.reshape(top, rows).T
    grid = grid[jax.random.permutation(jax.random.fold_in(own, 1), rows)]
    rotation = jax.random.randint(jax.random.fold_in(own, 2), (rows, 1), 0, top)
    return jnp.take_along_axis(grid, (jnp.arange(top)[None, :] + rotation) % top, axis=1)


def portions_of(amount, total, most, slope, full):
    weights = [(1 << 20) // math.isqrt(grade ** slope) + 1 for grade in range(1, amount + 1)]
    largest = most if full else min(most, max(-(-total // amount), total * weights[0] // sum(weights)))
    least = 1 if total - largest >= amount - 1 else 0
    counts, rest = [largest] + [least] * (amount - 1), total - largest - least * (amount - 1)
    while rest > 0:
        free = [i for i in range(1, amount) if counts[i] < largest] or [i for i in range(1, amount) if counts[i] < most]
        mass, budget = sum([weights[i] for i in free]), rest
        for i in free:
            extra = min(most - counts[i], max(1, budget * weights[i] // mass), rest)
            counts[i] = counts[i] + extra
            rest = rest - extra
    return np.array(counts)


def centred(stream_key, dims, scale, bound, cuts=(), kind=jnp.bfloat16):
    array = jax.random.normal(stream_key, dims, jnp.float32) * scale
    if len(cuts) > 0:
        array = levels(stream_key, dims, cuts, -0.22, 0.18) * array
    return jnp.clip(array, min=-bound, max=bound).astype(kind)


def setup_inputs(seed: int = 0) -> dict:
    splits = jax.random.split(jax.random.key(seed), 9)
    features = centred(splits[0], (UTTS * ROWS_UTT, C_IN), 1.0, 6.0, ((0, 8),))
    lengths = draw_lengths(jax.random.fold_in(splits[8], 71), 0)
    routes_keys = jax.random.split(jax.random.fold_in(splits[2], 1), PIECES // PIECE_DEV)
    routes_turns = jax.random.permutation(jax.random.fold_in(splits[2], 3), PIECES // PIECE_DEV)
    routes = jax.vmap(lambda own, number: assign_block(jax.random.fold_in(splits[2], 2), own, number, PIECE_DEV, N_DP, 1, CAP, 1))(routes_keys, routes_turns).reshape((PIECES, 1))
    res_in_weight = centred(splits[3], (3 * C_IN, C_HID), (3 * C_IN) ** -0.5, 0.21875)
    res_out_weight = centred(splits[4], (C_HID, C_IN), C_HID ** -0.5, 0.5)
    down_weight = centred(splits[5], (KERNEL * C_IN, C_OUT), (KERNEL * C_IN) ** -0.5, 0.09375, ((1, 4),))
    proj_weight = centred(splits[6], (C_OUT, LAT), C_OUT ** -0.5, 0.25, ((0, 4),))
    cotangent = centred(splits[7], (N_DP * SLOTS, PIECE * LAT), (1.0 / (PIECES * PIECE) ** 0.5), 0.25, ((0, 8), (1, 4)))
    return {"features": features, "lengths": lengths, "routes": routes, "res_in_weight": res_in_weight, "res_out_weight": res_out_weight, "down_weight": down_weight, "proj_weight": proj_weight, "cotangent": cotangent}


def elu_value(values):
    return jnp.where(values > 0, values, jnp.expm1(jnp.minimum(values, 0.0)))


def elu_slope(values):
    return jnp.where(values > 0, 1.0, jnp.exp(jnp.minimum(values, 0.0)))


def dilated(padded_rows, weight, total_rows):
    channel_count = padded_rows.shape[-1]
    running = jnp.zeros((padded_rows.shape[0], total_rows, weight.shape[1]), jnp.float32)
    for kernel_offset in range(3):
        sliding_window = padded_rows[:, kernel_offset * DILATION_SPAN:kernel_offset * DILATION_SPAN + total_rows].astype(jnp.float32)
        tap_rows = weight[kernel_offset * channel_count:(kernel_offset + 1) * channel_count].astype(jnp.float32)
        running = running + jnp.einsum("urc,ch->urh", sliding_window, tap_rows)
    return running


def forward_block(feature_rows, length_rows, res_in_weight, res_out_weight, down_weight, proj_weight):
    utt_count = length_rows.shape[0]
    total_rows = STRIDE * LMAX
    waveform = feature_rows.reshape(utt_count, total_rows, C_IN)
    row_mask = (jnp.arange(total_rows, dtype=jnp.int32)[None, :] < STRIDE * length_rows[:, None])[:, :, None]
    frame_mask = (jnp.arange(LMAX, dtype=jnp.int32)[None, :] < length_rows[:, None])[:, :, None]
    waveform = jnp.where(row_mask, waveform, jnp.zeros_like(waveform))
    input_activation = elu_value(waveform.astype(jnp.float32)).astype(jnp.bfloat16)
    padded_rows = jnp.pad(input_activation, ((0, 0), (DILATION_SPAN, DILATION_SPAN), (0, 0)))
    hidden = dilated(padded_rows, res_in_weight, total_rows)
    act_hid = elu_value(hidden).astype(jnp.bfloat16)
    branch = jnp.einsum("urh,hc->urc", act_hid.astype(jnp.float32), res_out_weight.astype(jnp.float32))
    section_out = jnp.where(row_mask, waveform.astype(jnp.float32) + branch, 0.0).astype(jnp.bfloat16)
    act_section = elu_value(section_out.astype(jnp.float32)).astype(jnp.bfloat16)
    tap_width = STRIDE * C_IN
    blocks = jnp.pad(act_section, ((0, 0), (STRIDE // 2, STRIDE // 2), (0, 0))).reshape(utt_count, LMAX + 1, tap_width)
    lower_taps = blocks[:, :-1].astype(jnp.float32)
    upper_taps = blocks[:, 1:].astype(jnp.float32)
    down_out = jnp.einsum("ujk,ko->ujo", lower_taps, down_weight[:tap_width].astype(jnp.float32))
    down_out = down_out + jnp.einsum("ujk,ko->ujo", upper_taps, down_weight[tap_width:].astype(jnp.float32))
    act_down = elu_value(down_out).astype(jnp.bfloat16)
    projected = jnp.einsum("ujo,ol->ujl", act_down.astype(jnp.float32), proj_weight.astype(jnp.float32))
    latent = jnp.where(frame_mask, projected, 0.0).astype(jnp.bfloat16)
    saved = (row_mask, frame_mask, padded_rows, hidden, act_hid, section_out, lower_taps, upper_taps, down_out, act_down)
    return latent, saved


def backward_block(feature_rows, length_rows, grad_rows, res_in_weight, res_out_weight, down_weight, proj_weight):
    latent, saved = forward_block(feature_rows, length_rows, res_in_weight, res_out_weight, down_weight, proj_weight)
    row_mask, frame_mask, padded_rows, hidden, act_hid, section_out, lower_taps, upper_taps, down_out, act_down = saved
    utt_count = length_rows.shape[0]
    total_rows = STRIDE * LMAX
    tap_width = STRIDE * C_IN
    g_latent = jnp.where(frame_mask, grad_rows, jnp.zeros_like(grad_rows)).astype(jnp.float32)
    grad_proj = jnp.einsum("ujo,ujl->ol", act_down.astype(jnp.float32), g_latent)
    g_down = (jnp.einsum("ujl,ol->ujo", g_latent, proj_weight.astype(jnp.float32)) * elu_slope(down_out)).astype(jnp.bfloat16)
    g_down32 = g_down.astype(jnp.float32)
    grad_down = jnp.concatenate([jnp.einsum("ujk,ujo->ko", lower_taps, g_down32), jnp.einsum("ujk,ujo->ko", upper_taps, g_down32)], 0)
    group_width = C_OUT // N_MP
    g_section = jnp.zeros((utt_count, total_rows, C_IN), jnp.float32)
    for member in range(N_MP):
        g_group = g_down32[:, :, member * group_width:(member + 1) * group_width]
        low_back = jnp.einsum("ujo,ko->ujk", g_group, down_weight[:tap_width, member * group_width:(member + 1) * group_width].astype(jnp.float32))
        high_back = jnp.einsum("ujo,ko->ujk", g_group, down_weight[tap_width:, member * group_width:(member + 1) * group_width].astype(jnp.float32))
        spread = jnp.pad(low_back, ((0, 0), (0, 1), (0, 0))) + jnp.pad(high_back, ((0, 0), (1, 0), (0, 0)))
        group_rows = spread.reshape(utt_count, total_rows + STRIDE, C_IN)[:, STRIDE // 2:STRIDE // 2 + total_rows]
        rounded = lax.optimization_barrier(group_rows.astype(jnp.bfloat16))
        g_section = g_section + rounded.astype(jnp.float32)
    g_branch = jnp.where(row_mask, g_section * elu_slope(section_out.astype(jnp.float32)), 0.0).astype(jnp.bfloat16).astype(jnp.float32)
    grad_res_out = jnp.einsum("urh,urc->hc", act_hid.astype(jnp.float32), g_branch)
    g_hidden = (jnp.einsum("urc,hc->urh", g_branch, res_out_weight.astype(jnp.float32)) * elu_slope(hidden)).astype(jnp.bfloat16).astype(jnp.float32)
    tap_grads = []
    for kernel_offset in range(3):
        sliding_window = padded_rows[:, kernel_offset * DILATION_SPAN:kernel_offset * DILATION_SPAN + total_rows].astype(jnp.float32)
        tap_grads.append(jnp.einsum("urc,urh->ch", sliding_window, g_hidden))
    grad_res_in = jnp.concatenate(tap_grads, 0)
    return grad_res_in, grad_res_out, grad_down, grad_proj


def piece_rows(routes):
    targets = routes[:, 0].astype(jnp.int32)
    chosen = (targets[:, None] == jnp.arange(N_DP, dtype=jnp.int32)[None, :]).astype(jnp.int32)
    blocks = chosen.reshape(N_DP, PIECE_DEV, N_DP)
    earlier = (jnp.cumsum(blocks, axis=1) - blocks).astype(jnp.int32)
    slot_rank = jnp.sum(earlier * blocks, axis=2).reshape(-1).astype(jnp.int32)
    source = (jnp.arange(PIECES, dtype=jnp.int32) // PIECE_DEV).astype(jnp.int32)
    return (targets * (N_DP * CAP) + source * CAP + slot_rank).astype(jnp.int32)


def reference(features, lengths, routes, res_in_weight, res_out_weight, down_weight, proj_weight, cotangent):
    feature_blocks = features.reshape(N_DP, UTT_DEV * ROWS_UTT, C_IN)
    length_blocks = lengths.reshape(N_DP, UTT_DEV)

    def forward_only(pair):
        return forward_block(pair[0], pair[1], res_in_weight, res_out_weight, down_weight, proj_weight)[0]

    latents = lax.map(forward_only, (feature_blocks, length_blocks))
    pieces = latents.reshape(PIECES, PIECE * LAT)
    target_rows = piece_rows(routes)
    packed = jnp.zeros((N_DP * SLOTS, PIECE * LAT), jnp.bfloat16).at[target_rows].set(pieces)
    grad_pieces = cotangent[target_rows].reshape(N_DP, UTT_DEV, LMAX, LAT)

    def accumulate(carry, triple):
        parts = backward_block(triple[0], triple[1], triple[2], res_in_weight, res_out_weight, down_weight, proj_weight)
        return tuple(held + part for held, part in zip(carry, parts)), None

    start = (jnp.zeros((3 * C_IN, C_HID), jnp.float32), jnp.zeros((C_HID, C_IN), jnp.float32),
             jnp.zeros((KERNEL * C_IN, C_OUT), jnp.float32), jnp.zeros((C_OUT, LAT), jnp.float32))
    totals, unused = lax.scan(accumulate, start, (feature_blocks, length_blocks, grad_pieces))
    return (packed, totals[0], totals[1], totals[2], totals[3])
```

```python
import functools
import jax
import jax.numpy as jnp
from jax import lax
from jax.experimental import pallas as pl
from jax.experimental.pallas import tpu as pltpu
from jax.sharding import PartitionSpec as P

STRIDE = 8
LANES = 128
BF = jnp.bfloat16
F32 = jnp.float32
VMEM_LIMIT = 56 << 20


def elu(v):
    return jnp.where(v > 0, v, jnp.exp(jnp.minimum(v, 0.0)) - 1.0)


def slope(v):
    return jnp.where(v > 0, 1.0, jnp.exp(jnp.minimum(v, 0.0)))


def mm(a, b):
    return jnp.dot(a, b, preferred_element_type=F32)


def mm_nt(a, b):
    return lax.dot_general(a, b, (((1,), (1,)), ((), ())), preferred_element_type=F32)


def mm_tn(a, b):
    return lax.dot_general(a, b, (((0,), (0,)), ((), ())), preferred_element_type=F32)


def shift(v, s):
    n = v.shape[0]
    rows = lax.broadcasted_iota(jnp.int32, v.shape, 0)
    rolled = pltpu.roll(v, (-s) % n, 0)
    keep = rows < n - s if s > 0 else rows >= -s
    return jnp.where(keep, rolled, 0.0)


def spread(ref, value):
    for i in range(ref.shape[0]):
        ref[i] = value[:, i * LANES : (i + 1) * LANES]


def every(ref, start, size):
    return jnp.concatenate(
        [ref[i, pl.ds(start, size, stride=STRIDE), :] for i in range(ref.shape[0])], 1
    )


def call(kernel, outs, ins, scratch=(), prefetch=None, specs=None, name=None, flops=0):
    whole = [
        pl.BlockSpec(a.shape, functools.partial(lambda n, *_: (0,) * n, a.ndim)) for a in ins
    ]
    for i, spec in (specs or {}).items():
        whole[i] = spec
    return pl.pallas_call(
        kernel,
        out_shape=[jax.ShapeDtypeStruct(s, d) for s, d in outs],
        grid_spec=pltpu.PrefetchScalarGridSpec(
            num_scalar_prefetch=1,
            grid=(1,),
            in_specs=whole,
            out_specs=[
                pl.BlockSpec(s, functools.partial(lambda n, *_: (0,) * n, len(s))) for s, d in outs
            ],
            scratch_shapes=list(scratch),
        ),
        compiler_params=pltpu.CompilerParams(vmem_limit_bytes=VMEM_LIMIT),
        cost_estimate=pl.CostEstimate(flops=flops, transcendentals=0, bytes_accessed=1 << 20),
        name=name,
    )(prefetch, *ins)


def forward_kernel(
    sc, feat, wi, wo, dwa, dwb, pa, pb,
    a1, a2, sec, ahid, shid, adown, sdown, lat_send, lat_keep,
    xs, ys, ls,
):
    frames, ch = a1.shape[1], a1.shape[2]
    hid = wo.shape[0]
    length, y = sc[0], sc[2]
    spread(xs, feat[...].astype(F32))
    wcat = jnp.concatenate([wi[k * ch : (k + 1) * ch, :] for k in range(3)], 1)
    live = lax.broadcasted_iota(jnp.int32, (frames, ch), 0) < length

    def signal(p):
        return jnp.where(live, every(xs, p, frames), 0.0)

    for p in range(STRIDE):
        act = elu(signal(p)).astype(BF)
        a1[p] = act
        ys[p] = mm(act, wcat)
    down = jnp.zeros((frames, 2 * dwa.shape[1]), F32)
    before = jnp.zeros_like(down)
    after = jnp.zeros_like(down)

    def tap(k):
        return jnp.concatenate([dwa[k * ch : (k + 1) * ch, :], dwb[k * ch : (k + 1) * ch, :]], 1)

    for p in range(STRIDE):
        left = shift(ys[(p - 1) % STRIDE, :, :hid], -1 if p > 0 else -2)
        right = shift(ys[(p + 1) % STRIDE, :, 2 * hid :], 1 if p < STRIDE - 1 else 2)
        hidden = left + ys[p, :, hid : 2 * hid] + right
        act_hid = elu(hidden).astype(BF)
        ahid[p] = act_hid
        shid[p] = slope(hidden).astype(BF)
        section = jnp.where(live, signal(p) + mm(act_hid, wo[...]), 0.0).astype(BF)
        sec[p] = section
        act = elu(section.astype(F32)).astype(BF)
        a2[p] = act
        half = STRIDE // 2
        down = down + mm(act, tap(p + half))
        if p < half:
            after = after + mm(act, tap(p + 3 * half))
        else:
            before = before + mm(act, tap(p - half))
    down = down + shift(before, -1) + shift(after, 1)
    act_down = elu(down).astype(BF)
    adown[...] = act_down
    sdown[...] = slope(down)
    proj = jnp.concatenate([pa[...], pb[...]], 0)
    spread(ls, jnp.where(live, mm(act_down, proj), 0.0))
    pieces = frames // STRIDE
    lat = ch
    for j in range(STRIDE // 2):
        half = STRIDE // 2
        cols = slice(j * lat, (j + 1) * lat)
        lat_send[:, cols] = every(ls, half * (1 - y) + j, pieces).astype(BF)
        lat_keep[:, cols] = every(ls, half * y + j, pieces).astype(BF)


def placing_of(targets, slots, capacity, groups):
    pieces = targets.shape[0]
    lanes = lax.broadcasted_iota(jnp.int32, (pieces, 128), 1)
    hit = targets == lanes
    chosen = jnp.where(hit, 1.0, 0.0)
    lower = (
        lax.broadcasted_iota(jnp.int32, (pieces, pieces), 0)
        > lax.broadcasted_iota(jnp.int32, (pieces, pieces), 1)
    )
    earlier = mm(jnp.where(lower, 1.0, 0.0).astype(BF), chosen.astype(BF))
    rank = jnp.sum(earlier * chosen, axis=1, keepdims=True).astype(jnp.int32)
    slot = targets * capacity + rank
    ids = lax.broadcasted_iota(jnp.int32, (pieces, slots), 1)
    return jnp.where(slot == ids, 1.0, 0.0).astype(BF)


def pick_kernel(capacity, groups, sc, routes, returned, own, other, buf):
    pieces = routes.shape[0]
    placing = placing_of(routes[...], returned.shape[0], capacity, groups)
    buf[...] = mm(placing, returned[...])
    half = pieces // 2
    own[...] = buf[pl.ds(pl.multiple_of(sc[1] * half, half), half), :].astype(BF)
    other[...] = buf[pl.ds(pl.multiple_of((1 - sc[1]) * half, half), half), :].astype(BF)


def place_kernel(capacity, groups, sc, routes, mine, theirs, outgoing, buf):
    pieces = routes.shape[0]
    half = pieces // 2
    placing = placing_of(routes[...], outgoing.shape[0], capacity, groups)
    buf[pl.ds(pl.multiple_of(sc[1] * half, half), half), :] = mine[...].astype(F32)
    buf[pl.ds(pl.multiple_of((1 - sc[1]) * half, half), half), :] = theirs[...].astype(F32)
    outgoing[...] = mm_tn(placing, buf[...].astype(BF)).astype(BF)


def section_grad(sc, gd, gshift, wa, wb, part, j, ch):
    half = STRIDE // 2
    first = part * half + j + half
    second = jnp.where(part == 0, 3 * half + j, j)
    rows1 = pl.ds(pl.multiple_of(first * ch, ch), ch)
    rows2 = pl.ds(pl.multiple_of(second * ch, ch), ch)
    w1 = jnp.concatenate([wa[rows1, :], wb[rows1, :]], 1)
    w2 = jnp.concatenate([wa[rows2, :], wb[rows2, :]], 1)
    return mm_nt(gd, w1) + mm_nt(gshift, w2)


def moved(gd, part):
    g = gd.astype(F32)
    return jnp.where(part == 0, shift(g, -1), shift(g, 1)).astype(BF)


def latent_grad_kernel(
    sc, g_own, g_core, g_y, adown, sdown, pa, pb, dwa, dwb,
    gd_out, swap, gproj_keep, send, gl,
):
    frames = adown.shape[0]
    lat = pa.shape[1]
    width = pa.shape[0]
    ch = send.shape[2]
    pieces = g_own.shape[0]
    length, c, y = sc[0], sc[1], sc[2]
    m = 2 * y + c
    blocks = (
        (g_own[...], m),
        (g_core[...], 2 * y + 1 - c),
        (g_y[:, : 2 * lat], 2 * (1 - y) + c),
        (g_y[:, 2 * lat :], 2 * (1 - y) + 1 - c),
    )
    for block, owner in blocks:
        for j in range(2):
            for i in range(gl.shape[0]):
                at = j * lat + i * LANES
                gl[i, pl.ds(2 * owner + j, pieces, stride=STRIDE), :] = block[
                    :, at : at + LANES
                ].astype(F32)
    live = lax.broadcasted_iota(jnp.int32, (frames, lat), 0) < length
    g_latent = jnp.where(live, jnp.concatenate([gl[i] for i in range(gl.shape[0])], 1), 0.0)
    g_latent = g_latent.astype(BF)
    proj = jnp.concatenate([pa[...], pb[...]], 0)
    gd = (mm_nt(g_latent, proj) * sdown[...]).astype(BF)
    gd_out[...] = gd
    swap[:frames] = gd[:, width:]
    gproj = mm_tn(adown[...], g_latent)
    swap[frames : frames + width] = gproj[width:, :width].astype(BF)
    swap[frames + width :] = gproj[width:, width:].astype(BF)
    gproj_keep[:width] = gproj[:width, :width]
    gproj_keep[width:] = gproj[:width, width:]
    g2 = moved(gd, 1 - y)
    for j in range(STRIDE // 2):
        send[j] = section_grad(sc, gd, g2, dwa, dwb, 1 - y, j, ch).astype(BF)


def weight_grads(sc, a2a, a2b, ga, gb, part, j):
    half = STRIDE // 2
    p = part * half + j
    return mm_tn(a2a[p], ga) + mm_tn(a2b[p], gb)


def pair(g, part):
    return jnp.concatenate([g, moved(g, part)], 1)


def down_send_kernel(sc, a2a, a2b, gd, swap, gproj, send_u, send_s):
    frames = gd.shape[0]
    width = swap.shape[1]
    x = sc[3]
    ga = pair(gd[:, :width], x)
    gb = pair(swap[:frames], x)
    extra = send_s.shape[1] - send_u.shape[1]
    rows = send_u.shape[1]
    for j in range(STRIDE // 2):
        w = weight_grads(sc, a2a, a2b, ga, gb, x, j)
        send_u[j] = w[:, :width].astype(BF)
        send_s[j, :rows] = w[:, width:].astype(BF)
        at = pl.ds(pl.multiple_of(((1 - x) * 4 + j) * extra, extra), extra)
        send_s[j, rows:] = (gproj[at, :] + swap[pl.ds(pl.multiple_of(frames + ((1 - x) * 4 + j) * extra, extra), extra), :].astype(F32)).astype(BF)


def down_keep_kernel(sc, gd, swap, gproj, a2a, a2b, dwa, dwb, keep_u, keep_s, keep_g):
    frames = gd.shape[0]
    width = swap.shape[1]
    ch = keep_g.shape[2]
    x, y = sc[3], sc[2]
    part = 1 - x
    ga = pair(gd[:, :width], part)
    gb = pair(swap[:frames], part)
    extra = keep_s.shape[1] - keep_u.shape[1]
    rows = keep_u.shape[1]
    for j in range(STRIDE // 2):
        w = weight_grads(sc, a2a, a2b, ga, gb, part, j)
        keep_u[j] = w[:, :width]
        keep_s[j, :rows] = w[:, width:]
        at = pl.ds(pl.multiple_of((x * 4 + j) * extra, extra), extra)
        keep_s[j, rows:] = gproj[at, :] + swap[pl.ds(pl.multiple_of(frames + (x * 4 + j) * extra, extra), extra), :].astype(F32)
    full = gd[...]
    g2 = moved(full, y)
    for j in range(STRIDE // 2):
        keep_g[j] = section_grad(sc, full, g2, dwa, dwb, y, j, ch)


def residual_kernel(sc, keep, recv, sec, ahid, shid, wo, a1, send, kept, gh, buf):
    half = STRIDE // 2
    frames, ch = keep.shape[1], keep.shape[2]
    hid = wo.shape[0]
    length, c, y = sc[0], sc[1], sc[2]
    live = lax.broadcasted_iota(jnp.int32, (frames, ch), 0) < length
    g_out = jnp.zeros((hid, ch), F32)
    for j in range(half):
        g = keep[j] + recv[j].astype(F32)
        g_branch = jnp.where(live, g * slope(sec[j].astype(F32)), 0.0).astype(BF)
        g_out = g_out + mm_tn(ahid[j], g_branch)
        gh[j] = mm_nt(g_branch, wo[...]) * shid[j].astype(F32)
    taps = [jnp.zeros((ch, hid), F32) for _ in range(3)]
    for j in range(half):
        g = gh[j]
        p = y * half + j
        here = g.astype(BF)
        taps[1] = taps[1] + mm_tn(a1[p], here)
        down1 = shift(g, 1)
        up1 = shift(g, -1)
        if j == 0:
            down1 = jnp.where(y == 0, shift(g, 2), down1)
        if j == half - 1:
            up1 = jnp.where(y == 1, shift(g, -2), up1)
        taps[0] = taps[0] + mm_tn(a1[lax.rem(p + STRIDE - 1, STRIDE)], down1.astype(BF))
        taps[2] = taps[2] + mm_tn(a1[lax.rem(p + 1, STRIDE)], up1.astype(BF))
    for k in range(3):
        for i in range(ch // hid):
            buf[k * (ch // hid) + i] = taps[k][i * hid : (i + 1) * hid]
    for i in range(ch // hid):
        buf[3 * (ch // hid) + i] = g_out[:, i * hid : (i + 1) * hid]
    n = send.shape[0]
    for i in range(n):
        send[i] = buf[(1 - c) * n + i].astype(BF)
        kept[i] = buf[c * n + i]


def swap_bit(value, axis, bit):
    n = lax.axis_size(axis)
    return lax.ppermute(value, axis, [(i, i ^ bit) for i in range(n)])


def stages_of(n):
    found, bit = [], 2
    while bit < n:
        members = 4 if n // bit >= 4 else 2
        found.append((bit, members))
        bit *= members
    return found


def pick(stack, index):
    return lax.dynamic_index_in_dim(stack, index, 0, keepdims=False)


def reduce_rest(kept, received, me, stages):
    total = kept + received.astype(F32)
    for bit, members in stages:
        parts = total.reshape(members, -1, total.shape[-1])
        place = (me // bit) % members
        got = [swap_bit(pick(parts, place ^ k).astype(BF), "dp", bit * k) for k in range(1, members)]
        total = pick(parts, place)
        for g in got:
            total = total + g.astype(F32)
    return total.astype(BF)


def gather_rest(own, me, stages):
    for bit, members in reversed(stages):
        place = (me // bit) % members
        blocks = [own] + [swap_bit(own, "dp", bit * k) for k in range(1, members)]
        ordered = jnp.stack(blocks)
        own = jnp.concatenate([pick(ordered, place ^ k) for k in range(members)], 0)
    return own


def finish_kernel(sc, mine_u, mine_s, their_u, their_s, out, out_proj):
    x = sc[3]
    members, rows, width = mine_u.shape
    extra = mine_s.shape[1] - rows
    half = STRIDE // 2
    ch = rows
    per = out_proj.shape[0] // extra
    for u, s, part, xp in (
        (mine_u, mine_s, 1 - x, x),
        (their_u, their_s, x, 1 - x),
    ):
        for j in range(half):
            p = part * half + j
            first = p + half
            second = jnp.where(part == 0, 3 * half + j, j)
            out[pl.ds(pl.multiple_of(first * ch, ch), ch), :] = u[j].astype(F32)
            out[pl.ds(pl.multiple_of(second * ch, ch), ch), :] = s[j, :rows].astype(F32)
            block = xp * half + j
            at = lax.rem(block, per) * extra
            side = block // per
            value = s[j, rows:].astype(F32)
            where = pl.ds(pl.multiple_of(at, extra), extra)

            @pl.when(side == 0)
            def _():
                out_proj[where, :width] = value

            @pl.when(side == 1)
            def _():
                out_proj[where, width:] = value


def body(
    features, lengths, routes, res_in_weight, res_out_weight, down_weight, proj_weight, cotangent
):
    utts = lengths.shape[0]
    total_rows = features.shape[0] // utts
    ch = features.shape[1]
    frames = total_rows // STRIDE
    hid = res_out_weight.shape[0]
    width = down_weight.shape[1]
    lat = proj_weight.shape[1]
    dp_count = lax.axis_size("dp")
    pieces = routes.shape[0]
    half_pieces = pieces // utts
    capacity = 2 * pieces // dp_count
    slots = dp_count * capacity
    cols = cotangent.shape[1]
    half = STRIDE // 2
    me_dp = lax.axis_index("dp")
    me_mp = lax.axis_index("mp")
    c, y, x = me_mp % 2, me_mp // 2, me_dp % 2
    own_length = lax.dynamic_index_in_dim(lengths, c, 0, keepdims=False)
    sc = jnp.stack([own_length, c, y, x]).astype(jnp.int32)

    other_down = swap_bit(down_weight, "mp", 1)
    other_proj = swap_bit(proj_weight, "mp", 1)
    returned = lax.all_to_all(
        cotangent.reshape(dp_count, capacity, cols), "dp", split_axis=0, concat_axis=0
    ).reshape(slots, cols)

    own_rows = pl.BlockSpec((total_rows, ch), lambda i, s: (s[1], 0))
    a1, a2, sec, ahid, shid, adown, sdown, lat_send, lat_keep = call(
        forward_kernel,
        [
            ((STRIDE, frames, ch), BF),
            ((STRIDE, frames, ch), BF),
            ((STRIDE, frames, ch), BF),
            ((STRIDE, frames, hid), BF),
            ((STRIDE, frames, hid), BF),
            ((frames, 2 * width), BF),
            ((frames, 2 * width), F32),
            ((half_pieces, half * lat), BF),
            ((half_pieces, half * lat), BF),
        ],
        [
            features, res_in_weight, res_out_weight, down_weight, other_down,
            proj_weight, other_proj,
        ],
        scratch=[
            pltpu.VMEM((ch // LANES, total_rows, LANES), F32),
            pltpu.VMEM((STRIDE, frames, 3 * hid), F32),
            pltpu.VMEM((lat // LANES, frames, LANES), F32),
        ],
        prefetch=sc,
        specs={0: own_rows},
        name="forward",
        flops=4 << 30,
    )
    other_a2 = swap_bit(a2, "mp", 1)

    g_own, g_other = call(
        functools.partial(pick_kernel, capacity, dp_count),
        [((half_pieces, cols), BF), ((half_pieces, cols), BF)],
        [routes, returned],
        scratch=[pltpu.VMEM((pieces, cols), F32)],
        prefetch=sc,
        name="pick",
    )
    g_core = swap_bit(g_other, "mp", 1)
    g_y = swap_bit(jnp.concatenate([g_own, g_core], 1), "mp", 2)

    gd, swap, gproj, g_send = call(
        latent_grad_kernel,
        [
            ((frames, 2 * width), BF),
            ((frames + 2 * width, width), BF),
            ((2 * width, lat // 2), F32),
            ((half, frames, ch), BF),
        ],
        [
            g_own, g_core, g_y, adown, sdown, proj_weight, other_proj, down_weight, other_down,
        ],
        scratch=[pltpu.VMEM((lat // LANES, frames, LANES), F32)],
        prefetch=sc,
        name="latent_grad",
        flops=1 << 30,
    )
    g_recv = swap_bit(g_send, "mp", 2)
    got = swap_bit(swap, "mp", 1)
    extra = 2 * width // STRIDE
    send_u, send_s = call(
        down_send_kernel,
        [((half, ch, width), BF), ((half, ch + extra, width), BF)],
        [a2, other_a2, gd, got, gproj],
        prefetch=sc,
        name="down_send",
        flops=1 << 29,
    )
    recv_u = swap_bit(send_u, "dp", 1)
    recv_s = swap_bit(send_s, "dp", 1)
    keep_u, keep_s, keep_g = call(
        down_keep_kernel,
        [
            ((half, ch, width), F32),
            ((half, ch + extra, width), F32),
            ((half, frames, ch), F32),
        ],
        [gd, got, gproj, a2, other_a2, down_weight, other_down],
        prefetch=sc,
        name="down_keep",
        flops=1 << 30,
    )

    def phases(n):
        return pl.BlockSpec((half, frames, n), lambda i, s: (s[2], 0, 0))

    blocks = 4 * (ch // hid)
    e_send, e_keep = call(
        residual_kernel,
        [((blocks // 2, hid, hid), BF), ((blocks // 2, hid, hid), F32)],
        [keep_g, g_recv, sec, ahid, shid, res_out_weight, a1],
        scratch=[pltpu.VMEM((half, frames, hid), F32), pltpu.VMEM((blocks, hid, hid), F32)],
        prefetch=sc,
        specs={2: phases(ch), 3: phases(hid), 4: phases(hid)},
        name="residual",
        flops=1 << 30,
    )
    e = (e_keep + swap_bit(e_send, "mp", 1).astype(F32)).reshape(2, -1, hid)
    e_own = pick(e, y) + swap_bit(pick(e, 1 - y).astype(BF), "mp", 2).astype(F32)
    e_own = e_own + swap_bit(e_own.astype(BF), "dp", 1).astype(F32)
    for bit, members in stages_of(dp_count):
        sent = e_own.astype(BF)
        got_e = [swap_bit(sent, "dp", bit * k) for k in range(1, members)]
        for g in got_e:
            e_own = e_own + g.astype(F32)
    sent = e_own.astype(BF)
    other = swap_bit(sent, "mp", 2)
    both = jnp.where(y == 0, jnp.concatenate([sent, other]), jnp.concatenate([other, sent]))
    far = swap_bit(both, "mp", 1)
    e_all = jnp.where(c == 0, jnp.concatenate([both, far]), jnp.concatenate([far, both]))
    e_all = e_all.astype(F32).reshape(blocks, hid, hid)
    split = 3 * (ch // hid)
    grad_res_in = e_all[:split].reshape(3 * ch, hid)
    grad_res_out = jnp.concatenate([e_all[split + i] for i in range(ch // hid)], 1)

    stages = stages_of(dp_count)
    sum_u = reduce_rest(keep_u, recv_u, me_dp, stages)
    all_u = gather_rest(sum_u, me_dp, stages).reshape(half, ch, width)
    their_u = swap_bit(all_u, "dp", 1)
    sum_s = reduce_rest(keep_s, recv_s, me_dp, stages)
    all_s = gather_rest(sum_s, me_dp, stages).reshape(half, ch + extra, width)
    their_s = swap_bit(all_s, "dp", 1)
    grad_down, grad_proj = call(
        finish_kernel,
        [((2 * STRIDE * ch, width), F32), ((width, lat), F32)],
        [all_u, all_s, their_u, their_s],
        prefetch=sc,
        name="finish",
    )

    lat_y = swap_bit(lat_send, "mp", 2)
    summed = (lat_keep.astype(F32) + lat_y.astype(F32)).astype(BF).reshape(half_pieces, 2, cols)
    mine = lax.dynamic_index_in_dim(summed, c, 1, keepdims=False)
    theirs = swap_bit(lax.dynamic_index_in_dim(summed, 1 - c, 1, keepdims=False), "mp", 1)
    (outgoing,) = call(
        functools.partial(place_kernel, capacity, dp_count),
        [((slots, cols), BF)],
        [routes, mine, theirs],
        scratch=[pltpu.VMEM((pieces, cols), F32)],
        prefetch=sc,
        name="place",
    )
    packed = lax.all_to_all(
        outgoing.reshape(dp_count, capacity, cols), "dp", split_axis=0, concat_axis=0
    ).reshape(slots, cols)
    return (packed, grad_res_in, grad_res_out, grad_down, grad_proj)


def solution(mesh):
    return jax.shard_map(
        body,
        mesh=mesh,
        in_specs=(
            P("dp", None),
            P("dp"),
            P("dp", None),
            P(),
            P(),
            P(None, "mp"),
            P("mp", None),
            P("dp", "mp"),
        ),
        out_specs=(P("dp", "mp"), P(), P(), P(None, "mp"), P("mp", None)),
        check_vma=False,
    )
```

```python
import functools
import jax
import jax.numpy as jnp
from jax import lax
from jax.experimental import pallas as pl
from jax.experimental.pallas import tpu as pltpu
from jax.sharding import PartitionSpec as P

STRIDE = 8
LANES = 128
BF = jnp.bfloat16
F32 = jnp.float32
VMEM_LIMIT = 12 << 20


def elu(v):
    return jnp.where(v > 0, v, jnp.exp(jnp.minimum(v, 0.0)) - 1.0)


def slope(v):
    return jnp.where(v > 0, 1.0, jnp.exp(jnp.minimum(v, 0.0)))


def mm(a, b):
    return jnp.dot(a, b, preferred_element_type=F32)


def mm_nt(a, b):
    return lax.dot_general(a, b, (((1,), (1,)), ((), ())), preferred_element_type=F32)


def mm_tn(a, b):
    return lax.dot_general(a, b, (((0,), (0,)), ((), ())), preferred_element_type=F32)


def shift(v, s):
    n = v.shape[0]
    rows = lax.broadcasted_iota(jnp.int32, v.shape, 0)
    rolled = pltpu.roll(v, (-s) % n, 0)
    keep = rows < n - s if s > 0 else rows >= -s
    return jnp.where(keep, rolled, 0.0)


def spread(ref, value):
    for i in range(ref.shape[0]):
        ref[i] = value[:, i * LANES : (i + 1) * LANES]


def every(ref, start, size):
    return jnp.concatenate(
        [ref[i, pl.ds(start, size, stride=STRIDE), :] for i in range(ref.shape[0])], 1
    )


def call(kernel, outs, ins, scratch=(), flops=0):
    whole = pl.BlockSpec(memory_space=pltpu.VMEM)
    return pl.pallas_call(
        kernel,
        out_shape=[jax.ShapeDtypeStruct(s, d) for s, d in outs],
        in_specs=[pl.BlockSpec(memory_space=pltpu.SMEM)] + [whole] * (len(ins) - 1),
        out_specs=[whole] * len(outs),
        scratch_shapes=list(scratch),
        compiler_params=pltpu.CompilerParams(vmem_limit_bytes=VMEM_LIMIT),
        cost_estimate=pl.CostEstimate(
            flops=flops, transcendentals=0, bytes_accessed=1 << 20
        ),
    )(*ins)


def position(lengths):
    m = lax.axis_index("mp")
    c = lax.rem(m, 2)
    return lengths[c], c, m // 2, lax.rem(lax.axis_index("dp"), 2)


def forward_kernel(
    capacity, lengths, feat, routes, wi, wo, dwa, dwb, pa, pb,
    a1, a2, sec, ahid, shid, adown, sdown, lat_send, lat_keep, placing,
    xs, ys, ls,
):
    frames, ch = a1.shape[1], a1.shape[2]
    hid = wo.shape[0]
    length, c, y, _ = position(lengths)
    rows = frames * STRIDE
    spread(xs, feat[pl.ds(pl.multiple_of(c * rows, rows), rows), :].astype(F32))
    placing[...] = placing_of(routes[...], placing.shape[1], capacity)
    wcat = jnp.concatenate([wi[k * ch : (k + 1) * ch, :] for k in range(3)], 1)
    live = lax.broadcasted_iota(jnp.int32, (frames, ch), 0) < length

    def signal(p):
        return jnp.where(live, every(xs, p, frames), 0.0)

    for p in range(STRIDE):
        act = elu(signal(p)).astype(BF)
        a1[p] = act
        ys[p] = mm(act, wcat)
    down = jnp.zeros((frames, 2 * dwa.shape[1]), F32)
    before = jnp.zeros_like(down)
    after = jnp.zeros_like(down)

    def tap(k):
        return jnp.concatenate([dwa[k * ch : (k + 1) * ch, :], dwb[k * ch : (k + 1) * ch, :]], 1)

    for p in range(STRIDE):
        left = shift(ys[(p - 1) % STRIDE, :, :hid], -1 if p > 0 else -2)
        right = shift(ys[(p + 1) % STRIDE, :, 2 * hid :], 1 if p < STRIDE - 1 else 2)
        hidden = left + ys[p, :, hid : 2 * hid] + right
        act_hid = elu(hidden).astype(BF)
        ahid[p] = act_hid
        shid[p] = slope(hidden).astype(BF)
        section = jnp.where(live, signal(p) + mm(act_hid, wo[...]), 0.0).astype(BF)
        sec[p] = section
        act = elu(section.astype(F32)).astype(BF)
        a2[p] = act
        half = STRIDE // 2
        down = down + mm(act, tap(p + half))
        if p < half:
            after = after + mm(act, tap(p + 3 * half))
        else:
            before = before + mm(act, tap(p - half))
    down = down + shift(before, -1) + shift(after, 1)
    act_down = elu(down).astype(BF)
    adown[...] = act_down
    sdown[...] = slope(down)
    proj = jnp.concatenate([pa[...], pb[...]], 0)
    spread(ls, jnp.where(live, mm(act_down, proj), 0.0))
    pieces = frames // STRIDE
    lat = ch
    for j in range(STRIDE // 2):
        half = STRIDE // 2
        cols = slice(j * lat, (j + 1) * lat)
        lat_send[:, cols] = every(ls, half * (1 - y) + j, pieces).astype(BF)
        lat_keep[:, cols] = every(ls, half * y + j, pieces).astype(BF)


def placing_of(targets, slots, capacity):
    pieces = targets.shape[0]
    lanes = lax.broadcasted_iota(jnp.int32, (pieces, 128), 1)
    hit = targets == lanes
    chosen = jnp.where(hit, 1.0, 0.0)
    lower = (
        lax.broadcasted_iota(jnp.int32, (pieces, pieces), 0)
        > lax.broadcasted_iota(jnp.int32, (pieces, pieces), 1)
    )
    earlier = mm(jnp.where(lower, 1.0, 0.0).astype(BF), chosen.astype(BF))
    rank = jnp.sum(earlier * chosen, axis=1, keepdims=True).astype(jnp.int32)
    slot = targets * capacity + rank
    ids = lax.broadcasted_iota(jnp.int32, (pieces, slots), 1)
    return jnp.where(slot == ids, 1.0, 0.0).astype(BF)


def pick_kernel(lengths, placing, returned, own, other, buf):
    _, c, _, _ = position(lengths)
    buf[...] = mm(placing[...], returned[...])
    half = own.shape[0]
    own[...] = buf[pl.ds(pl.multiple_of(c * half, half), half), :].astype(BF)
    other[...] = buf[pl.ds(pl.multiple_of((1 - c) * half, half), half), :].astype(BF)


def place_kernel(lengths, placing, mine, theirs, outgoing, buf):
    _, c, _, _ = position(lengths)
    half = mine.shape[0]
    buf[pl.ds(pl.multiple_of(c * half, half), half), :] = mine[...].astype(F32)
    buf[pl.ds(pl.multiple_of((1 - c) * half, half), half), :] = theirs[...].astype(F32)
    outgoing[...] = mm_tn(placing[...], buf[...].astype(BF)).astype(BF)


def section_grad(gd, gshift, wa, wb, part, j, ch):
    half = STRIDE // 2
    first = part * half + j + half
    second = jnp.where(part == 0, 3 * half + j, j)
    rows1 = pl.ds(pl.multiple_of(first * ch, ch), ch)
    rows2 = pl.ds(pl.multiple_of(second * ch, ch), ch)
    w1 = jnp.concatenate([wa[rows1, :], wb[rows1, :]], 1)
    w2 = jnp.concatenate([wa[rows2, :], wb[rows2, :]], 1)
    return mm_nt(gd, w1) + mm_nt(gshift, w2)


def moved(gd, part):
    g = gd.astype(F32)
    return jnp.where(part == 0, shift(g, -1), shift(g, 1)).astype(BF)


def latent_grad_kernel(
    lengths, g_own, g_core, g_y, g_far, adown, sdown, pa, pb,
    gd_out, swap, gproj_keep, gl,
):
    frames = adown.shape[0]
    width, lat = pa.shape
    pieces = g_own.shape[0]
    length, c, y, _ = position(lengths)
    blocks = (
        (g_own, 2 * y + c),
        (g_core, 2 * y + 1 - c),
        (g_y, 2 * (1 - y) + c),
        (g_far, 2 * (1 - y) + 1 - c),
    )
    for block, owner in blocks:
        for j in range(2):
            for i in range(gl.shape[0]):
                at = j * lat + i * LANES
                gl[i, pl.ds(2 * owner + j, pieces, stride=STRIDE), :] = block[
                    :, at : at + LANES
                ].astype(F32)
    live = lax.broadcasted_iota(jnp.int32, (frames, lat), 0) < length
    g_latent = jnp.where(live, jnp.concatenate([gl[i] for i in range(gl.shape[0])], 1), 0.0)
    g_latent = g_latent.astype(BF)
    proj = jnp.concatenate([pa[...], pb[...]], 0)
    gd = (mm_nt(g_latent, proj) * sdown[...]).astype(BF)
    gd_out[...] = gd
    swap[:frames] = gd[:, width:]
    gproj = mm_tn(adown[...], g_latent)
    swap[frames : frames + width] = gproj[width:, :width].astype(BF)
    swap[frames + width :] = gproj[width:, width:].astype(BF)
    gproj_keep[:width] = gproj[:width, :width]
    gproj_keep[width:] = gproj[:width, width:]


def section_send_kernel(lengths, gd, dwa, dwb, send):
    _, _, y, _ = position(lengths)
    full = gd[...]
    g2 = moved(full, 1 - y)
    for j in range(STRIDE // 2):
        send[j] = section_grad(full, g2, dwa, dwb, 1 - y, j, send.shape[2]).astype(BF)


def section_keep_kernel(lengths, gd, dwa, dwb, keep):
    _, _, y, _ = position(lengths)
    full = gd[...]
    g2 = moved(full, y)
    for j in range(STRIDE // 2):
        keep[j] = section_grad(full, g2, dwa, dwb, y, j, keep.shape[2])


def weight_grads(a2a, a2b, ga, gb, part, j):
    half = STRIDE // 2
    p = part * half + j
    return mm_tn(a2a[p], ga) + mm_tn(a2b[p], gb)


def pair(g, part):
    return jnp.concatenate([g, moved(g, part)], 1)


def down_send_kernel(lengths, a2a, a2b, gd, swap, gproj, send_u, send_s):
    frames = gd.shape[0]
    width = swap.shape[1]
    _, _, _, x = position(lengths)
    ga = pair(gd[:, :width], x)
    gb = pair(swap[:frames], x)
    extra = send_s.shape[1] - send_u.shape[1]
    rows = send_u.shape[1]
    for j in range(STRIDE // 2):
        w = weight_grads(a2a, a2b, ga, gb, x, j)
        send_u[j] = w[:, :width].astype(BF)
        send_s[j, :rows] = w[:, width:].astype(BF)
        at = pl.ds(pl.multiple_of(((1 - x) * 4 + j) * extra, extra), extra)
        send_s[j, rows:] = (gproj[at, :] + swap[pl.ds(pl.multiple_of(frames + ((1 - x) * 4 + j) * extra, extra), extra), :].astype(F32)).astype(BF)


def down_keep_kernel(lengths, a2a, a2b, gd, swap, gproj, keep_u, keep_s):
    frames = gd.shape[0]
    width = swap.shape[1]
    _, _, _, x = position(lengths)
    part = 1 - x
    ga = pair(gd[:, :width], part)
    gb = pair(swap[:frames], part)
    extra = keep_s.shape[1] - keep_u.shape[1]
    rows = keep_u.shape[1]
    for j in range(STRIDE // 2):
        w = weight_grads(a2a, a2b, ga, gb, part, j)
        keep_u[j] = w[:, :width]
        keep_s[j, :rows] = w[:, width:]
        at = pl.ds(pl.multiple_of((x * 4 + j) * extra, extra), extra)
        keep_s[j, rows:] = gproj[at, :] + swap[pl.ds(pl.multiple_of(frames + (x * 4 + j) * extra, extra), extra), :].astype(F32)


def residual_kernel(lengths, keep, recv, sec, ahid, shid, wo, a1, send, kept, gh, buf):
    half = STRIDE // 2
    frames, ch = keep.shape[1], keep.shape[2]
    hid = wo.shape[0]
    length, c, y, _ = position(lengths)
    live = lax.broadcasted_iota(jnp.int32, (frames, ch), 0) < length
    g_out = jnp.zeros((hid, ch), F32)
    for j in range(half):
        g = keep[j] + recv[j].astype(F32)
        g_branch = jnp.where(live, g * slope(sec[y * half + j].astype(F32)), 0.0).astype(BF)
        g_out = g_out + mm_tn(ahid[y * half + j], g_branch)
        gh[j] = mm_nt(g_branch, wo[...]) * shid[y * half + j].astype(F32)
    taps = [jnp.zeros((ch, hid), F32) for _ in range(3)]
    for j in range(half):
        g = gh[j]
        p = y * half + j
        here = g.astype(BF)
        taps[1] = taps[1] + mm_tn(a1[p], here)
        down1 = shift(g, 1)
        up1 = shift(g, -1)
        if j == 0:
            down1 = jnp.where(y == 0, shift(g, 2), down1)
        if j == half - 1:
            up1 = jnp.where(y == 1, shift(g, -2), up1)
        taps[0] = taps[0] + mm_tn(a1[lax.rem(p + STRIDE - 1, STRIDE)], down1.astype(BF))
        taps[2] = taps[2] + mm_tn(a1[lax.rem(p + 1, STRIDE)], up1.astype(BF))
    for k in range(3):
        for i in range(ch // hid):
            buf[k * (ch // hid) + i] = taps[k][i * hid : (i + 1) * hid]
    for i in range(ch // hid):
        buf[3 * (ch // hid) + i] = g_out[:, i * hid : (i + 1) * hid]
    n = send.shape[0]
    for i in range(n):
        send[i] = buf[(1 - c) * n + i].astype(BF)
        kept[i] = buf[c * n + i]


def swap_bit(value, axis, bit):
    n = lax.axis_size(axis)
    return lax.ppermute(value, axis, [(i, i ^ bit) for i in range(n)])


def stages_of(n):
    found, bit = [], 2
    while bit < n:
        members = 4 if n // bit >= 4 else 2
        found.append((bit, members))
        bit *= members
    return found


def pick(stack, index):
    return lax.dynamic_index_in_dim(stack, index, 0, keepdims=False)


def reduce_rest(kept, received, me, stages):
    total = kept + received.astype(F32)
    for bit, members in stages:
        parts = total.reshape(members, -1, total.shape[-1])
        place = (me // bit) % members
        got = [
            swap_bit(pick(parts, place ^ k).astype(BF), "dp", bit * k)
            for k in range(1, members)
        ]
        total = pick(parts, place)
        for g in got:
            total = total + g.astype(F32)
    return total.astype(BF)


def gather_rest(own, me, stages):
    for bit, members in reversed(stages):
        place = (me // bit) % members
        blocks = [own] + [swap_bit(own, "dp", bit * k) for k in range(1, members)]
        ordered = jnp.stack(blocks)
        own = jnp.concatenate([pick(ordered, place ^ k) for k in range(members)], 0)
    return own


def finish_kernel(lengths, mine_u, mine_s, their_u, their_s, out, out_proj):
    _, _, _, x = position(lengths)
    _, rows, width = mine_u.shape
    extra = mine_s.shape[1] - rows
    half = STRIDE // 2
    ch = rows
    per = out_proj.shape[0] // extra
    for u, s, part, xp in (
        (mine_u, mine_s, 1 - x, x),
        (their_u, their_s, x, 1 - x),
    ):
        for j in range(half):
            p = part * half + j
            first = p + half
            second = jnp.where(part == 0, 3 * half + j, j)
            out[pl.ds(pl.multiple_of(first * ch, ch), ch), :] = u[j].astype(F32)
            out[pl.ds(pl.multiple_of(second * ch, ch), ch), :] = s[j, :rows].astype(F32)
            block = xp * half + j
            at = lax.rem(block, per) * extra
            side = block // per
            value = s[j, rows:].astype(F32)
            where = pl.ds(pl.multiple_of(at, extra), extra)

            @pl.when(side == 0)
            def _():
                out_proj[where, :width] = value

            @pl.when(side == 1)
            def _():
                out_proj[where, width:] = value


def body(
    features, lengths, routes, res_in_weight, res_out_weight, down_weight, proj_weight, cotangent
):
    utts = lengths.shape[0]
    total_rows = features.shape[0] // utts
    ch = features.shape[1]
    frames = total_rows // STRIDE
    hid = res_out_weight.shape[0]
    width = down_weight.shape[1]
    lat = proj_weight.shape[1]
    dp_count = lax.axis_size("dp")
    pieces = routes.shape[0]
    half_pieces = pieces // utts
    capacity = 2 * pieces // dp_count
    slots = dp_count * capacity
    cols = cotangent.shape[1]
    half = STRIDE // 2
    me_dp = lax.axis_index("dp")
    me_mp = lax.axis_index("mp")
    c, y = me_mp % 2, me_mp // 2

    other_down = swap_bit(down_weight, "mp", 1)
    other_proj = swap_bit(proj_weight, "mp", 1)
    returned = lax.all_to_all(
        cotangent.reshape(dp_count, capacity, cols), "dp", split_axis=0, concat_axis=0
    ).reshape(slots, cols)

    a1, a2, sec, ahid, shid, adown, sdown, lat_send, lat_keep, placing = call(
        functools.partial(forward_kernel, capacity),
        [
            ((STRIDE, frames, ch), BF),
            ((STRIDE, frames, ch), BF),
            ((STRIDE, frames, ch), BF),
            ((STRIDE, frames, hid), BF),
            ((STRIDE, frames, hid), BF),
            ((frames, 2 * width), BF),
            ((frames, 2 * width), F32),
            ((half_pieces, half * lat), BF),
            ((half_pieces, half * lat), BF),
            ((pieces, slots), BF),
        ],
        [
            lengths, features, routes, res_in_weight, res_out_weight, down_weight, other_down,
            proj_weight, other_proj,
        ],
        scratch=[
            pltpu.VMEM((ch // LANES, total_rows, LANES), F32),
            pltpu.VMEM((STRIDE, frames, 3 * hid), F32),
            pltpu.VMEM((lat // LANES, frames, LANES), F32),
        ],
        flops=4 << 30,
    )
    other_a2 = swap_bit(a2, "mp", 1)

    g_own, g_other = call(
        pick_kernel,
        [((half_pieces, cols), BF), ((half_pieces, cols), BF)],
        [lengths, placing, returned],
        scratch=[pltpu.VMEM((pieces, cols), F32)],
    )
    g_y = swap_bit(g_own, "mp", 2)
    g_far = swap_bit(g_other, "mp", 3)
    g_core = swap_bit(g_other, "mp", 1)

    gd, swap, gproj = call(
        latent_grad_kernel,
        [
            ((frames, 2 * width), BF),
            ((frames + 2 * width, width), BF),
            ((2 * width, lat // 2), F32),
        ],
        [lengths, g_own, g_core, g_y, g_far, adown, sdown, proj_weight, other_proj],
        scratch=[pltpu.VMEM((lat // LANES, frames, LANES), F32)],
        flops=1 << 30,
    )
    got = swap_bit(swap, "mp", 1)
    (g_send,) = call(
        section_send_kernel,
        [((half, frames, ch), BF)],
        [lengths, gd, down_weight, other_down],
        flops=1 << 29,
    )
    g_recv = swap_bit(g_send, "mp", 2)
    extra = 2 * width // STRIDE
    send_u, send_s = call(
        down_send_kernel,
        [((half, ch, width), BF), ((half, ch + extra, width), BF)],
        [lengths, a2, other_a2, gd, got, gproj],
        flops=1 << 29,
    )
    recv_u = swap_bit(send_u, "dp", 1)
    recv_s = swap_bit(send_s, "dp", 1)
    keep_u, keep_s = call(
        down_keep_kernel,
        [((half, ch, width), F32), ((half, ch + extra, width), F32)],
        [lengths, a2, other_a2, gd, got, gproj],
        flops=1 << 29,
    )
    (keep_g,) = call(
        section_keep_kernel,
        [((half, frames, ch), F32)],
        [lengths, gd, down_weight, other_down],
        flops=1 << 29,
    )

    blocks = 4 * (ch // hid)
    e_send, e_keep = call(
        residual_kernel,
        [((blocks // 2, hid, hid), BF), ((blocks // 2, hid, hid), F32)],
        [lengths, keep_g, g_recv, sec, ahid, shid, res_out_weight, a1],
        scratch=[pltpu.VMEM((half, frames, hid), F32), pltpu.VMEM((blocks, hid, hid), F32)],
        flops=1 << 30,
    )
    e = (e_keep + swap_bit(e_send, "mp", 1).astype(F32)).reshape(2, -1, hid)
    e_own = pick(e, y) + swap_bit(pick(e, 1 - y).astype(BF), "mp", 2).astype(F32)
    e_own = e_own + swap_bit(e_own.astype(BF), "dp", 1).astype(F32)
    for bit, members in stages_of(dp_count):
        sent = e_own.astype(BF)
        got_e = [swap_bit(sent, "dp", bit * k) for k in range(1, members)]
        for g in got_e:
            e_own = e_own + g.astype(F32)
    sent = e_own.astype(BF)
    other = swap_bit(sent, "mp", 2)
    both = jnp.where(y == 0, jnp.concatenate([sent, other]), jnp.concatenate([other, sent]))
    far = swap_bit(both, "mp", 1)
    e_all = jnp.where(c == 0, jnp.concatenate([both, far]), jnp.concatenate([far, both]))
    e_all = e_all.astype(F32).reshape(blocks, hid, hid)
    split = 3 * (ch // hid)
    grad_res_in = e_all[:split].reshape(3 * ch, hid)
    grad_res_out = jnp.concatenate([e_all[split + i] for i in range(ch // hid)], 1)

    stages = stages_of(dp_count)
    sum_u = reduce_rest(keep_u, recv_u, me_dp, stages)
    all_u = gather_rest(sum_u, me_dp, stages).reshape(half, ch, width)
    their_u = swap_bit(all_u, "dp", 1)
    sum_s = reduce_rest(keep_s, recv_s, me_dp, stages)
    all_s = gather_rest(sum_s, me_dp, stages).reshape(half, ch + extra, width)
    their_s = swap_bit(all_s, "dp", 1)
    grad_down, grad_proj = call(
        finish_kernel,
        [((2 * STRIDE * ch, width), F32), ((width, lat), F32)],
        [lengths, all_u, all_s, their_u, their_s],
    )

    lat_y = swap_bit(lat_send, "mp", 2)
    summed = (lat_keep.astype(F32) + lat_y.astype(F32)).astype(BF).reshape(half_pieces, 2, cols)
    mine = lax.dynamic_index_in_dim(summed, c, 1, keepdims=False)
    theirs = lax.dynamic_index_in_dim(summed, 1 - c, 1, keepdims=False)
    theirs = swap_bit(theirs, "mp", 1)
    (outgoing,) = call(
        place_kernel,
        [((slots, cols), BF)],
        [lengths, placing, mine, theirs],
        scratch=[pltpu.VMEM((pieces, cols), F32)],
    )
    packed = lax.all_to_all(
        outgoing.reshape(dp_count, capacity, cols), "dp", split_axis=0, concat_axis=0
    ).reshape(slots, cols)
    return (packed, grad_res_in, grad_res_out, grad_down, grad_proj)


def solution(mesh):
    return jax.shard_map(
        body,
        mesh=mesh,
        in_specs=(
            P("dp", None),
            P("dp"),
            P("dp", None),
            P(),
            P(),
            P(None, "mp"),
            P("mp", None),
            P("dp", "mp"),
        ),
        out_specs=(P("dp", "mp"), P(), P(), P(None, "mp"), P("mp", None)),
        check_vma=False,
    )
```

```python
import functools
import jax
import jax.numpy as jnp
from jax import lax
from jax.experimental import pallas as pl
from jax.experimental.pallas import tpu as pltpu
from jax.sharding import PartitionSpec as P

STRIDE = 8
LANES = 128
BF = jnp.bfloat16
F32 = jnp.float32
VMEM_LIMIT = 16 << 20


def elu(v):
    return jnp.where(v > 0, v, jnp.exp(jnp.minimum(v, 0.0)) - 1.0)


def slope(v):
    return jnp.where(v > 0, 1.0, jnp.exp(jnp.minimum(v, 0.0)))


def mm(a, b):
    return jnp.dot(a, b, preferred_element_type=F32)


def mm_nt(a, b):
    return lax.dot_general(a, b, (((1,), (1,)), ((), ())), preferred_element_type=F32)


def mm_tn(a, b):
    return lax.dot_general(a, b, (((0,), (0,)), ((), ())), preferred_element_type=F32)


def shift(v, s):
    n = v.shape[0]
    rows = lax.broadcasted_iota(jnp.int32, v.shape, 0)
    rolled = pltpu.roll(v, (-s) % n, 0)
    keep = rows < n - s if s > 0 else rows >= -s
    return jnp.where(keep, rolled, 0.0)


def spread(ref, value):
    for i in range(ref.shape[0]):
        ref[i] = value[:, i * LANES : (i + 1) * LANES]


def every(ref, start, size):
    return jnp.concatenate(
        [ref[i, pl.ds(start, size, stride=STRIDE), :] for i in range(ref.shape[0])], 1
    )


def call(kernel, outs, ins, scratch=(), flops=0, where=None, aliases=None):
    whole = pl.BlockSpec(memory_space=pltpu.VMEM)
    spaces = {i: pl.BlockSpec(memory_space=space) for i, space in (where or {}).items()}
    return pl.pallas_call(
        kernel,
        out_shape=[jax.ShapeDtypeStruct(s, d) for s, d in outs],
        in_specs=[spaces.get(i, whole) for i in range(len(ins))],
        out_specs=[spaces.get(len(ins) + i, whole) for i in range(len(outs))],
        scratch_shapes=list(scratch),
        input_output_aliases=aliases or {},
        compiler_params=pltpu.CompilerParams(vmem_limit_bytes=VMEM_LIMIT),
        cost_estimate=pl.CostEstimate(
            flops=flops, transcendentals=0, bytes_accessed=1 << 20
        ),
    )(*ins)


def position():
    m = lax.axis_index("mp")
    return lax.rem(m, 2), m // 2, lax.rem(lax.axis_index("dp"), 2)


def masked(value, mask):
    wide = jnp.concatenate([mask[...]] * (value.shape[1] // mask.shape[1]), 1)
    return jnp.where(wide > 0, value, 0.0)


def depth():
    return lax.rem(lax.axis_index("dp") // 2, 4)


def forward_kernel(
    capacity, lengths, feat_hbm, routes_hbm, wi_hbm, wo_hbm,
    a1, a2, sec, ahid, shid, placing, mask, xs, ys, feat, routes, wi, wo, sems,
):
    frames, ch = a1.shape[1], a1.shape[2]
    hid = wo.shape[0]
    c, _, _ = position()
    rows = frames * STRIDE
    parts = feat.shape[0]
    size = rows // parts
    copies = [
        pltpu.make_async_copy(
            feat_hbm.at[pl.ds(pl.multiple_of(c * rows + i * size, size), size), :],
            feat.at[i],
            sems.at[i],
        )
        for i in range(parts)
    ]
    rest = [
        pltpu.make_async_copy(src, dst, sems.at[parts + i])
        for i, (src, dst) in enumerate(((routes_hbm, routes), (wi_hbm, wi), (wo_hbm, wo)))
    ]
    for copy in copies + rest:
        copy.start()
    length = lengths[c]
    live = lax.broadcasted_iota(jnp.int32, (frames, ch), 0) < length
    mask[...] = jnp.where(live[:, : mask.shape[1]], 1.0, 0.0)
    for i in range(parts):
        copies[i].wait()
        value = feat[i].astype(F32)
        for k in range(xs.shape[0]):
            xs[k, i * size : (i + 1) * size] = value[:, k * LANES : (k + 1) * LANES]
    for copy in rest:
        copy.wait()
    placing[...] = placing_of(routes[...], placing.shape[1], capacity)
    wcat = jnp.concatenate([wi[k * ch : (k + 1) * ch, :] for k in range(3)], 1)

    def signal(p):
        return jnp.where(live, every(xs, p, frames), 0.0)

    for p in range(STRIDE):
        act = elu(signal(p)).astype(BF)
        a1[p] = act
        ys[p] = mm(act, wcat)
    for p in range(STRIDE):
        left = shift(ys[(p - 1) % STRIDE, :, :hid], -1 if p > 0 else -2)
        right = shift(ys[(p + 1) % STRIDE, :, 2 * hid :], 1 if p < STRIDE - 1 else 2)
        hidden = left + ys[p, :, hid : 2 * hid] + right
        act_hid = elu(hidden).astype(BF)
        ahid[p] = act_hid
        shid[p] = slope(hidden).astype(BF)
        section = jnp.where(live, signal(p) + mm(act_hid, wo[...]), 0.0).astype(BF)
        sec[p] = section
        a2[p] = elu(section.astype(F32)).astype(BF)


def down_kernel(
    mask, a2, dwa, dwb, pa, pb, adown, sdown, lat_send, lat_keep, ls,
):
    frames, ch = a2.shape[1], a2.shape[2]
    _, y, _ = position()
    half = STRIDE // 2

    def tap(k):
        return jnp.concatenate([dwa[k * ch : (k + 1) * ch, :], dwb[k * ch : (k + 1) * ch, :]], 1)

    down = jnp.zeros((frames, 2 * dwa.shape[1]), F32)
    before = jnp.zeros_like(down)
    after = jnp.zeros_like(down)
    for p in range(STRIDE):
        act = a2[p]
        down = down + mm(act, tap(p + half))
        if p < half:
            after = after + mm(act, tap(p + 3 * half))
        else:
            before = before + mm(act, tap(p - half))
    down = down + shift(before, -1) + shift(after, 1)
    act_down = elu(down).astype(BF)
    adown[...] = act_down
    sdown[...] = slope(down)
    proj = jnp.concatenate([pa[...], pb[...]], 0)
    lat = proj.shape[1]
    spread(ls, masked(mm(act_down, proj), mask))
    pieces = frames // STRIDE
    for j in range(half):
        cols = slice(j * lat, (j + 1) * lat)
        lat_send[:, cols] = every(ls, half * (1 - y) + j, pieces).astype(BF)
        lat_keep[:, cols] = every(ls, half * y + j, pieces).astype(BF)


def placing_of(targets, slots, capacity):
    pieces = targets.shape[0]
    lanes = lax.broadcasted_iota(jnp.int32, (pieces, 128), 1)
    hit = targets == lanes
    chosen = jnp.where(hit, 1.0, 0.0)
    lower = (
        lax.broadcasted_iota(jnp.int32, (pieces, pieces), 0)
        > lax.broadcasted_iota(jnp.int32, (pieces, pieces), 1)
    )
    earlier = mm(jnp.where(lower, 1.0, 0.0).astype(BF), chosen.astype(BF))
    rank = jnp.sum(earlier * chosen, axis=1, keepdims=True).astype(jnp.int32)
    slot = targets * capacity + rank
    ids = lax.broadcasted_iota(jnp.int32, (pieces, slots), 1)
    return jnp.where(slot == ids, 1.0, 0.0).astype(BF)


def ways_kernel(whole, send, keep, sems):
    _, _, x = position()
    copies = [
        pltpu.make_async_copy(whole.at[i, place], out.at[i], sems.at[2 * i + k])
        for i in range(send.shape[0])
        for k, (place, out) in enumerate(((1 - x, send), (x, keep)))
    ]
    for copy in copies:
        copy.start()
    for copy in copies:
        copy.wait()


def levels_kernel(keep, recv, *outs):
    z = depth()
    for k, out in enumerate(outs):
        out[0] = keep[z ^ k]
        out[1] = recv[z ^ k]


def assemble(parts, out, x):
    z = depth()
    size = parts[0].shape[1]
    for k, part in enumerate(parts):
        for i, column in enumerate((x, 1 - x)):
            at = (2 * (z ^ k) + column) * size
            out[pl.ds(pl.multiple_of(at, size), size), :] = part[i]


def pick_kernel(placing, *refs):
    *parts, own, other, rows, buf = refs
    c, _, x = position()
    if len(parts) == 1:
        rows[...] = parts[0][...]
    else:
        assemble(parts, rows, x)
    buf[...] = mm(placing[...], rows[...])
    half = own.shape[0]
    own[...] = buf[pl.ds(pl.multiple_of(c * half, half), half), :].astype(BF)
    other[...] = buf[pl.ds(pl.multiple_of((1 - c) * half, half), half), :].astype(BF)


def place_kernel(placing, mine, theirs, outgoing, buf):
    c, _, _ = position()
    half = mine.shape[0]
    buf[pl.ds(pl.multiple_of(c * half, half), half), :] = mine[...].astype(F32)
    buf[pl.ds(pl.multiple_of((1 - c) * half, half), half), :] = theirs[...].astype(F32)
    outgoing[...] = mm_tn(placing[...], buf[...].astype(BF)).astype(BF)


def place_ways_kernel(placing, mine, theirs, send, keep, buf, rows):
    _, _, x = position()
    place_kernel(placing, mine, theirs, rows, buf)
    size = send.shape[1]
    for i in range(send.shape[0]):
        send[i] = rows[pl.ds(pl.multiple_of((2 * i + 1 - x) * size, size), size), :]
        keep[i] = rows[pl.ds(pl.multiple_of((2 * i + x) * size, size), size), :]


def packed_kernel(*refs):
    *parts, out = refs
    _, _, x = position()
    assemble(parts, out, x)


def section_grad(gd, gshift, wa, wb, part, j, ch):
    half = STRIDE // 2
    first = part * half + j + half
    second = jnp.where(part == 0, 3 * half + j, j)
    rows1 = pl.ds(pl.multiple_of(first * ch, ch), ch)
    rows2 = pl.ds(pl.multiple_of(second * ch, ch), ch)
    w1 = jnp.concatenate([wa[rows1, :], wb[rows1, :]], 1)
    w2 = jnp.concatenate([wa[rows2, :], wb[rows2, :]], 1)
    return mm_nt(gd, w1) + mm_nt(gshift, w2)


def moved(gd, part):
    g = gd.astype(F32)
    return jnp.where(part == 0, shift(g, -1), shift(g, 1)).astype(BF)


def latent_grad_kernel(
    mask, g_own, g_core, g_y, g_far, adown, sdown, pa, pb,
    gd_out, swap, gproj_keep, gl,
):
    frames = adown.shape[0]
    width, lat = pa.shape
    pieces = g_own.shape[0]
    c, y, _ = position()
    blocks = (
        (g_own, 2 * y + c),
        (g_core, 2 * y + 1 - c),
        (g_y, 2 * (1 - y) + c),
        (g_far, 2 * (1 - y) + 1 - c),
    )
    for block, owner in blocks:
        for j in range(2):
            for i in range(gl.shape[0]):
                at = j * lat + i * LANES
                gl[i, pl.ds(2 * owner + j, pieces, stride=STRIDE), :] = block[
                    :, at : at + LANES
                ].astype(F32)
    g_latent = masked(jnp.concatenate([gl[i] for i in range(gl.shape[0])], 1), mask).astype(BF)
    proj = jnp.concatenate([pa[...], pb[...]], 0)
    gd = (mm_nt(g_latent, proj) * sdown[...]).astype(BF)
    gd_out[...] = gd
    swap[:frames] = gd[:, width:]
    gproj = mm_tn(adown[...], g_latent)
    swap[frames : frames + width] = gproj[width:, :width].astype(BF)
    swap[frames + width :] = gproj[width:, width:].astype(BF)
    gproj_keep[:width] = gproj[:width, :width]
    gproj_keep[width:] = gproj[:width, width:]


def section_send_kernel(gd, dwa, dwb, lat_keep, lat_y, send, mine, theirs):
    c, y, _ = position()
    full = gd[...]
    g2 = moved(full, 1 - y)
    for j in range(STRIDE // 2):
        send[j] = section_grad(full, g2, dwa, dwb, 1 - y, j, send.shape[2]).astype(BF)
    total = (lat_keep[...].astype(F32) + lat_y[...].astype(F32)).astype(BF)
    cols = mine.shape[1]
    mine[...] = jnp.where(c == 0, total[:, :cols], total[:, cols:])
    theirs[...] = jnp.where(c == 0, total[:, cols:], total[:, :cols])


def section_keep_kernel(gd, dwa, dwb, keep):
    _, y, _ = position()
    full = gd[...]
    g2 = moved(full, y)
    for j in range(STRIDE // 2):
        keep[j] = section_grad(full, g2, dwa, dwb, y, j, keep.shape[2])


def weight_grads(a2a, a2b, ga, gb, part, j):
    half = STRIDE // 2
    p = part * half + j
    return mm_tn(a2a[p], ga) + mm_tn(a2b[p], gb)


def pair(g, part):
    return jnp.concatenate([g, moved(g, part)], 1)


def down_send_kernel(a2a, a2b, gd, swap, gproj, send_u, send_s):
    frames = gd.shape[0]
    width = swap.shape[1]
    _, _, x = position()
    ga = pair(gd[:, :width], x)
    gb = pair(swap[:frames], x)
    extra = send_s.shape[1] - send_u.shape[1]
    rows = send_u.shape[1]
    for j in range(STRIDE // 2):
        w = weight_grads(a2a, a2b, ga, gb, x, j)
        send_u[j] = w[:, :width].astype(BF)
        send_s[j, :rows] = w[:, width:].astype(BF)
        at = pl.ds(pl.multiple_of(((1 - x) * 4 + j) * extra, extra), extra)
        send_s[j, rows:] = (gproj[at, :] + swap[pl.ds(pl.multiple_of(frames + ((1 - x) * 4 + j) * extra, extra), extra), :].astype(F32)).astype(BF)


def down_keep_kernel(a2a, a2b, gd, swap, gproj, keep_u, keep_s):
    frames = gd.shape[0]
    width = swap.shape[1]
    _, _, x = position()
    part = 1 - x
    ga = pair(gd[:, :width], part)
    gb = pair(swap[:frames], part)
    extra = keep_s.shape[1] - keep_u.shape[1]
    rows = keep_u.shape[1]
    for j in range(STRIDE // 2):
        w = weight_grads(a2a, a2b, ga, gb, part, j)
        keep_u[j] = w[:, :width]
        keep_s[j, :rows] = w[:, width:]
        at = pl.ds(pl.multiple_of((x * 4 + j) * extra, extra), extra)
        keep_s[j, rows:] = gproj[at, :] + swap[pl.ds(pl.multiple_of(frames + (x * 4 + j) * extra, extra), extra), :].astype(F32)


def residual_kernel(
    mask, keep, recv, sec, ahid, shid, wo, a1, kept, send1, send2, send3, gh, buf,
):
    half = STRIDE // 2
    ch = keep.shape[2]
    hid = wo.shape[0]
    c, y, _ = position()
    g_out = jnp.zeros((hid, ch), F32)
    for j in range(half):
        g = keep[j] + recv[j].astype(F32)
        g_branch = masked(g * slope(sec[y * half + j].astype(F32)), mask).astype(BF)
        g_out = g_out + mm_tn(ahid[y * half + j], g_branch)
        gh[j] = mm_nt(g_branch, wo[...]) * shid[y * half + j].astype(F32)
    taps = [jnp.zeros((ch, hid), F32) for _ in range(3)]
    for j in range(half):
        g = gh[j]
        p = y * half + j
        here = g.astype(BF)
        taps[1] = taps[1] + mm_tn(a1[p], here)
        down1 = shift(g, 1)
        up1 = shift(g, -1)
        if j == 0:
            down1 = jnp.where(y == 0, shift(g, 2), down1)
        if j == half - 1:
            up1 = jnp.where(y == 1, shift(g, -2), up1)
        taps[0] = taps[0] + mm_tn(a1[lax.rem(p + STRIDE - 1, STRIDE)], down1.astype(BF))
        taps[2] = taps[2] + mm_tn(a1[lax.rem(p + 1, STRIDE)], up1.astype(BF))
    for k in range(3):
        for i in range(ch // hid):
            buf[k * (ch // hid) + i] = taps[k][i * hid : (i + 1) * hid]
    for i in range(ch // hid):
        buf[3 * (ch // hid) + i] = g_out[:, i * hid : (i + 1) * hid]
    m = 2 * y + c
    n = buf.shape[0] // 4
    for i in range(n):
        at = slice(i * hid, (i + 1) * hid)
        kept[at] = buf[m * n + i]
        for k, out in enumerate((send1, send2, send3)):
            out[at] = buf[(m ^ (k + 1)) * n + i].astype(BF)


def residual_finish_kernel(r0, r1, r2, r3, out_in, out_out, buf):
    c, y, _ = position()
    m = 2 * y + c
    rows, hid = r0.shape
    for k, r in enumerate((r0, r1, r2, r3)):
        buf[m ^ k] = r[...].astype(F32)
    for q in range(3):
        out_in[q * rows : (q + 1) * rows] = buf[q]
    for i in range(rows // hid):
        out_out[:, i * hid : (i + 1) * hid] = buf[3, i * hid : (i + 1) * hid]


def sum_kernel(keep, recv, own, *sends):
    z = depth()
    own[...] = keep[z] + recv[z].astype(F32)
    for k, out in enumerate(sends):
        at = z ^ (k + 1)
        out[...] = (keep[at] + recv[at].astype(F32)).astype(BF)


def swap_bit(value, axis, bit):
    n = lax.axis_size(axis)
    return lax.ppermute(value, axis, [(i, i ^ bit) for i in range(n)])


def stages_of(n):
    found, bit = [], 2
    while bit < n:
        members = 4 if n // bit >= 4 else 2
        found.append((bit, members))
        bit *= members
    return found


def pick(stack, index):
    return lax.dynamic_index_in_dim(stack, index, 0, keepdims=False)


def fan(values, axis, bit):
    return [swap_bit(v, axis, bit * (k + 1)) for k, v in enumerate(values)]


def plus(total, received):
    for r in received:
        total = total + r.astype(F32)
    return total


def reduce_rest(kept, received, me, stages):
    shape = kept.shape[1:]
    own, *sends = call(sum_kernel, [(shape, F32)] + [(shape, BF)] * 3, [kept, received])
    total = plus(own, fan(sends, "dp", stages[0][0]))
    for bit, members in stages[1:]:
        parts = total.reshape(members, -1, total.shape[-1])
        place = (me // bit) % members
        sends = [pick(parts, place ^ k).astype(BF) for k in range(1, members)]
        total = plus(pick(parts, place), fan(sends, "dp", bit))
    return total.astype(BF)


def gather_rest(own, me, stages):
    for bit, members in reversed(stages[1:]):
        place = (me // bit) % members
        blocks = [own] + fan([own] * (members - 1), "dp", bit)
        ordered = jnp.stack(blocks)
        own = jnp.concatenate([pick(ordered, place ^ k) for k in range(members)], 0)
    return [own] + fan([own] * 3, "dp", stages[0][0])


def finish_kernel(shifted, *refs):
    if shifted:
        m0, m1, m2, m3, theirs, _, out, out_proj, buf, sems = refs
        per = out_proj.shape[0] * 2 // STRIDE
    else:
        m0, m1, m2, m3, theirs, out, buf, sems = refs
    _, _, x = position()
    z = depth()
    half = STRIDE // 2
    rows = buf.shape[1]
    copies = []
    for k, mine in enumerate((m0, m1, m2, m3)):
        j = z ^ k
        for i, (value, part, xp) in enumerate(((mine, 1 - x, x), (theirs.at[k], x, 1 - x))):
            tap = part * half + j + half
            if shifted:
                tap = jnp.where(part == 0, 3 * half + j, j)
            n = 2 * k + i
            buf[n] = value[:rows].astype(F32)
            copy = pltpu.make_async_copy(
                buf.at[n],
                out.at[pl.ds(pl.multiple_of(tap * rows, rows), rows), :],
                sems.at[n],
            )
            copy.start()
            copies.append(copy)
            if shifted:
                where = pl.ds(pl.multiple_of(j * per, per), per)
                width = value.shape[1]
                extra = value[rows:].astype(F32)

                @pl.when(xp == 0)
                def _():
                    out_proj[where, :width] = extra

                @pl.when(xp == 1)
                def _():
                    out_proj[where, width:] = extra

    for copy in copies:
        copy.wait()


def body(
    features, lengths, routes, res_in_weight, res_out_weight, down_weight, proj_weight, cotangent
):
    utts = lengths.shape[0]
    total_rows = features.shape[0] // utts
    ch = features.shape[1]
    frames = total_rows // STRIDE
    hid = res_out_weight.shape[0]
    width = down_weight.shape[1]
    lat = proj_weight.shape[1]
    dp_count = lax.axis_size("dp")
    pieces = routes.shape[0]
    half_pieces = pieces // utts
    capacity = 2 * pieces // dp_count
    slots = dp_count * capacity
    cols = cotangent.shape[1]
    half = STRIDE // 2
    me_dp = lax.axis_index("dp")
    stages = stages_of(dp_count)
    staged = dp_count == 8
    lane_block = ((dp_count // 2, capacity, cols), BF)
    pair_block = ((2, capacity, cols), BF)

    def through_dp(send, keep):
        recv = swap_bit(send, "dp", 1)
        own, *sends = call(levels_kernel, [pair_block] * 4, [keep, recv])
        return [own] + fan(sends, "dp", 2)

    def all_to_all(value):
        return lax.all_to_all(
            value.reshape(dp_count, capacity, cols), "dp", split_axis=0, concat_axis=0
        ).reshape(slots, cols)

    other_down = swap_bit(down_weight, "mp", 1)
    other_proj = swap_bit(proj_weight, "mp", 1)
    if staged:
        send, keep = call(
            ways_kernel,
            [lane_block] * 2,
            [cotangent.reshape(dp_count // 2, 2, capacity, cols)],
            scratch=[pltpu.SemaphoreType.DMA((dp_count,))],
            where={0: pl.ANY},
        )
        returned = through_dp(send, keep)
    else:
        returned = [all_to_all(cotangent)]

    loads = 4
    a1, a2, sec, ahid, shid, placing, mask = call(
        functools.partial(forward_kernel, capacity),
        [
            ((STRIDE, frames, ch), BF),
            ((STRIDE, frames, ch), BF),
            ((STRIDE, frames, ch), BF),
            ((STRIDE, frames, hid), BF),
            ((STRIDE, frames, hid), BF),
            ((pieces, slots), BF),
            ((frames, LANES), F32),
        ],
        [lengths, features, routes, res_in_weight, res_out_weight],
        scratch=[
            pltpu.VMEM((ch // LANES, total_rows, LANES), F32),
            pltpu.VMEM((STRIDE, frames, 3 * hid), F32),
            pltpu.VMEM((loads, total_rows // loads, ch), BF),
            pltpu.VMEM(routes.shape, routes.dtype),
            pltpu.VMEM(res_in_weight.shape, BF),
            pltpu.VMEM(res_out_weight.shape, BF),
            pltpu.SemaphoreType.DMA((loads + 3,)),
        ],
        where={0: pltpu.SMEM, 1: pl.ANY, 2: pl.ANY, 3: pl.ANY, 4: pl.ANY},
        flops=4 << 30,
    )
    other_a2 = swap_bit(a2, "mp", 1)
    adown, sdown, lat_send, lat_keep = call(
        down_kernel,
        [
            ((frames, 2 * width), BF),
            ((frames, 2 * width), F32),
            ((half_pieces, half * lat), BF),
            ((half_pieces, half * lat), BF),
        ],
        [mask, a2, down_weight, other_down, proj_weight, other_proj],
        scratch=[pltpu.VMEM((lat // LANES, frames, LANES), F32)],
        flops=1 << 30,
    )
    lat_y = swap_bit(lat_send, "mp", 2)

    g_own, g_other = call(
        pick_kernel,
        [((half_pieces, cols), BF), ((half_pieces, cols), BF)],
        [placing, *returned],
        scratch=[pltpu.VMEM((slots, cols), BF), pltpu.VMEM((pieces, cols), F32)],
    )
    g_y = swap_bit(g_own, "mp", 2)
    g_far = swap_bit(g_other, "mp", 3)
    g_core = swap_bit(g_other, "mp", 1)

    gd, swap, gproj = call(
        latent_grad_kernel,
        [
            ((frames, 2 * width), BF),
            ((frames + 2 * width, width), BF),
            ((2 * width, lat // 2), F32),
        ],
        [mask, g_own, g_core, g_y, g_far, adown, sdown, proj_weight, other_proj],
        scratch=[pltpu.VMEM((lat // LANES, frames, LANES), F32)],
        flops=1 << 30,
    )
    got = swap_bit(swap, "mp", 1)
    g_send, mine, theirs = call(
        section_send_kernel,
        [((half, frames, ch), BF), ((half_pieces, cols), BF), ((half_pieces, cols), BF)],
        [gd, down_weight, other_down, lat_keep, lat_y],
        flops=1 << 29,
    )
    g_recv = swap_bit(g_send, "mp", 2)
    theirs = swap_bit(theirs, "mp", 1)
    extra = 2 * width // STRIDE
    send_u, send_s = call(
        down_send_kernel,
        [((half, ch, width), BF), ((half, ch + extra, width), BF)],
        [a2, other_a2, gd, got, gproj],
        flops=1 << 29,
    )
    recv_u = swap_bit(send_u, "dp", 1)
    recv_s = swap_bit(send_s, "dp", 1)
    keep_u, keep_s = call(
        down_keep_kernel,
        [((half, ch, width), F32), ((half, ch + extra, width), F32)],
        [a2, other_a2, gd, got, gproj],
        flops=1 << 29,
    )
    (keep_g,) = call(
        section_keep_kernel,
        [((half, frames, ch), F32)],
        [gd, down_weight, other_down],
        flops=1 << 29,
    )

    row_scratch = pltpu.VMEM((pieces, cols), F32)
    if staged:
        send, keep = call(
            place_ways_kernel,
            [lane_block] * 2,
            [placing, mine, theirs],
            scratch=[row_scratch, pltpu.VMEM((slots, cols), BF)],
        )
        (packed,) = call(packed_kernel, [((slots, cols), BF)], [*through_dp(send, keep)])
    else:
        (outgoing,) = call(
            place_kernel, [((slots, cols), BF)], [placing, mine, theirs], scratch=[row_scratch]
        )
        packed = all_to_all(outgoing)

    blocks = 4 * (ch // hid)
    quarter = (blocks // 4 * hid, hid)
    e_own, *e_sends = call(
        residual_kernel,
        [(quarter, F32)] + [(quarter, BF)] * 3,
        [mask, keep_g, g_recv, sec, ahid, shid, res_out_weight, a1],
        scratch=[pltpu.VMEM((half, frames, hid), F32), pltpu.VMEM((blocks, hid, hid), F32)],
        flops=1 << 30,
    )
    e_own = plus(e_own, fan(e_sends, "mp", 1))
    e_own = plus(e_own, [swap_bit(e_own.astype(BF), "dp", 1)])
    for bit, members in stages:
        sent = e_own.astype(BF)
        e_own = plus(e_own, fan([sent] * (members - 1), "dp", bit))
    sent = e_own.astype(BF)
    grad_res_in, grad_res_out = call(
        residual_finish_kernel,
        [((3 * ch, hid), F32), ((hid, ch), F32)],
        [sent, *fan([sent] * 3, "mp", 1)],
        scratch=[pltpu.VMEM((4,) + quarter, F32)],
    )

    all_u = gather_rest(reduce_rest(keep_u, recv_u, me_dp, stages), me_dp, stages)
    their_u = swap_bit(jnp.stack(all_u), "dp", 1)
    all_s = gather_rest(reduce_rest(keep_s, recv_s, me_dp, stages), me_dp, stages)
    their_s = swap_bit(jnp.stack(all_s), "dp", 1)
    down_out = ((2 * STRIDE * ch, width), F32)
    taps = [pltpu.VMEM((STRIDE, ch, width), F32), pltpu.SemaphoreType.DMA((STRIDE,))]
    (grad_down,) = call(
        functools.partial(finish_kernel, False),
        [down_out],
        [*all_u, their_u],
        scratch=taps,
        where={5: pl.ANY},
    )
    grad_down, grad_proj = call(
        functools.partial(finish_kernel, True),
        [down_out, ((width, lat), F32)],
        [*all_s, their_s, grad_down],
        scratch=taps,
        where={5: pl.ANY, 6: pl.ANY},
        aliases={5: 0},
    )
    return (packed, grad_res_in, grad_res_out, grad_down, grad_proj)


def solution(mesh):
    return jax.shard_map(
        body,
        mesh=mesh,
        in_specs=(
            P("dp", None),
            P("dp"),
            P("dp", None),
            P(),
            P(),
            P(None, "mp"),
            P("mp", None),
            P("dp", "mp"),
        ),
        out_specs=(P("dp", "mp"), P(), P(), P(None, "mp"), P("mp", None)),
        check_vma=False,
    )
```

```python
import functools
import jax
import jax.numpy as jnp
from jax import lax
from jax.experimental import pallas as pl
from jax.experimental.pallas import tpu as pltpu
from jax.sharding import PartitionSpec as P

STRIDE = 8
LANES = 128
BF = jnp.bfloat16
F32 = jnp.float32
VMEM_LIMIT = 16 << 20


def elu(v):
    return jnp.where(v > 0, v, jnp.exp(jnp.minimum(v, 0.0)) - 1.0)


def slope(v):
    return jnp.where(v > 0, 1.0, jnp.exp(jnp.minimum(v, 0.0)))


def mm(a, b):
    return jnp.dot(a, b, preferred_element_type=F32)


def mm_nt(a, b):
    return lax.dot_general(a, b, (((1,), (1,)), ((), ())), preferred_element_type=F32)


def mm_tn(a, b):
    return lax.dot_general(a, b, (((0,), (0,)), ((), ())), preferred_element_type=F32)


def shift(v, s):
    n = v.shape[0]
    rows = lax.broadcasted_iota(jnp.int32, v.shape, 0)
    rolled = pltpu.roll(v, (-s) % n, 0)
    keep = rows < n - s if s > 0 else rows >= -s
    return jnp.where(keep, rolled, 0.0)


def spread(ref, value):
    for i in range(ref.shape[0]):
        ref[i] = value[:, i * LANES : (i + 1) * LANES]


def every(ref, start, size):
    return jnp.concatenate(
        [ref[i, pl.ds(start, size, stride=STRIDE), :] for i in range(ref.shape[0])], 1
    )


def call(kernel, outs, ins, scratch=(), flops=0, where=None, aliases=None):
    whole = pl.BlockSpec(memory_space=pltpu.VMEM)
    spaces = {i: pl.BlockSpec(memory_space=space) for i, space in (where or {}).items()}
    ins = [
        pltpu.with_memory_space_constraint(a, pltpu.HBM) if i in spaces else a
        for i, a in enumerate(ins)
    ]
    return pl.pallas_call(
        kernel,
        out_shape=[jax.ShapeDtypeStruct(s, d) for s, d in outs],
        in_specs=[spaces.get(i, whole) for i in range(len(ins))],
        out_specs=[spaces.get(len(ins) + i, whole) for i in range(len(outs))],
        scratch_shapes=list(scratch),
        input_output_aliases=aliases or {},
        compiler_params=pltpu.CompilerParams(vmem_limit_bytes=VMEM_LIMIT),
        cost_estimate=pl.CostEstimate(
            flops=flops, transcendentals=0, bytes_accessed=1 << 20
        ),
    )(*ins)


def position():
    m = lax.axis_index("mp")
    return lax.rem(m, 2), m // 2, lax.rem(lax.axis_index("dp"), 2)


def masked(value, mask):
    wide = jnp.concatenate([mask[...]] * (value.shape[1] // mask.shape[1]), 1)
    return jnp.where(wide > 0, value, 0.0)


def depth():
    return lax.rem(lax.axis_index("dp") // 2, 4)


def forward_kernel(
    capacity, lengths_hbm, feat_hbm, routes_hbm, wi_hbm, wo_hbm,
    a1, a2, sec, ahid, shid, placing, mask, xs, ys, lengths, feat, routes, wi, wo, sems,
):
    frames, ch = a1.shape[1], a1.shape[2]
    hid = wo.shape[0]
    c, _, _ = position()
    rows = frames * STRIDE
    parts = feat.shape[0]
    size = rows // parts
    copies = [
        pltpu.make_async_copy(
            feat_hbm.at[pl.ds(pl.multiple_of(c * rows + i * size, size), size), :],
            feat.at[i],
            sems.at[i],
        )
        for i in range(parts)
    ]
    rest = [
        pltpu.make_async_copy(src, dst, sems.at[parts + i])
        for i, (src, dst) in enumerate(((routes_hbm, routes), (wi_hbm, wi), (wo_hbm, wo)))
    ]
    table = pltpu.make_async_copy(lengths_hbm, lengths, sems.at[parts + len(rest)])
    table.start()
    for copy in copies + rest:
        copy.start()
    table.wait()
    length = lengths[c]
    live = lax.broadcasted_iota(jnp.int32, (frames, ch), 0) < length
    mask[...] = jnp.where(live[:, : mask.shape[1]], 1.0, 0.0)
    for i in range(parts):
        copies[i].wait()
        value = feat[i].astype(F32)
        for k in range(xs.shape[0]):
            xs[k, i * size : (i + 1) * size] = value[:, k * LANES : (k + 1) * LANES]
    for copy in rest:
        copy.wait()
    placing[...] = placing_of(routes[...], placing.shape[0], capacity)
    wcat = jnp.concatenate([wi[k * ch : (k + 1) * ch, :] for k in range(3)], 1)

    def signal(p):
        return jnp.where(live, every(xs, p, frames), 0.0)

    for p in range(STRIDE):
        act = elu(signal(p)).astype(BF)
        a1[p] = act
        ys[p] = mm(act, wcat)
    for p in range(STRIDE):
        left = shift(ys[(p - 1) % STRIDE, :, :hid], -1 if p > 0 else -2)
        right = shift(ys[(p + 1) % STRIDE, :, 2 * hid :], 1 if p < STRIDE - 1 else 2)
        hidden = left + ys[p, :, hid : 2 * hid] + right
        act_hid = elu(hidden).astype(BF)
        ahid[p] = act_hid
        shid[p] = slope(hidden).astype(BF)
        section = jnp.where(live, signal(p) + mm(act_hid, wo[...]), 0.0).astype(BF)
        sec[p] = section
        a2[p] = elu(section.astype(F32)).astype(BF)


def down_kernel(
    mask, a2, dwa, dwb, pa, pb, adown, sdown, lat_send, lat_keep, ls,
):
    frames, ch = a2.shape[1], a2.shape[2]
    _, y, _ = position()
    half = STRIDE // 2

    def tap(k):
        return jnp.concatenate([dwa[k * ch : (k + 1) * ch, :], dwb[k * ch : (k + 1) * ch, :]], 1)

    down = jnp.zeros((frames, 2 * dwa.shape[1]), F32)
    before = jnp.zeros_like(down)
    after = jnp.zeros_like(down)
    for p in range(STRIDE):
        act = a2[p]
        down = down + mm(act, tap(p + half))
        if p < half:
            after = after + mm(act, tap(p + 3 * half))
        else:
            before = before + mm(act, tap(p - half))
    down = down + shift(before, -1) + shift(after, 1)
    act_down = elu(down).astype(BF)
    adown[...] = act_down
    sdown[...] = slope(down)
    proj = jnp.concatenate([pa[...], pb[...]], 0)
    lat = proj.shape[1]
    spread(ls, masked(mm(act_down, proj), mask))
    pieces = frames // STRIDE
    for j in range(half):
        cols = slice(j * lat, (j + 1) * lat)
        lat_send[:, cols] = every(ls, half * (1 - y) + j, pieces).astype(BF)
        lat_keep[:, cols] = every(ls, half * y + j, pieces).astype(BF)


def placing_of(targets, slots, capacity):
    pieces = targets.shape[1]
    chosen = jnp.where(targets == lax.broadcasted_iota(jnp.int32, (128, pieces), 0), 1.0, 0.0)
    upper = (
        lax.broadcasted_iota(jnp.int32, (pieces, pieces), 0)
        < lax.broadcasted_iota(jnp.int32, (pieces, pieces), 1)
    )
    earlier = mm(chosen.astype(BF), jnp.where(upper, 1.0, 0.0).astype(BF))
    rank = jnp.sum(earlier * chosen, axis=0, keepdims=True).astype(jnp.int32)
    slot = targets * capacity + rank
    ids = lax.broadcasted_iota(jnp.int32, (slots, pieces), 0)
    return jnp.where(slot == ids, 1.0, 0.0).astype(BF)


def parts_kernel(whole, *refs):
    *outs, sems = refs
    z = depth()
    copies = [
        pltpu.make_async_copy(whole.at[z ^ k], out, sems.at[k]) for k, out in enumerate(outs)
    ]
    for copy in copies:
        copy.start()
    for copy in copies:
        copy.wait()


def columns_kernel(*refs):
    *parts, send, keep = refs
    _, _, x = position()
    for k, part in enumerate(parts):
        send[k] = part[1 - x]
        keep[k] = part[x]


def assemble(keep, recv, out):
    _, _, x = position()
    z = depth()
    size = keep.shape[1]
    for k in range(keep.shape[0]):
        for part, column in ((keep, x), (recv, 1 - x)):
            at = (2 * (z ^ k) + column) * size
            out[pl.ds(pl.multiple_of(at, size), size), :] = part[k]


def pick_kernel(placing, *refs):
    *parts, own, other, rows, buf = refs
    c, _, _ = position()
    if len(parts) == 1:
        rows[...] = parts[0][...]
    else:
        assemble(*parts, rows)
    buf[...] = mm_tn(placing[...], rows[...])
    half = own.shape[0]
    own[...] = buf[pl.ds(pl.multiple_of(c * half, half), half), :].astype(BF)
    other[...] = buf[pl.ds(pl.multiple_of((1 - c) * half, half), half), :].astype(BF)


def place_kernel(placing, mine, theirs, outgoing, buf):
    c, _, _ = position()
    half = mine.shape[0]
    buf[pl.ds(pl.multiple_of(c * half, half), half), :] = mine[...].astype(F32)
    buf[pl.ds(pl.multiple_of((1 - c) * half, half), half), :] = theirs[...].astype(F32)
    outgoing[...] = mm(placing[...], buf[...].astype(BF)).astype(BF)


def place_parts_kernel(placing, mine, theirs, *refs):
    *outs, buf, rows = refs
    place_kernel(placing, mine, theirs, rows, buf)
    z = depth()
    _, columns, size, _ = (1,) + outs[0].shape
    for k, out in enumerate(outs):
        for i in range(columns):
            at = ((z ^ k) * columns + i) * size
            out[i] = rows[pl.ds(pl.multiple_of(at, size), size), :]


def packed_kernel(keep, recv, out):
    assemble(keep, recv, out)


def lat_mix_kernel(lat_keep, lat_y, mine, theirs):
    c, _, _ = position()
    total = (lat_keep[...].astype(F32) + lat_y[...].astype(F32)).astype(BF)
    cols = mine.shape[1]
    mine[...] = jnp.where(c == 0, total[:, :cols], total[:, cols:])
    theirs[...] = jnp.where(c == 0, total[:, cols:], total[:, :cols])


def section_grad(gd, gshift, wa, wb, part, j, ch):
    half = STRIDE // 2
    first = part * half + j + half
    second = jnp.where(part == 0, 3 * half + j, j)
    rows1 = pl.ds(pl.multiple_of(first * ch, ch), ch)
    rows2 = pl.ds(pl.multiple_of(second * ch, ch), ch)
    w1 = jnp.concatenate([wa[rows1, :], wb[rows1, :]], 1)
    w2 = jnp.concatenate([wa[rows2, :], wb[rows2, :]], 1)
    return mm_nt(gd, w1) + mm_nt(gshift, w2)


def moved(gd, part):
    g = gd.astype(F32)
    return jnp.where(part == 0, shift(g, -1), shift(g, 1)).astype(BF)


def latent_grad_kernel(
    mask, g_own, g_core, g_y, g_far, adown, sdown, pa, pb,
    gd_out, swap, gproj_keep, gl,
):
    frames = adown.shape[0]
    width, lat = pa.shape
    pieces = g_own.shape[0]
    c, y, _ = position()
    blocks = (
        (g_own, 2 * y + c),
        (g_core, 2 * y + 1 - c),
        (g_y, 2 * (1 - y) + c),
        (g_far, 2 * (1 - y) + 1 - c),
    )
    for block, owner in blocks:
        for j in range(2):
            for i in range(gl.shape[0]):
                at = j * lat + i * LANES
                gl[i, pl.ds(2 * owner + j, pieces, stride=STRIDE), :] = block[
                    :, at : at + LANES
                ].astype(F32)
    g_latent = masked(jnp.concatenate([gl[i] for i in range(gl.shape[0])], 1), mask).astype(BF)
    proj = jnp.concatenate([pa[...], pb[...]], 0)
    gd = (mm_nt(g_latent, proj) * sdown[...]).astype(BF)
    gd_out[...] = gd
    swap[:frames] = gd[:, width:]
    gproj = mm_tn(adown[...], g_latent)
    swap[frames : frames + width] = gproj[width:, :width].astype(BF)
    swap[frames + width :] = gproj[width:, width:].astype(BF)
    gproj_keep[:width] = gproj[:width, :width]
    gproj_keep[width:] = gproj[:width, width:]


def section_send_kernel(gd, dwa, dwb, send):
    _, y, _ = position()
    full = gd[...]
    g2 = moved(full, 1 - y)
    for j in range(STRIDE // 2):
        send[j] = section_grad(full, g2, dwa, dwb, 1 - y, j, send.shape[2]).astype(BF)


def section_keep_kernel(gd, dwa, dwb, keep):
    _, y, _ = position()
    full = gd[...]
    g2 = moved(full, y)
    for j in range(STRIDE // 2):
        keep[j] = section_grad(full, g2, dwa, dwb, y, j, keep.shape[2])


def weight_grads(a2a, a2b, ga, gb, part, j):
    half = STRIDE // 2
    p = part * half + j
    return mm_tn(a2a[p], ga) + mm_tn(a2b[p], gb)


def pair(g, part):
    return jnp.concatenate([g, moved(g, part)], 1)


def down_send_kernel(a2a, a2b, gd, swap, gproj, send_u, send_s):
    frames = gd.shape[0]
    width = swap.shape[1]
    _, _, x = position()
    ga = pair(gd[:, :width], x)
    gb = pair(swap[:frames], x)
    extra = send_s.shape[1] - send_u.shape[1]
    rows = send_u.shape[1]
    for j in range(STRIDE // 2):
        w = weight_grads(a2a, a2b, ga, gb, x, j)
        send_u[j] = w[:, :width].astype(BF)
        send_s[j, :rows] = w[:, width:].astype(BF)
        at = pl.ds(pl.multiple_of(((1 - x) * 4 + j) * extra, extra), extra)
        send_s[j, rows:] = (gproj[at, :] + swap[pl.ds(pl.multiple_of(frames + ((1 - x) * 4 + j) * extra, extra), extra), :].astype(F32)).astype(BF)


def down_keep_kernel(a2a, a2b, gd, swap, gproj, keep_u, keep_s):
    frames = gd.shape[0]
    width = swap.shape[1]
    _, _, x = position()
    part = 1 - x
    ga = pair(gd[:, :width], part)
    gb = pair(swap[:frames], part)
    extra = keep_s.shape[1] - keep_u.shape[1]
    rows = keep_u.shape[1]
    for j in range(STRIDE // 2):
        w = weight_grads(a2a, a2b, ga, gb, part, j)
        keep_u[j] = w[:, :width]
        keep_s[j, :rows] = w[:, width:]
        at = pl.ds(pl.multiple_of((x * 4 + j) * extra, extra), extra)
        keep_s[j, rows:] = gproj[at, :] + swap[pl.ds(pl.multiple_of(frames + (x * 4 + j) * extra, extra), extra), :].astype(F32)


def residual_kernel(
    mask, keep, recv, sec, ahid, shid, wo, a1, kept, send1, send2, send3, gh, buf,
):
    half = STRIDE // 2
    ch = keep.shape[2]
    hid = wo.shape[0]
    c, y, _ = position()
    g_out = jnp.zeros((hid, ch), F32)
    for j in range(half):
        g = keep[j] + recv[j].astype(F32)
        g_branch = masked(g * slope(sec[y * half + j].astype(F32)), mask).astype(BF)
        g_out = g_out + mm_tn(ahid[y * half + j], g_branch)
        gh[j] = mm_nt(g_branch, wo[...]) * shid[y * half + j].astype(F32)
    taps = [jnp.zeros((ch, hid), F32) for _ in range(3)]
    for j in range(half):
        g = gh[j]
        p = y * half + j
        here = g.astype(BF)
        taps[1] = taps[1] + mm_tn(a1[p], here)
        down1 = shift(g, 1)
        up1 = shift(g, -1)
        if j == 0:
            down1 = jnp.where(y == 0, shift(g, 2), down1)
        if j == half - 1:
            up1 = jnp.where(y == 1, shift(g, -2), up1)
        taps[0] = taps[0] + mm_tn(a1[lax.rem(p + STRIDE - 1, STRIDE)], down1.astype(BF))
        taps[2] = taps[2] + mm_tn(a1[lax.rem(p + 1, STRIDE)], up1.astype(BF))
    for k in range(3):
        for i in range(ch // hid):
            buf[k * (ch // hid) + i] = taps[k][i * hid : (i + 1) * hid]
    for i in range(ch // hid):
        buf[3 * (ch // hid) + i] = g_out[:, i * hid : (i + 1) * hid]
    m = 2 * y + c
    n = buf.shape[0] // 4
    for i in range(n):
        at = slice(i * hid, (i + 1) * hid)
        kept[at] = buf[m * n + i]
        for k, out in enumerate((send1, send2, send3)):
            out[at] = buf[(m ^ (k + 1)) * n + i].astype(BF)


def residual_finish_kernel(r0, r1, r2, r3, out_in, out_out, buf):
    c, y, _ = position()
    m = 2 * y + c
    rows, hid = r0.shape
    for k, r in enumerate((r0, r1, r2, r3)):
        buf[m ^ k] = r[...].astype(F32)
    for q in range(3):
        out_in[q * rows : (q + 1) * rows] = buf[q]
    for i in range(rows // hid):
        out_out[:, i * hid : (i + 1) * hid] = buf[3, i * hid : (i + 1) * hid]


def sum_kernel(keep, recv, own, *sends):
    z = depth()
    own[...] = keep[z] + recv[z].astype(F32)
    for k, out in enumerate(sends):
        at = z ^ (k + 1)
        out[...] = (keep[at] + recv[at].astype(F32)).astype(BF)


def swap_bit(value, axis, bit):
    n = lax.axis_size(axis)
    return lax.ppermute(value, axis, [(i, i ^ bit) for i in range(n)])


def stages_of(n):
    found, bit = [], 2
    while bit < n:
        members = 4 if n // bit >= 4 else 2
        found.append((bit, members))
        bit *= members
    return found


def pick(stack, index):
    return lax.dynamic_index_in_dim(stack, index, 0, keepdims=False)


def fan(values, axis, bit):
    return [swap_bit(v, axis, bit * (k + 1)) for k, v in enumerate(values)]


def plus(total, received):
    for r in received:
        total = total + r.astype(F32)
    return total


def reduce_rest(kept, received, me, stages):
    shape = kept.shape[1:]
    own, *sends = call(sum_kernel, [(shape, F32)] + [(shape, BF)] * 3, [kept, received])
    total = plus(own, fan(sends, "dp", stages[0][0]))
    for bit, members in stages[1:]:
        parts = total.reshape(members, -1, total.shape[-1])
        place = (me // bit) % members
        sends = [pick(parts, place ^ k).astype(BF) for k in range(1, members)]
        total = plus(pick(parts, place), fan(sends, "dp", bit))
    return total.astype(BF)


def gather_rest(own, me, stages):
    for bit, members in reversed(stages[1:]):
        place = (me // bit) % members
        blocks = [own] + fan([own] * (members - 1), "dp", bit)
        ordered = jnp.stack(blocks)
        own = jnp.concatenate([pick(ordered, place ^ k) for k in range(members)], 0)
    return [own] + fan([own] * 3, "dp", stages[0][0])


def finish_kernel(shifted, *refs):
    if shifted:
        m0, m1, m2, m3, theirs, _, out, out_proj, buf, sems = refs
        per = out_proj.shape[0] * 2 // STRIDE
    else:
        m0, m1, m2, m3, theirs, out, buf, sems = refs
    _, _, x = position()
    z = depth()
    half = STRIDE // 2
    rows = buf.shape[1]
    copies = []
    for k, mine in enumerate((m0, m1, m2, m3)):
        j = z ^ k
        for i, (value, part, xp) in enumerate(((mine, 1 - x, x), (theirs.at[k], x, 1 - x))):
            tap = part * half + j + half
            if shifted:
                tap = jnp.where(part == 0, 3 * half + j, j)
            n = 2 * k + i
            buf[n] = value[:rows].astype(F32)
            copy = pltpu.make_async_copy(
                buf.at[n],
                out.at[pl.ds(pl.multiple_of(tap * rows, rows), rows), :],
                sems.at[n],
            )
            copy.start()
            copies.append(copy)
            if shifted:
                where = pl.ds(pl.multiple_of(j * per, per), per)
                width = value.shape[1]
                extra = value[rows:].astype(F32)

                @pl.when(xp == 0)
                def _():
                    out_proj[where, :width] = extra

                @pl.when(xp == 1)
                def _():
                    out_proj[where, width:] = extra

    for copy in copies:
        copy.wait()


def body(
    features, lengths, routes, res_in_weight, res_out_weight, down_weight, proj_weight, cotangent
):
    utts = lengths.shape[0]
    total_rows = features.shape[0] // utts
    ch = features.shape[1]
    frames = total_rows // STRIDE
    hid = res_out_weight.shape[0]
    width = down_weight.shape[1]
    lat = proj_weight.shape[1]
    dp_count = lax.axis_size("dp")
    pieces = routes.shape[0]
    half_pieces = pieces // utts
    capacity = 2 * pieces // dp_count
    slots = dp_count * capacity
    cols = cotangent.shape[1]
    half = STRIDE // 2
    me_dp = lax.axis_index("dp")
    stages = stages_of(dp_count)
    staged = dp_count == 8
    lane_block = ((dp_count // 2, capacity, cols), BF)
    pair_block = ((2, capacity, cols), BF)

    def through_dp(parts):
        received = fan(parts[1:], "dp", 2)
        send, keep = call(columns_kernel, [lane_block] * 2, [parts[0], *received])
        return keep, swap_bit(send, "dp", 1)

    def all_to_all(value):
        return lax.all_to_all(
            value.reshape(dp_count, capacity, cols), "dp", split_axis=0, concat_axis=0
        ).reshape(slots, cols)

    other_down = swap_bit(down_weight, "mp", 1)
    other_proj = swap_bit(proj_weight, "mp", 1)
    if staged:
        parts = call(
            parts_kernel,
            [pair_block] * 4,
            [cotangent.reshape(dp_count // 2, 2, capacity, cols)],
            scratch=[pltpu.SemaphoreType.DMA((4,))],
            where={0: pltpu.HBM},
        )
        returned = through_dp(parts)
    else:
        returned = [all_to_all(cotangent)]

    loads = 4
    a1, a2, sec, ahid, shid, placing, mask = call(
        functools.partial(forward_kernel, capacity),
        [
            ((STRIDE, frames, ch), BF),
            ((STRIDE, frames, ch), BF),
            ((STRIDE, frames, ch), BF),
            ((STRIDE, frames, hid), BF),
            ((STRIDE, frames, hid), BF),
            ((slots, pieces), BF),
            ((frames, LANES), F32),
        ],
        [lengths, features, routes.reshape(1, pieces), res_in_weight, res_out_weight],
        scratch=[
            pltpu.VMEM((ch // LANES, total_rows, LANES), F32),
            pltpu.VMEM((STRIDE, frames, 3 * hid), F32),
            pltpu.SMEM(lengths.shape, lengths.dtype),
            pltpu.VMEM((loads, total_rows // loads, ch), BF),
            pltpu.VMEM((1, pieces), routes.dtype),
            pltpu.VMEM(res_in_weight.shape, BF),
            pltpu.VMEM(res_out_weight.shape, BF),
            pltpu.SemaphoreType.DMA((loads + 4,)),
        ],
        where={i: pltpu.HBM for i in range(5)},
        flops=4 << 30,
    )
    other_a2 = swap_bit(a2, "mp", 1)
    adown, sdown, lat_send, lat_keep = call(
        down_kernel,
        [
            ((frames, 2 * width), BF),
            ((frames, 2 * width), F32),
            ((half_pieces, half * lat), BF),
            ((half_pieces, half * lat), BF),
        ],
        [mask, a2, down_weight, other_down, proj_weight, other_proj],
        scratch=[pltpu.VMEM((lat // LANES, frames, LANES), F32)],
        flops=1 << 30,
    )
    lat_y = swap_bit(lat_send, "mp", 2)

    g_own, g_other = call(
        pick_kernel,
        [((half_pieces, cols), BF), ((half_pieces, cols), BF)],
        [placing, *returned],
        scratch=[pltpu.VMEM((slots, cols), BF), pltpu.VMEM((pieces, cols), F32)],
    )
    g_y = swap_bit(g_own, "mp", 2)
    g_far = swap_bit(g_other, "mp", 3)
    g_core = swap_bit(g_other, "mp", 1)

    mine, theirs = call(lat_mix_kernel, [((half_pieces, cols), BF)] * 2, [lat_keep, lat_y])
    theirs = swap_bit(theirs, "mp", 1)

    gd, swap, gproj = call(
        latent_grad_kernel,
        [
            ((frames, 2 * width), BF),
            ((frames + 2 * width, width), BF),
            ((2 * width, lat // 2), F32),
        ],
        [mask, g_own, g_core, g_y, g_far, adown, sdown, proj_weight, other_proj],
        scratch=[pltpu.VMEM((lat // LANES, frames, LANES), F32)],
        flops=1 << 30,
    )
    got = swap_bit(swap, "mp", 1)
    (g_send,) = call(
        section_send_kernel,
        [((half, frames, ch), BF)],
        [gd, down_weight, other_down],
        flops=1 << 29,
    )
    g_recv = swap_bit(g_send, "mp", 2)
    extra = 2 * width // STRIDE
    send_u, send_s = call(
        down_send_kernel,
        [((half, ch, width), BF), ((half, ch + extra, width), BF)],
        [a2, other_a2, gd, got, gproj],
        flops=1 << 29,
    )
    recv_u = swap_bit(send_u, "dp", 1)
    recv_s = swap_bit(send_s, "dp", 1)
    keep_u, keep_s = call(
        down_keep_kernel,
        [((half, ch, width), F32), ((half, ch + extra, width), F32)],
        [a2, other_a2, gd, got, gproj],
        flops=1 << 29,
    )
    (keep_g,) = call(
        section_keep_kernel,
        [((half, frames, ch), F32)],
        [gd, down_weight, other_down],
        flops=1 << 29,
    )

    row_scratch = pltpu.VMEM((pieces, cols), F32)
    if staged:
        parts = call(
            place_parts_kernel,
            [pair_block] * 4,
            [placing, mine, theirs],
            scratch=[row_scratch, pltpu.VMEM((slots, cols), BF)],
        )
        (packed,) = call(packed_kernel, [((slots, cols), BF)], [*through_dp(parts)])
    else:
        (outgoing,) = call(
            place_kernel, [((slots, cols), BF)], [placing, mine, theirs], scratch=[row_scratch]
        )
        packed = all_to_all(outgoing)

    blocks = 4 * (ch // hid)
    quarter = (blocks // 4 * hid, hid)
    e_own, *e_sends = call(
        residual_kernel,
        [(quarter, F32)] + [(quarter, BF)] * 3,
        [mask, keep_g, g_recv, sec, ahid, shid, res_out_weight, a1],
        scratch=[pltpu.VMEM((half, frames, hid), F32), pltpu.VMEM((blocks, hid, hid), F32)],
        flops=1 << 30,
    )
    e_own = plus(e_own, fan(e_sends, "mp", 1))
    e_own = plus(e_own, [swap_bit(e_own.astype(BF), "dp", 1)])
    for bit, members in stages:
        sent = e_own.astype(BF)
        e_own = plus(e_own, fan([sent] * (members - 1), "dp", bit))
    sent = e_own.astype(BF)
    grad_res_in, grad_res_out = call(
        residual_finish_kernel,
        [((3 * ch, hid), F32), ((hid, ch), F32)],
        [sent, *fan([sent] * 3, "mp", 1)],
        scratch=[pltpu.VMEM((4,) + quarter, F32)],
    )

    all_u = gather_rest(reduce_rest(keep_u, recv_u, me_dp, stages), me_dp, stages)
    their_u = swap_bit(jnp.stack(all_u), "dp", 1)
    all_s = gather_rest(reduce_rest(keep_s, recv_s, me_dp, stages), me_dp, stages)
    their_s = swap_bit(jnp.stack(all_s), "dp", 1)
    down_out = ((2 * STRIDE * ch, width), F32)
    taps = [pltpu.VMEM((STRIDE, ch, width), F32), pltpu.SemaphoreType.DMA((STRIDE,))]
    (grad_down,) = call(
        functools.partial(finish_kernel, False),
        [down_out],
        [*all_u, their_u],
        scratch=taps,
        where={5: pltpu.HBM},
    )
    grad_down, grad_proj = call(
        functools.partial(finish_kernel, True),
        [down_out, ((width, lat), F32)],
        [*all_s, their_s, grad_down],
        scratch=taps,
        where={5: pltpu.HBM, 6: pltpu.HBM},
        aliases={5: 0},
    )
    return (packed, grad_res_in, grad_res_out, grad_down, grad_proj)


def solution(mesh):
    return jax.shard_map(
        body,
        mesh=mesh,
        in_specs=(
            P("dp", None),
            P("dp"),
            P("dp", None),
            P(),
            P(),
            P(None, "mp"),
            P("mp", None),
            P("dp", "mp"),
        ),
        out_specs=(P("dp", "mp"), P(), P(), P(None, "mp"), P("mp", None)),
        check_vma=False,
    )
```

```python
import functools
import jax
import jax.numpy as jnp
from jax import lax
from jax.experimental import pallas as pl
from jax.experimental.pallas import tpu as pltpu
from jax.sharding import PartitionSpec as P

STRIDE = 8
DP, MP = "dp", "mp"
LANES = 128
BF = jnp.bfloat16
F32 = jnp.float32
VMEM_LIMIT = 16 << 20


def elu(v):
    return jnp.where(v > 0, v, jnp.exp(jnp.minimum(v, 0.0)) - 1.0)


def slope(v):
    return jnp.where(v > 0, 1.0, jnp.exp(jnp.minimum(v, 0.0)))


def mm(a, b):
    return jnp.dot(a, b, preferred_element_type=F32)


def mm_nt(a, b):
    return lax.dot_general(a, b, (((1,), (1,)), ((), ())), preferred_element_type=F32)


def mm_tn(a, b):
    return lax.dot_general(a, b, (((0,), (0,)), ((), ())), preferred_element_type=F32)


def shift(v, s):
    n = v.shape[0]
    rows = lax.broadcasted_iota(jnp.int32, v.shape, 0)
    rolled = pltpu.roll(v, (-s) % n, 0)
    keep = rows < n - s if s > 0 else rows >= -s
    return jnp.where(keep, rolled, 0.0)


def spread(ref, value):
    for i in range(ref.shape[0]):
        ref[i] = value[:, i * LANES : (i + 1) * LANES]


def every(ref, start, size):
    return jnp.concatenate(
        [ref[i, pl.ds(start, size, stride=STRIDE), :] for i in range(ref.shape[0])], 1
    )


def call(kernel, outs, ins, scratch=(), flops=0, where=None, aliases=None):
    whole = pl.BlockSpec(memory_space=pltpu.VMEM)
    spaces = {i: pl.BlockSpec(memory_space=space) for i, space in (where or {}).items()}
    ins = [
        pltpu.with_memory_space_constraint(a, pltpu.HBM) if i in spaces else a
        for i, a in enumerate(ins)
    ]
    return pl.pallas_call(
        kernel,
        out_shape=[jax.ShapeDtypeStruct(s, d) for s, d in outs],
        in_specs=[spaces.get(i, whole) for i in range(len(ins))],
        out_specs=[spaces.get(len(ins) + i, whole) for i in range(len(outs))],
        scratch_shapes=list(scratch),
        input_output_aliases=aliases or {},
        compiler_params=pltpu.CompilerParams(vmem_limit_bytes=VMEM_LIMIT),
        cost_estimate=pl.CostEstimate(
            flops=flops, transcendentals=0, bytes_accessed=1 << 20
        ),
    )(*ins)


def position():
    m = lax.axis_index(MP)
    return lax.rem(m, 2), m // 2, lax.rem(lax.axis_index(DP), 2)


def masked(value, mask):
    wide = jnp.concatenate([mask[...]] * (value.shape[1] // mask.shape[1]), 1)
    return jnp.where(wide > 0, value, 0.0)


def depth():
    return lax.rem(lax.axis_index(DP) // 2, 4)


def forward_kernel(
    capacity, lengths_hbm, feat_hbm, routes_hbm, wi_hbm, wo_hbm,
    a1, a2, sec, ahid, shid, placing, mask, xs, ys, lengths, feat, routes, wi, wo, sems,
):
    frames, ch = a1.shape[1], a1.shape[2]
    hid = wo.shape[0]
    c, _, _ = position()
    rows = frames * STRIDE
    parts = feat.shape[0]
    size = rows // parts
    copies = [
        pltpu.make_async_copy(
            feat_hbm.at[pl.ds(pl.multiple_of(c * rows + i * size, size), size), :],
            feat.at[i],
            sems.at[i],
        )
        for i in range(parts)
    ]
    rest = [
        pltpu.make_async_copy(src, dst, sems.at[parts + i])
        for i, (src, dst) in enumerate(((routes_hbm, routes), (wi_hbm, wi), (wo_hbm, wo)))
    ]
    table = pltpu.make_async_copy(lengths_hbm, lengths, sems.at[parts + len(rest)])
    table.start()
    for copy in copies + rest:
        copy.start()
    table.wait()
    length = lengths[c]
    live = lax.broadcasted_iota(jnp.int32, (frames, ch), 0) < length
    mask[...] = jnp.where(live[:, : mask.shape[1]], 1.0, 0.0)
    for i in range(parts):
        copies[i].wait()
        value = feat[i].astype(F32)
        for k in range(xs.shape[0]):
            xs[k, i * size : (i + 1) * size] = value[:, k * LANES : (k + 1) * LANES]
    for copy in rest:
        copy.wait()
    placing[...] = placing_of(routes[...], placing.shape[0], capacity)
    wcat = jnp.concatenate([wi[k * ch : (k + 1) * ch, :] for k in range(3)], 1)

    def signal(p):
        return jnp.where(live, every(xs, p, frames), 0.0)

    for p in range(STRIDE):
        act = elu(signal(p)).astype(BF)
        a1[p] = act
        ys[p] = mm(act, wcat)
    for p in range(STRIDE):
        left = shift(ys[(p - 1) % STRIDE, :, :hid], -1 if p > 0 else -2)
        right = shift(ys[(p + 1) % STRIDE, :, 2 * hid :], 1 if p < STRIDE - 1 else 2)
        hidden = left + ys[p, :, hid : 2 * hid] + right
        act_hid = elu(hidden).astype(BF)
        ahid[p] = act_hid
        shid[p] = slope(hidden).astype(BF)
        section = jnp.where(live, signal(p) + mm(act_hid, wo[...]), 0.0).astype(BF)
        sec[p] = section
        a2[p] = elu(section.astype(F32)).astype(BF)


def down_kernel(
    mask, a2, dwa, dwb, pa, pb, adown, sdown, lat_send, lat_keep, ls,
):
    frames, ch = a2.shape[1], a2.shape[2]
    _, y, _ = position()
    half = STRIDE // 2

    def tap(k):
        return jnp.concatenate([dwa[k * ch : (k + 1) * ch, :], dwb[k * ch : (k + 1) * ch, :]], 1)

    down = jnp.zeros((frames, 2 * dwa.shape[1]), F32)
    before = jnp.zeros_like(down)
    after = jnp.zeros_like(down)
    for p in range(STRIDE):
        act = a2[p]
        down = down + mm(act, tap(p + half))
        if p < half:
            after = after + mm(act, tap(p + 3 * half))
        else:
            before = before + mm(act, tap(p - half))
    down = down + shift(before, -1) + shift(after, 1)
    act_down = elu(down).astype(BF)
    adown[...] = act_down
    sdown[...] = slope(down)
    proj = jnp.concatenate([pa[...], pb[...]], 0)
    lat = proj.shape[1]
    spread(ls, masked(mm(act_down, proj), mask))
    pieces = frames // STRIDE
    for j in range(half):
        cols = slice(j * lat, (j + 1) * lat)
        lat_send[:, cols] = every(ls, half * (1 - y) + j, pieces).astype(BF)
        lat_keep[:, cols] = every(ls, half * y + j, pieces).astype(BF)


def placing_of(targets, slots, capacity):
    pieces = targets.shape[1]
    chosen = jnp.where(targets == lax.broadcasted_iota(jnp.int32, (128, pieces), 0), 1.0, 0.0)
    upper = (
        lax.broadcasted_iota(jnp.int32, (pieces, pieces), 0)
        < lax.broadcasted_iota(jnp.int32, (pieces, pieces), 1)
    )
    earlier = mm(chosen.astype(BF), jnp.where(upper, 1.0, 0.0).astype(BF))
    rank = jnp.sum(earlier * chosen, axis=0, keepdims=True).astype(jnp.int32)
    slot = targets * capacity + rank
    ids = lax.broadcasted_iota(jnp.int32, (slots, pieces), 0)
    return jnp.where(slot == ids, 1.0, 0.0).astype(BF)


def parts_kernel(whole, *refs):
    *outs, sems = refs
    z = depth()
    copies = [
        pltpu.make_async_copy(whole.at[z ^ k], out, sems.at[k]) for k, out in enumerate(outs)
    ]
    for copy in copies:
        copy.start()
    for copy in copies:
        copy.wait()


def columns_kernel(*refs):
    *parts, send, keep = refs
    _, _, x = position()
    for k, part in enumerate(parts):
        send[k] = part[1 - x]
        keep[k] = part[x]


def assemble(keep, recv, out):
    _, _, x = position()
    z = depth()
    size = keep.shape[1]
    for k in range(keep.shape[0]):
        for part, column in ((keep, x), (recv, 1 - x)):
            at = (2 * (z ^ k) + column) * size
            out[pl.ds(pl.multiple_of(at, size), size), :] = part[k]


def pick_kernel(placing, *refs):
    *parts, own, other, rows, buf = refs
    c, _, _ = position()
    if len(parts) == 1:
        rows[...] = parts[0][...]
    else:
        assemble(*parts, rows)
    buf[...] = mm_tn(placing[...], rows[...])
    half = own.shape[0]
    own[...] = buf[pl.ds(pl.multiple_of(c * half, half), half), :].astype(BF)
    other[...] = buf[pl.ds(pl.multiple_of((1 - c) * half, half), half), :].astype(BF)


def place_kernel(placing, mine, theirs, outgoing, buf):
    c, _, _ = position()
    half = mine.shape[0]
    buf[pl.ds(pl.multiple_of(c * half, half), half), :] = mine[...].astype(F32)
    buf[pl.ds(pl.multiple_of((1 - c) * half, half), half), :] = theirs[...].astype(F32)
    outgoing[...] = mm(placing[...], buf[...].astype(BF)).astype(BF)


def place_parts_kernel(placing, mine, theirs, *refs):
    *outs, buf, rows = refs
    place_kernel(placing, mine, theirs, rows, buf)
    z = depth()
    _, columns, size, _ = (1,) + outs[0].shape
    for k, out in enumerate(outs):
        for i in range(columns):
            at = ((z ^ k) * columns + i) * size
            out[i] = rows[pl.ds(pl.multiple_of(at, size), size), :]


def packed_kernel(keep, recv, out):
    assemble(keep, recv, out)


def lat_mix_kernel(lat_keep, lat_y, mine, theirs):
    c, _, _ = position()
    total = (lat_keep[...].astype(F32) + lat_y[...].astype(F32)).astype(BF)
    cols = mine.shape[1]
    mine[...] = jnp.where(c == 0, total[:, :cols], total[:, cols:])
    theirs[...] = jnp.where(c == 0, total[:, cols:], total[:, :cols])


def section_grad(gd, gshift, wa, wb, part, j, ch):
    half = STRIDE // 2
    first = part * half + j + half
    second = jnp.where(part == 0, 3 * half + j, j)
    rows1 = pl.ds(pl.multiple_of(first * ch, ch), ch)
    rows2 = pl.ds(pl.multiple_of(second * ch, ch), ch)
    w1 = jnp.concatenate([wa[rows1, :], wb[rows1, :]], 1)
    w2 = jnp.concatenate([wa[rows2, :], wb[rows2, :]], 1)
    return mm_nt(gd, w1) + mm_nt(gshift, w2)


def moved(gd, part):
    g = gd.astype(F32)
    return jnp.where(part == 0, shift(g, -1), shift(g, 1)).astype(BF)


def latent_grad_kernel(
    mask, g_own, g_core, g_y, g_far, adown, sdown, pa, pb,
    gd_out, swap, gproj_keep, gl,
):
    frames = adown.shape[0]
    width, lat = pa.shape
    pieces = g_own.shape[0]
    c, y, _ = position()
    blocks = (
        (g_own, 2 * y + c),
        (g_core, 2 * y + 1 - c),
        (g_y, 2 * (1 - y) + c),
        (g_far, 2 * (1 - y) + 1 - c),
    )
    for block, owner in blocks:
        for j in range(2):
            for i in range(gl.shape[0]):
                at = j * lat + i * LANES
                gl[i, pl.ds(2 * owner + j, pieces, stride=STRIDE), :] = block[
                    :, at : at + LANES
                ].astype(F32)
    g_latent = masked(jnp.concatenate([gl[i] for i in range(gl.shape[0])], 1), mask).astype(BF)
    proj = jnp.concatenate([pa[...], pb[...]], 0)
    gd = (mm_nt(g_latent, proj) * sdown[...]).astype(BF)
    gd_out[...] = gd
    swap[:frames] = gd[:, width:]
    gproj = mm_tn(adown[...], g_latent)
    swap[frames : frames + width] = gproj[width:, :width].astype(BF)
    swap[frames + width :] = gproj[width:, width:].astype(BF)
    gproj_keep[:width] = gproj[:width, :width]
    gproj_keep[width:] = gproj[:width, width:]


def section_send_kernel(gd, dwa, dwb, send):
    _, y, _ = position()
    full = gd[...]
    g2 = moved(full, 1 - y)
    for j in range(STRIDE // 2):
        send[j] = section_grad(full, g2, dwa, dwb, 1 - y, j, send.shape[2]).astype(BF)


def section_keep_kernel(gd, dwa, dwb, keep):
    _, y, _ = position()
    full = gd[...]
    g2 = moved(full, y)
    for j in range(STRIDE // 2):
        keep[j] = section_grad(full, g2, dwa, dwb, y, j, keep.shape[2])


def weight_grads(a2a, a2b, ga, gb, part, j):
    half = STRIDE // 2
    p = part * half + j
    return mm_tn(a2a[p], ga) + mm_tn(a2b[p], gb)


def pair(g, part):
    return jnp.concatenate([g, moved(g, part)], 1)


def down_send_kernel(a2a, a2b, gd, swap, gproj, send_u, send_s):
    frames = gd.shape[0]
    width = swap.shape[1]
    _, _, x = position()
    ga = pair(gd[:, :width], x)
    gb = pair(swap[:frames], x)
    extra = send_s.shape[1] - send_u.shape[1]
    rows = send_u.shape[1]
    for j in range(STRIDE // 2):
        w = weight_grads(a2a, a2b, ga, gb, x, j)
        send_u[j] = w[:, :width].astype(BF)
        send_s[j, :rows] = w[:, width:].astype(BF)
        at = pl.ds(pl.multiple_of(((1 - x) * 4 + j) * extra, extra), extra)
        send_s[j, rows:] = (gproj[at, :] + swap[pl.ds(pl.multiple_of(frames + ((1 - x) * 4 + j) * extra, extra), extra), :].astype(F32)).astype(BF)


def down_keep_kernel(a2a, a2b, gd, swap, gproj, keep_u, keep_s):
    frames = gd.shape[0]
    width = swap.shape[1]
    _, _, x = position()
    part = 1 - x
    ga = pair(gd[:, :width], part)
    gb = pair(swap[:frames], part)
    extra = keep_s.shape[1] - keep_u.shape[1]
    rows = keep_u.shape[1]
    for j in range(STRIDE // 2):
        w = weight_grads(a2a, a2b, ga, gb, part, j)
        keep_u[j] = w[:, :width]
        keep_s[j, :rows] = w[:, width:]
        at = pl.ds(pl.multiple_of((x * 4 + j) * extra, extra), extra)
        keep_s[j, rows:] = gproj[at, :] + swap[pl.ds(pl.multiple_of(frames + (x * 4 + j) * extra, extra), extra), :].astype(F32)


def residual_kernel(
    mask, keep, recv, sec, ahid, shid, wo, a1, kept, send1, send2, send3, gh, buf,
):
    half = STRIDE // 2
    ch = keep.shape[2]
    hid = wo.shape[0]
    c, y, _ = position()
    g_out = jnp.zeros((hid, ch), F32)
    for j in range(half):
        g = keep[j] + recv[j].astype(F32)
        g_branch = masked(g * slope(sec[y * half + j].astype(F32)), mask).astype(BF)
        g_out = g_out + mm_tn(ahid[y * half + j], g_branch)
        gh[j] = mm_nt(g_branch, wo[...]) * shid[y * half + j].astype(F32)
    taps = [jnp.zeros((ch, hid), F32) for _ in range(3)]
    for j in range(half):
        g = gh[j]
        p = y * half + j
        here = g.astype(BF)
        taps[1] = taps[1] + mm_tn(a1[p], here)
        down1 = shift(g, 1)
        up1 = shift(g, -1)
        if j == 0:
            down1 = jnp.where(y == 0, shift(g, 2), down1)
        if j == half - 1:
            up1 = jnp.where(y == 1, shift(g, -2), up1)
        taps[0] = taps[0] + mm_tn(a1[lax.rem(p + STRIDE - 1, STRIDE)], down1.astype(BF))
        taps[2] = taps[2] + mm_tn(a1[lax.rem(p + 1, STRIDE)], up1.astype(BF))
    for k in range(3):
        for i in range(ch // hid):
            buf[k * (ch // hid) + i] = taps[k][i * hid : (i + 1) * hid]
    for i in range(ch // hid):
        buf[3 * (ch // hid) + i] = g_out[:, i * hid : (i + 1) * hid]
    m = 2 * y + c
    n = buf.shape[0] // 4
    for i in range(n):
        at = slice(i * hid, (i + 1) * hid)
        kept[at] = buf[m * n + i]
        for k, out in enumerate((send1, send2, send3)):
            out[at] = buf[(m ^ (k + 1)) * n + i].astype(BF)


def residual_finish_kernel(r0, r1, r2, r3, out_in, out_out, buf):
    c, y, _ = position()
    m = 2 * y + c
    rows, hid = r0.shape
    for k, r in enumerate((r0, r1, r2, r3)):
        buf[m ^ k] = r[...].astype(F32)
    for q in range(3):
        out_in[q * rows : (q + 1) * rows] = buf[q]
    for i in range(rows // hid):
        out_out[:, i * hid : (i + 1) * hid] = buf[3, i * hid : (i + 1) * hid]


def sum_kernel(keep, recv, own, *sends):
    z = depth()
    own[...] = keep[z] + recv[z].astype(F32)
    for k, out in enumerate(sends):
        at = z ^ (k + 1)
        out[...] = (keep[at] + recv[at].astype(F32)).astype(BF)


def swap_bit(value, axis, bit):
    n = lax.axis_size(axis)
    return lax.ppermute(value, axis, [(i, i ^ bit) for i in range(n)])


def stages_of(n):
    found, bit = [], 2
    while bit < n:
        members = 4 if n // bit >= 4 else 2
        found.append((bit, members))
        bit *= members
    return found


def pick(stack, index):
    return lax.dynamic_index_in_dim(stack, index, 0, keepdims=False)


def fan(values, axis, bit):
    return [swap_bit(v, axis, bit * (k + 1)) for k, v in enumerate(values)]


def plus(total, received):
    for r in received:
        total = total + r.astype(F32)
    return total


def reduce_rest(kept, received, me, stages):
    shape = kept.shape[1:]
    own, *sends = call(sum_kernel, [(shape, F32)] + [(shape, BF)] * 3, [kept, received])
    received = fan(sends, DP, stages[0][0])
    for bit, members in stages[1:]:
        parts = plus(own, received).reshape(members, -1, own.shape[-1])
        place = (me // bit) % members
        sends = [pick(parts, place ^ k).astype(BF) for k in range(1, members)]
        own, received = pick(parts, place), fan(sends, DP, bit)
    return plus(own, received).astype(BF)


def gather_rest(own, me, stages):
    for bit, members in reversed(stages[1:]):
        place = (me // bit) % members
        blocks = [own] + fan([own] * (members - 1), DP, bit)
        ordered = jnp.stack(blocks)
        own = jnp.concatenate([pick(ordered, place ^ k) for k in range(members)], 0)
    return [own] + fan([own] * 3, DP, stages[0][0])


def finish_kernel(shifted, *refs):
    if shifted:
        m0, m1, m2, m3, theirs, _, out, out_proj, buf, sems = refs
        per = out_proj.shape[0] * 2 // STRIDE
    else:
        m0, m1, m2, m3, theirs, out, buf, sems = refs
    _, _, x = position()
    z = depth()
    half = STRIDE // 2
    rows = buf.shape[1]
    copies = []
    for k, mine in enumerate((m0, m1, m2, m3)):
        j = z ^ k
        for i, (value, part, xp) in enumerate(((mine, 1 - x, x), (theirs.at[k], x, 1 - x))):
            tap = part * half + j + half
            if shifted:
                tap = jnp.where(part == 0, 3 * half + j, j)
            n = 2 * k + i
            buf[n] = value[:rows].astype(F32)
            copy = pltpu.make_async_copy(
                buf.at[n],
                out.at[pl.ds(pl.multiple_of(tap * rows, rows), rows), :],
                sems.at[n],
            )
            copy.start()
            copies.append(copy)
            if shifted:
                where = pl.ds(pl.multiple_of(j * per, per), per)
                width = value.shape[1]
                extra = value[rows:].astype(F32)

                @pl.when(xp == 0)
                def _():
                    out_proj[where, :width] = extra

                @pl.when(xp == 1)
                def _():
                    out_proj[where, width:] = extra

    for copy in copies:
        copy.wait()


def body(
    features, lengths, routes, res_in_weight, res_out_weight, down_weight, proj_weight, cotangent
):
    utts = lengths.shape[0]
    total_rows = features.shape[0] // utts
    ch = features.shape[1]
    frames = total_rows // STRIDE
    hid = res_out_weight.shape[0]
    width = down_weight.shape[1]
    lat = proj_weight.shape[1]
    dp_count = lax.axis_size(DP)
    pieces = routes.shape[0]
    half_pieces = pieces // utts
    capacity = 2 * pieces // dp_count
    slots = dp_count * capacity
    cols = cotangent.shape[1]
    half = STRIDE // 2
    me_dp = lax.axis_index(DP)
    stages = stages_of(dp_count)
    staged = dp_count == 8
    lane_block = ((dp_count // 2, capacity, cols), BF)
    pair_block = ((2, capacity, cols), BF)

    def through_dp(parts):
        received = fan(parts[1:], DP, 2)
        send, keep = call(columns_kernel, [lane_block] * 2, [parts[0], *received])
        return keep, swap_bit(send, DP, 1)

    def all_to_all(value):
        return lax.all_to_all(
            value.reshape(dp_count, capacity, cols), DP, split_axis=0, concat_axis=0
        ).reshape(slots, cols)

    other_down = swap_bit(down_weight, MP, 1)
    other_proj = swap_bit(proj_weight, MP, 1)
    if staged:
        parts = call(
            parts_kernel,
            [pair_block] * 4,
            [cotangent.reshape(dp_count // 2, 2, capacity, cols)],
            scratch=[pltpu.SemaphoreType.DMA((4,))],
            where={0: pltpu.HBM},
        )
        returned = through_dp(parts)
    else:
        returned = [all_to_all(cotangent)]

    loads = 4
    a1, a2, sec, ahid, shid, placing, mask = call(
        functools.partial(forward_kernel, capacity),
        [
            ((STRIDE, frames, ch), BF),
            ((STRIDE, frames, ch), BF),
            ((STRIDE, frames, ch), BF),
            ((STRIDE, frames, hid), BF),
            ((STRIDE, frames, hid), BF),
            ((slots, pieces), BF),
            ((frames, LANES), F32),
        ],
        [lengths, features, routes.reshape(1, pieces), res_in_weight, res_out_weight],
        scratch=[
            pltpu.VMEM((ch // LANES, total_rows, LANES), F32),
            pltpu.VMEM((STRIDE, frames, 3 * hid), F32),
            pltpu.SMEM(lengths.shape, lengths.dtype),
            pltpu.VMEM((loads, total_rows // loads, ch), BF),
            pltpu.VMEM((1, pieces), routes.dtype),
            pltpu.VMEM(res_in_weight.shape, BF),
            pltpu.VMEM(res_out_weight.shape, BF),
            pltpu.SemaphoreType.DMA((loads + 4,)),
        ],
        where={i: pltpu.HBM for i in range(5)},
        flops=4 << 30,
    )
    other_a2 = swap_bit(a2, MP, 1)
    adown, sdown, lat_send, lat_keep = call(
        down_kernel,
        [
            ((frames, 2 * width), BF),
            ((frames, 2 * width), F32),
            ((half_pieces, half * lat), BF),
            ((half_pieces, half * lat), BF),
        ],
        [mask, a2, down_weight, other_down, proj_weight, other_proj],
        scratch=[pltpu.VMEM((lat // LANES, frames, LANES), F32)],
        flops=1 << 30,
    )
    lat_y = swap_bit(lat_send, MP, 2)

    g_own, g_other = call(
        pick_kernel,
        [((half_pieces, cols), BF), ((half_pieces, cols), BF)],
        [placing, *returned],
        scratch=[pltpu.VMEM((slots, cols), BF), pltpu.VMEM((pieces, cols), F32)],
    )
    g_y = swap_bit(g_own, MP, 2)
    g_far = swap_bit(g_other, MP, 3)
    g_core = swap_bit(g_other, MP, 1)

    mine, theirs = call(
        lat_mix_kernel, [((half_pieces, cols), BF)] * 2, [lat_keep, lat_y]
    )
    theirs = swap_bit(theirs, MP, 1)

    gd, swap, gproj = call(
        latent_grad_kernel,
        [
            ((frames, 2 * width), BF),
            ((frames + 2 * width, width), BF),
            ((2 * width, lat // 2), F32),
        ],
        [mask, g_own, g_core, g_y, g_far, adown, sdown, proj_weight, other_proj],
        scratch=[pltpu.VMEM((lat // LANES, frames, LANES), F32)],
        flops=1 << 30,
    )
    got = swap_bit(swap, MP, 1)
    (g_send,) = call(
        section_send_kernel,
        [((half, frames, ch), BF)],
        [gd, down_weight, other_down],
        flops=1 << 29,
    )
    g_recv = swap_bit(g_send, MP, 2)
    extra = 2 * width // STRIDE
    send_u, send_s = call(
        down_send_kernel,
        [((half, ch, width), BF), ((half, ch + extra, width), BF)],
        [a2, other_a2, gd, got, gproj],
        flops=1 << 29,
    )
    recv_u = swap_bit(send_u, DP, 1)
    recv_s = swap_bit(send_s, DP, 1)
    keep_u, keep_s = call(
        down_keep_kernel,
        [((half, ch, width), F32), ((half, ch + extra, width), F32)],
        [a2, other_a2, gd, got, gproj],
        flops=1 << 29,
    )
    (keep_g,) = call(
        section_keep_kernel,
        [((half, frames, ch), F32)],
        [gd, down_weight, other_down],
        flops=1 << 29,
    )

    row_scratch = pltpu.VMEM((pieces, cols), F32)
    if staged:
        parts = call(
            place_parts_kernel,
            [pair_block] * 4,
            [placing, mine, theirs],
            scratch=[row_scratch, pltpu.VMEM((slots, cols), BF)],
        )
        (packed,) = call(packed_kernel, [((slots, cols), BF)], [*through_dp(parts)])
    else:
        (outgoing,) = call(
            place_kernel,
            [((slots, cols), BF)],
            [placing, mine, theirs],
            scratch=[row_scratch],
        )
        packed = all_to_all(outgoing)

    blocks = 4 * (ch // hid)
    quarter = (blocks // 4 * hid, hid)
    e_own, *e_sends = call(
        residual_kernel,
        [(quarter, F32)] + [(quarter, BF)] * 3,
        [mask, keep_g, g_recv, sec, ahid, shid, res_out_weight, a1],
        scratch=[pltpu.VMEM((half, frames, hid), F32), pltpu.VMEM((blocks, hid, hid), F32)],
        flops=1 << 30,
    )
    received = fan(e_sends, MP, 1)
    e_own = plus(e_own, received)
    sent = e_own.astype(BF)
    received = [swap_bit(sent, DP, 1)]
    for bit, members in stages:
        e_own = plus(e_own, received)
        sent = e_own.astype(BF)
        received = fan([sent] * (members - 1), DP, bit)
    sent = plus(e_own, received).astype(BF)
    grad_res_in, grad_res_out = call(
        residual_finish_kernel,
        [((3 * ch, hid), F32), ((hid, ch), F32)],
        [sent, *fan([sent] * 3, MP, 1)],
        scratch=[pltpu.VMEM((4,) + quarter, F32)],
    )

    all_u = gather_rest(reduce_rest(keep_u, recv_u, me_dp, stages), me_dp, stages)
    their_u = swap_bit(jnp.stack(all_u), DP, 1)
    all_s = gather_rest(reduce_rest(keep_s, recv_s, me_dp, stages), me_dp, stages)
    their_s = swap_bit(jnp.stack(all_s), DP, 1)
    down_out = ((2 * STRIDE * ch, width), F32)
    taps = [pltpu.VMEM((STRIDE, ch, width), F32), pltpu.SemaphoreType.DMA((STRIDE,))]
    (grad_down,) = call(
        functools.partial(finish_kernel, False),
        [down_out],
        [*all_u, their_u],
        scratch=taps,
        where={5: pltpu.HBM},
    )
    grad_down, grad_proj = call(
        functools.partial(finish_kernel, True),
        [down_out, ((width, lat), F32)],
        [*all_s, their_s, grad_down],
        scratch=taps,
        where={5: pltpu.HBM, 6: pltpu.HBM},
        aliases={5: 0},
    )
    return (packed, grad_res_in, grad_res_out, grad_down, grad_proj)


def solution(mesh):
    return jax.shard_map(
        body,
        mesh=mesh,
        in_specs=(
            P(DP, None),
            P(DP),
            P(DP, None),
            P(),
            P(),
            P(None, MP),
            P(MP, None),
            P(DP, MP),
        ),
        out_specs=(P(DP, MP), P(), P(), P(None, MP), P(MP, None)),
        check_vma=False,
    )
```

```python
import functools
import jax
import jax.numpy as jnp
from jax import lax
from jax.experimental import pallas as pl
from jax.experimental.pallas import tpu as pltpu
from jax.sharding import PartitionSpec as P

STRIDE = 8
DP, MP = "dp", "mp"
LANES = 128
BF = jnp.bfloat16
F32 = jnp.float32
VMEM_LIMIT = 16 << 20


def elu(v):
    return jnp.where(v > 0, v, jnp.exp(jnp.minimum(v, 0.0)) - 1.0)


def slope(v):
    return jnp.where(v > 0, 1.0, jnp.exp(jnp.minimum(v, 0.0)))


def mm(a, b):
    return jnp.dot(a, b, preferred_element_type=F32)


def mm_nt(a, b):
    return lax.dot_general(a, b, (((1,), (1,)), ((), ())), preferred_element_type=F32)


def mm_tn(a, b):
    return lax.dot_general(a, b, (((0,), (0,)), ((), ())), preferred_element_type=F32)


def shift(v, s):
    n = v.shape[0]
    rows = lax.broadcasted_iota(jnp.int32, v.shape, 0)
    rolled = pltpu.roll(v, (-s) % n, 0)
    keep = rows < n - s if s > 0 else rows >= -s
    return jnp.where(keep, rolled, 0.0)


def spread(ref, value):
    for i in range(ref.shape[0]):
        ref[i] = value[:, i * LANES : (i + 1) * LANES]


def every(ref, start, size):
    return jnp.concatenate(
        [ref[i, pl.ds(start, size, stride=STRIDE), :] for i in range(ref.shape[0])], 1
    )


def call(kernel, outs, ins, scratch=(), flops=0, where=None, aliases=None):
    whole = pl.BlockSpec(memory_space=pltpu.VMEM)
    spaces = {i: pl.BlockSpec(memory_space=space) for i, space in (where or {}).items()}
    ins = [
        pltpu.with_memory_space_constraint(a, pltpu.HBM) if i in spaces else a
        for i, a in enumerate(ins)
    ]
    return pl.pallas_call(
        kernel,
        out_shape=[jax.ShapeDtypeStruct(s, d) for s, d in outs],
        in_specs=[spaces.get(i, whole) for i in range(len(ins))],
        out_specs=[spaces.get(len(ins) + i, whole) for i in range(len(outs))],
        scratch_shapes=list(scratch),
        input_output_aliases=aliases or {},
        compiler_params=pltpu.CompilerParams(vmem_limit_bytes=VMEM_LIMIT),
        cost_estimate=pl.CostEstimate(
            flops=flops, transcendentals=0, bytes_accessed=1 << 20
        ),
    )(*ins)


def position():
    m = lax.axis_index(MP)
    return lax.rem(m, 2), m // 2, lax.rem(lax.axis_index(DP), 2)


def masked(value, mask):
    wide = jnp.concatenate([mask[...]] * (value.shape[1] // mask.shape[1]), 1)
    return jnp.where(wide > 0, value, 0.0)


def depth():
    return lax.rem(lax.axis_index(DP) // 2, 4)


def forward_kernel(
    capacity, lengths_hbm, feat_hbm, routes_hbm, wi_hbm, wo_hbm,
    a1, a2, sec, ahid, shid, placing, mask, xs, ys, lengths, feat, routes, wi, wo, sems,
):
    frames, ch = a1.shape[1], a1.shape[2]
    hid = wo.shape[0]
    c, _, _ = position()
    rows = frames * STRIDE
    parts = feat.shape[0]
    size = rows // parts
    copies = [
        pltpu.make_async_copy(
            feat_hbm.at[pl.ds(pl.multiple_of(c * rows + i * size, size), size), :],
            feat.at[i],
            sems.at[i],
        )
        for i in range(parts)
    ]
    rest = [
        pltpu.make_async_copy(src, dst, sems.at[parts + i])
        for i, (src, dst) in enumerate(((routes_hbm, routes), (wi_hbm, wi), (wo_hbm, wo)))
    ]
    table = pltpu.make_async_copy(lengths_hbm, lengths, sems.at[parts + len(rest)])
    table.start()
    for copy in copies + rest:
        copy.start()
    table.wait()
    length = lengths[c]
    live = lax.broadcasted_iota(jnp.int32, (frames, ch), 0) < length
    mask[...] = jnp.where(live[:, : mask.shape[1]], 1.0, 0.0)
    for i in range(parts):
        copies[i].wait()
        value = feat[i].astype(F32)
        for k in range(xs.shape[0]):
            xs[k, i * size : (i + 1) * size] = value[:, k * LANES : (k + 1) * LANES]
    for copy in rest:
        copy.wait()
    placing[...] = placing_of(routes[...], placing.shape[0], capacity)
    wcat = jnp.concatenate([wi[k * ch : (k + 1) * ch, :] for k in range(3)], 1)

    def signal(p):
        return jnp.where(live, every(xs, p, frames), 0.0)

    for p in range(STRIDE):
        act = elu(signal(p)).astype(BF)
        a1[p] = act
        ys[p] = mm(act, wcat)
    for p in range(STRIDE):
        left = shift(ys[(p - 1) % STRIDE, :, :hid], -1 if p > 0 else -2)
        right = shift(ys[(p + 1) % STRIDE, :, 2 * hid :], 1 if p < STRIDE - 1 else 2)
        hidden = left + ys[p, :, hid : 2 * hid] + right
        act_hid = elu(hidden).astype(BF)
        ahid[p] = act_hid
        shid[p] = slope(hidden).astype(BF)
        section = jnp.where(live, signal(p) + mm(act_hid, wo[...]), 0.0).astype(BF)
        sec[p] = section
        a2[p] = elu(section.astype(F32)).astype(BF)


def down_kernel(
    mask, a2, dwa, dwb, pa, pb, adown, sdown, lat_send, lat_keep, ls,
):
    frames, ch = a2.shape[1], a2.shape[2]
    _, y, _ = position()
    half = STRIDE // 2

    def tap(k):
        return jnp.concatenate([dwa[k * ch : (k + 1) * ch, :], dwb[k * ch : (k + 1) * ch, :]], 1)

    down = jnp.zeros((frames, 2 * dwa.shape[1]), F32)
    before = jnp.zeros_like(down)
    after = jnp.zeros_like(down)
    for p in range(STRIDE):
        act = a2[p]
        down = down + mm(act, tap(p + half))
        if p < half:
            after = after + mm(act, tap(p + 3 * half))
        else:
            before = before + mm(act, tap(p - half))
    down = down + shift(before, -1) + shift(after, 1)
    act_down = elu(down).astype(BF)
    adown[...] = act_down
    sdown[...] = slope(down)
    proj = jnp.concatenate([pa[...], pb[...]], 0)
    lat = proj.shape[1]
    spread(ls, masked(mm(act_down, proj), mask))
    pieces = frames // STRIDE
    for j in range(half):
        cols = slice(j * lat, (j + 1) * lat)
        lat_send[:, cols] = every(ls, half * (1 - y) + j, pieces).astype(BF)
        lat_keep[:, cols] = every(ls, half * y + j, pieces).astype(BF)


def placing_of(targets, slots, capacity):
    pieces = targets.shape[1]
    chosen = jnp.where(targets == lax.broadcasted_iota(jnp.int32, (128, pieces), 0), 1.0, 0.0)
    upper = (
        lax.broadcasted_iota(jnp.int32, (pieces, pieces), 0)
        < lax.broadcasted_iota(jnp.int32, (pieces, pieces), 1)
    )
    earlier = mm(chosen.astype(BF), jnp.where(upper, 1.0, 0.0).astype(BF))
    rank = jnp.sum(earlier * chosen, axis=0, keepdims=True).astype(jnp.int32)
    slot = targets * capacity + rank
    ids = lax.broadcasted_iota(jnp.int32, (slots, pieces), 0)
    return jnp.where(slot == ids, 1.0, 0.0).astype(BF)


def parts_kernel(whole, *refs):
    *outs, sems = refs
    z = depth()
    copies = [
        pltpu.make_async_copy(whole.at[z ^ k], out, sems.at[k]) for k, out in enumerate(outs)
    ]
    for copy in copies:
        copy.start()
    for copy in copies:
        copy.wait()


def columns_kernel(*refs):
    *parts, send, keep = refs
    _, _, x = position()
    for k, part in enumerate(parts):
        send[k] = part[1 - x]
        keep[k] = part[x]


def assemble(keep, recv, out):
    _, _, x = position()
    z = depth()
    size = keep.shape[1]
    for k in range(keep.shape[0]):
        for part, column in ((keep, x), (recv, 1 - x)):
            at = (2 * (z ^ k) + column) * size
            out[pl.ds(pl.multiple_of(at, size), size), :] = part[k]


def pick_kernel(placing, *refs):
    *parts, own, other, rows, buf = refs
    c, _, _ = position()
    if len(parts) == 1:
        rows[...] = parts[0][...]
    else:
        assemble(*parts, rows)
    buf[...] = mm_tn(placing[...], rows[...])
    half = own.shape[0]
    own[...] = buf[pl.ds(pl.multiple_of(c * half, half), half), :].astype(BF)
    other[...] = buf[pl.ds(pl.multiple_of((1 - c) * half, half), half), :].astype(BF)


def place_kernel(placing, mine, theirs, outgoing, buf):
    c, _, _ = position()
    half = mine.shape[0]
    buf[pl.ds(pl.multiple_of(c * half, half), half), :] = mine[...].astype(F32)
    buf[pl.ds(pl.multiple_of((1 - c) * half, half), half), :] = theirs[...].astype(F32)
    outgoing[...] = mm(placing[...], buf[...].astype(BF)).astype(BF)


def place_parts_kernel(placing, mine, theirs, *refs):
    *outs, buf, rows = refs
    place_kernel(placing, mine, theirs, rows, buf)
    z = depth()
    _, columns, size, _ = (1,) + outs[0].shape
    for k, out in enumerate(outs):
        for i in range(columns):
            at = ((z ^ k) * columns + i) * size
            out[i] = rows[pl.ds(pl.multiple_of(at, size), size), :]


def packed_kernel(keep, recv, out):
    assemble(keep, recv, out)


def lat_mix_kernel(lat_keep, lat_y, mine, theirs):
    c, _, _ = position()
    total = (lat_keep[...].astype(F32) + lat_y[...].astype(F32)).astype(BF)
    cols = mine.shape[1]
    mine[...] = jnp.where(c == 0, total[:, :cols], total[:, cols:])
    theirs[...] = jnp.where(c == 0, total[:, cols:], total[:, :cols])


def section_grad(gd, gshift, wa, wb, part, j, ch):
    half = STRIDE // 2
    first = part * half + j + half
    second = jnp.where(part == 0, 3 * half + j, j)
    rows1 = pl.ds(pl.multiple_of(first * ch, ch), ch)
    rows2 = pl.ds(pl.multiple_of(second * ch, ch), ch)
    w1 = jnp.concatenate([wa[rows1, :], wb[rows1, :]], 1)
    w2 = jnp.concatenate([wa[rows2, :], wb[rows2, :]], 1)
    return mm_nt(gd, w1) + mm_nt(gshift, w2)


def moved(gd, part):
    g = gd.astype(F32)
    return jnp.where(part == 0, shift(g, -1), shift(g, 1)).astype(BF)


def latent_grad_kernel(
    mask, g_own, g_core, g_y, g_far, adown, sdown, pa, pb,
    gd_out, swap, gproj_keep, gl,
):
    frames = adown.shape[0]
    width, lat = pa.shape
    pieces = g_own.shape[0]
    c, y, _ = position()
    blocks = (
        (g_own, 2 * y + c),
        (g_core, 2 * y + 1 - c),
        (g_y, 2 * (1 - y) + c),
        (g_far, 2 * (1 - y) + 1 - c),
    )
    for block, owner in blocks:
        for j in range(2):
            for i in range(gl.shape[0]):
                at = j * lat + i * LANES
                gl[i, pl.ds(2 * owner + j, pieces, stride=STRIDE), :] = block[
                    :, at : at + LANES
                ].astype(F32)
    g_latent = masked(jnp.concatenate([gl[i] for i in range(gl.shape[0])], 1), mask).astype(BF)
    proj = jnp.concatenate([pa[...], pb[...]], 0)
    gd = (mm_nt(g_latent, proj) * sdown[...]).astype(BF)
    gd_out[...] = gd
    swap[:frames] = gd[:, width:]
    gproj = mm_tn(adown[...], g_latent)
    swap[frames : frames + width] = gproj[width:, :width].astype(BF)
    swap[frames + width :] = gproj[width:, width:].astype(BF)
    gproj_keep[:width] = gproj[:width, :width]
    gproj_keep[width:] = gproj[:width, width:]


def section_send_kernel(gd, dwa, dwb, send):
    _, y, _ = position()
    full = gd[...]
    g2 = moved(full, 1 - y)
    for j in range(STRIDE // 2):
        send[j] = section_grad(full, g2, dwa, dwb, 1 - y, j, send.shape[2]).astype(BF)


def section_keep_kernel(gd, dwa, dwb, keep):
    _, y, _ = position()
    full = gd[...]
    g2 = moved(full, y)
    for j in range(STRIDE // 2):
        keep[j] = section_grad(full, g2, dwa, dwb, y, j, keep.shape[2])


def weight_grads(a2a, a2b, ga, gb, part, j):
    half = STRIDE // 2
    p = part * half + j
    return mm_tn(a2a[p], ga) + mm_tn(a2b[p], gb)


def pair(g, part):
    return jnp.concatenate([g, moved(g, part)], 1)


def down_send_kernel(a2a, a2b, gd, swap, gproj, send_u, send_s):
    frames = gd.shape[0]
    width = swap.shape[1]
    _, _, x = position()
    ga = pair(gd[:, :width], x)
    gb = pair(swap[:frames], x)
    extra = send_s.shape[1] - send_u.shape[1]
    rows = send_u.shape[1]
    for j in range(STRIDE // 2):
        w = weight_grads(a2a, a2b, ga, gb, x, j)
        send_u[j] = w[:, :width].astype(BF)
        send_s[j, :rows] = w[:, width:].astype(BF)
        at = pl.ds(pl.multiple_of(((1 - x) * 4 + j) * extra, extra), extra)
        send_s[j, rows:] = (gproj[at, :] + swap[pl.ds(pl.multiple_of(frames + ((1 - x) * 4 + j) * extra, extra), extra), :].astype(F32)).astype(BF)


def down_keep_kernel(a2a, a2b, gd, swap, gproj, keep_u, keep_s):
    frames = gd.shape[0]
    width = swap.shape[1]
    _, _, x = position()
    part = 1 - x
    ga = pair(gd[:, :width], part)
    gb = pair(swap[:frames], part)
    extra = keep_s.shape[1] - keep_u.shape[1]
    rows = keep_u.shape[1]
    for j in range(STRIDE // 2):
        w = weight_grads(a2a, a2b, ga, gb, part, j)
        keep_u[j] = w[:, :width]
        keep_s[j, :rows] = w[:, width:]
        at = pl.ds(pl.multiple_of((x * 4 + j) * extra, extra), extra)
        keep_s[j, rows:] = gproj[at, :] + swap[pl.ds(pl.multiple_of(frames + (x * 4 + j) * extra, extra), extra), :].astype(F32)


def residual_kernel(
    mask, keep, recv, sec, ahid, shid, wo, a1, kept, send1, send2, send3, gh, buf,
):
    half = STRIDE // 2
    ch = keep.shape[2]
    hid = wo.shape[0]
    c, y, _ = position()
    g_out = jnp.zeros((hid, ch), F32)
    for j in range(half):
        g = keep[j] + recv[j].astype(F32)
        g_branch = masked(g * slope(sec[y * half + j].astype(F32)), mask).astype(BF)
        g_out = g_out + mm_tn(ahid[y * half + j], g_branch)
        gh[j] = mm_nt(g_branch, wo[...]) * shid[y * half + j].astype(F32)
    taps = [jnp.zeros((ch, hid), F32) for _ in range(3)]
    for j in range(half):
        g = gh[j]
        p = y * half + j
        here = g.astype(BF)
        taps[1] = taps[1] + mm_tn(a1[p], here)
        down1 = shift(g, 1)
        up1 = shift(g, -1)
        if j == 0:
            down1 = jnp.where(y == 0, shift(g, 2), down1)
        if j == half - 1:
            up1 = jnp.where(y == 1, shift(g, -2), up1)
        taps[0] = taps[0] + mm_tn(a1[lax.rem(p + STRIDE - 1, STRIDE)], down1.astype(BF))
        taps[2] = taps[2] + mm_tn(a1[lax.rem(p + 1, STRIDE)], up1.astype(BF))
    for k in range(3):
        for i in range(ch // hid):
            buf[k * (ch // hid) + i] = taps[k][i * hid : (i + 1) * hid]
    for i in range(ch // hid):
        buf[3 * (ch // hid) + i] = g_out[:, i * hid : (i + 1) * hid]
    m = 2 * y + c
    n = buf.shape[0] // 4
    for i in range(n):
        at = slice(i * hid, (i + 1) * hid)
        kept[at] = buf[m * n + i]
        for k, out in enumerate((send1, send2, send3)):
            out[at] = buf[(m ^ (k + 1)) * n + i].astype(BF)


def residual_finish_kernel(r0, r1, r2, r3, out_in, out_out, buf):
    c, y, _ = position()
    m = 2 * y + c
    rows, hid = r0.shape
    for k, r in enumerate((r0, r1, r2, r3)):
        buf[m ^ k] = r[...].astype(F32)
    for q in range(3):
        out_in[q * rows : (q + 1) * rows] = buf[q]
    for i in range(rows // hid):
        out_out[:, i * hid : (i + 1) * hid] = buf[3, i * hid : (i + 1) * hid]


def sum_kernel(keep, recv, own, *sends):
    z = depth()
    own[...] = keep[z] + recv[z].astype(F32)
    for k, out in enumerate(sends):
        at = z ^ (k + 1)
        out[...] = (keep[at] + recv[at].astype(F32)).astype(BF)


def swap_bit(value, axis, bit):
    n = lax.axis_size(axis)
    return lax.ppermute(value, axis, [(i, i ^ bit) for i in range(n)])


def stages_of(n):
    found, bit = [], 2
    while bit < n:
        members = 4 if n // bit >= 4 else 2
        found.append((bit, members))
        bit *= members
    return found


def pick(stack, index):
    return lax.dynamic_index_in_dim(stack, index, 0, keepdims=False)


def fan(values, axis, bit):
    return [swap_bit(v, axis, bit * (k + 1)) for k, v in enumerate(values)]


def plus(total, received):
    for r in received:
        total = total + r.astype(F32)
    return total


def reduce_rest(kept, received, me, stages):
    shape = kept.shape[1:]
    own, *sends = call(sum_kernel, [(shape, F32)] + [(shape, BF)] * 3, [kept, received])
    received = fan(sends, DP, stages[0][0])
    for bit, members in stages[1:]:
        parts = plus(own, received).reshape(members, -1, own.shape[-1])
        place = (me // bit) % members
        sends = [pick(parts, place ^ k).astype(BF) for k in range(1, members)]
        own, received = pick(parts, place), fan(sends, DP, bit)
    return plus(own, received).astype(BF)


def gather_high(own, me, stages):
    for bit, members in reversed(stages[1:]):
        place = (me // bit) % members
        blocks = [own] + fan([own] * (members - 1), DP, bit)
        ordered = jnp.stack(blocks)
        own = jnp.concatenate([pick(ordered, place ^ k) for k in range(members)], 0)
    return own


def finish_kernel(shifted, count, written, projected, *refs):
    ins, rest = refs[:count], refs[count:]
    if projected:
        *_, out, out_proj, buf, sems = rest
    else:
        *_, out, buf, sems = rest
    _, _, x = position()
    z = depth()
    half = STRIDE // 2
    rows = buf.shape[1]

    def block(entry):
        operand, lead, k, own = entry
        ref = ins[operand]
        value = ref if lead is None else ref.at[lead]
        part, xp = (1 - x, x) if own else (x, 1 - x)
        return value, z ^ k, part, xp

    copies = []
    for n, entry in enumerate(written):
        value, j, part, _ = block(entry)
        tap = part * half + j + half
        if shifted:
            tap = jnp.where(part == 0, 3 * half + j, j)
        buf[n] = value[:rows].astype(F32)
        copy = pltpu.make_async_copy(
            buf.at[n], out.at[pl.ds(pl.multiple_of(tap * rows, rows), rows), :], sems.at[n]
        )
        copy.start()
        copies.append(copy)
    for entry in projected:
        value, j, _, xp = block(entry)
        per = out_proj.shape[0] * 2 // STRIDE
        where = pl.ds(pl.multiple_of(j * per, per), per)
        width = value.shape[1]
        extra = value[rows : rows + per].astype(F32)

        @pl.when(xp == 0)
        def _():
            out_proj[where, :width] = extra

        @pl.when(xp == 1)
        def _():
            out_proj[where, width:] = extra

    for copy in copies:
        copy.wait()


def body(
    features, lengths, routes, res_in_weight, res_out_weight, down_weight, proj_weight, cotangent
):
    utts = lengths.shape[0]
    total_rows = features.shape[0] // utts
    ch = features.shape[1]
    frames = total_rows // STRIDE
    hid = res_out_weight.shape[0]
    width = down_weight.shape[1]
    lat = proj_weight.shape[1]
    dp_count = lax.axis_size(DP)
    pieces = routes.shape[0]
    half_pieces = pieces // utts
    capacity = 2 * pieces // dp_count
    slots = dp_count * capacity
    cols = cotangent.shape[1]
    half = STRIDE // 2
    me_dp = lax.axis_index(DP)
    stages = stages_of(dp_count)
    staged = dp_count == 8
    lane_block = ((dp_count // 2, capacity, cols), BF)
    pair_block = ((2, capacity, cols), BF)

    def through_dp(parts):
        received = fan(parts[1:], DP, 2)
        send, keep = call(columns_kernel, [lane_block] * 2, [parts[0], *received])
        return keep, swap_bit(send, DP, 1)

    def all_to_all(value):
        return lax.all_to_all(
            value.reshape(dp_count, capacity, cols), DP, split_axis=0, concat_axis=0
        ).reshape(slots, cols)

    other_down = swap_bit(down_weight, MP, 1)
    other_proj = swap_bit(proj_weight, MP, 1)
    if staged:
        parts = call(
            parts_kernel,
            [pair_block] * 4,
            [cotangent.reshape(dp_count // 2, 2, capacity, cols)],
            scratch=[pltpu.SemaphoreType.DMA((4,))],
            where={0: pltpu.HBM},
        )
        returned = through_dp(parts)
    else:
        returned = [all_to_all(cotangent)]

    loads = 4
    a1, a2, sec, ahid, shid, placing, mask = call(
        functools.partial(forward_kernel, capacity),
        [
            ((STRIDE, frames, ch), BF),
            ((STRIDE, frames, ch), BF),
            ((STRIDE, frames, ch), BF),
            ((STRIDE, frames, hid), BF),
            ((STRIDE, frames, hid), BF),
            ((slots, pieces), BF),
            ((frames, LANES), F32),
        ],
        [lengths, features, routes.reshape(1, pieces), res_in_weight, res_out_weight],
        scratch=[
            pltpu.VMEM((ch // LANES, total_rows, LANES), F32),
            pltpu.VMEM((STRIDE, frames, 3 * hid), F32),
            pltpu.SMEM(lengths.shape, lengths.dtype),
            pltpu.VMEM((loads, total_rows // loads, ch), BF),
            pltpu.VMEM((1, pieces), routes.dtype),
            pltpu.VMEM(res_in_weight.shape, BF),
            pltpu.VMEM(res_out_weight.shape, BF),
            pltpu.SemaphoreType.DMA((loads + 4,)),
        ],
        where={i: pltpu.HBM for i in range(5)},
        flops=4 << 30,
    )
    other_a2 = swap_bit(a2, MP, 1)
    adown, sdown, lat_send, lat_keep = call(
        down_kernel,
        [
            ((frames, 2 * width), BF),
            ((frames, 2 * width), F32),
            ((half_pieces, half * lat), BF),
            ((half_pieces, half * lat), BF),
        ],
        [mask, a2, down_weight, other_down, proj_weight, other_proj],
        scratch=[pltpu.VMEM((lat // LANES, frames, LANES), F32)],
        flops=1 << 30,
    )
    lat_y = swap_bit(lat_send, MP, 2)

    g_own, g_other = call(
        pick_kernel,
        [((half_pieces, cols), BF), ((half_pieces, cols), BF)],
        [placing, *returned],
        scratch=[pltpu.VMEM((slots, cols), BF), pltpu.VMEM((pieces, cols), F32)],
    )
    g_y = swap_bit(g_own, MP, 2)
    g_far = swap_bit(g_other, MP, 3)
    g_core = swap_bit(g_other, MP, 1)

    mine, theirs = call(
        lat_mix_kernel, [((half_pieces, cols), BF)] * 2, [lat_keep, lat_y]
    )
    theirs = swap_bit(theirs, MP, 1)

    gd, swap, gproj = call(
        latent_grad_kernel,
        [
            ((frames, 2 * width), BF),
            ((frames + 2 * width, width), BF),
            ((2 * width, lat // 2), F32),
        ],
        [mask, g_own, g_core, g_y, g_far, adown, sdown, proj_weight, other_proj],
        scratch=[pltpu.VMEM((lat // LANES, frames, LANES), F32)],
        flops=1 << 30,
    )
    got = swap_bit(swap, MP, 1)
    (g_send,) = call(
        section_send_kernel,
        [((half, frames, ch), BF)],
        [gd, down_weight, other_down],
        flops=1 << 29,
    )
    g_recv = swap_bit(g_send, MP, 2)
    extra = 2 * width // STRIDE
    send_u, send_s = call(
        down_send_kernel,
        [((half, ch, width), BF), ((half, ch + extra, width), BF)],
        [a2, other_a2, gd, got, gproj],
        flops=1 << 29,
    )
    recv_u = swap_bit(send_u, DP, 1)
    recv_s = swap_bit(send_s, DP, 1)
    keep_u, keep_s = call(
        down_keep_kernel,
        [((half, ch, width), F32), ((half, ch + extra, width), F32)],
        [a2, other_a2, gd, got, gproj],
        flops=1 << 29,
    )
    (keep_g,) = call(
        section_keep_kernel,
        [((half, frames, ch), F32)],
        [gd, down_weight, other_down],
        flops=1 << 29,
    )

    row_scratch = pltpu.VMEM((pieces, cols), F32)
    if staged:
        parts = call(
            place_parts_kernel,
            [pair_block] * 4,
            [placing, mine, theirs],
            scratch=[row_scratch, pltpu.VMEM((slots, cols), BF)],
        )
        (packed,) = call(packed_kernel, [((slots, cols), BF)], [*through_dp(parts)])
    else:
        (outgoing,) = call(
            place_kernel,
            [((slots, cols), BF)],
            [placing, mine, theirs],
            scratch=[row_scratch],
        )
        packed = all_to_all(outgoing)

    blocks = 4 * (ch // hid)
    quarter = (blocks // 4 * hid, hid)
    e_own, *e_sends = call(
        residual_kernel,
        [(quarter, F32)] + [(quarter, BF)] * 3,
        [mask, keep_g, g_recv, sec, ahid, shid, res_out_weight, a1],
        scratch=[pltpu.VMEM((half, frames, hid), F32), pltpu.VMEM((blocks, hid, hid), F32)],
        flops=1 << 30,
    )
    received = fan(e_sends, MP, 1)
    e_own = plus(e_own, received)
    sent = e_own.astype(BF)

    own_u = gather_high(reduce_rest(keep_u, recv_u, me_dp, stages), me_dp, stages)
    own_s = gather_high(reduce_rest(keep_s, recv_s, me_dp, stages), me_dp, stages)
    all_u = [own_u] + fan([own_u] * 3, DP, stages[0][0])
    both = jnp.concatenate([own_s, sent])
    first_s = swap_bit(both, DP, 1)
    all_s = [own_s] + fan([own_s] * 3, DP, stages[0][0])
    their_u = swap_bit(jnp.stack(all_u), DP, 1)
    their_s = swap_bit(jnp.stack(all_s[1:]), DP, 1)
    received = [first_s[own_s.shape[0] :]]
    for bit, members in stages:
        e_own = plus(e_own, received)
        sent = e_own.astype(BF)
        received = fan([sent] * (members - 1), DP, bit)
    sent = plus(e_own, received).astype(BF)
    grad_res_in, grad_res_out = call(
        residual_finish_kernel,
        [((3 * ch, hid), F32), ((hid, ch), F32)],
        [sent, *fan([sent] * 3, MP, 1)],
        scratch=[pltpu.VMEM((4,) + quarter, F32)],
    )

    down_out = ((2 * STRIDE * ch, width), F32)
    mine = tuple((k, None, k, True) for k in range(4))

    def finish(shifted, ins, written, projected, before=None):
        n = len(ins)
        aliased = before is not None
        return call(
            functools.partial(finish_kernel, shifted, n, written, projected),
            [down_out] + [((width, lat), F32)] * bool(projected),
            [*ins] + [before] * aliased,
            scratch=[
                pltpu.VMEM((len(written), ch, width), F32),
                pltpu.SemaphoreType.DMA((len(written),)),
            ],
            where={n: pltpu.HBM, n + aliased: pltpu.HBM},
            aliases={n: 0} if aliased else None,
        )

    (grad_down,) = finish(
        False, [*all_u, their_u], mine + tuple((4, k, k, False) for k in range(4)), ()
    )
    crossed = ((4, None, 0, False),)
    (grad_down,) = finish(True, [*all_s, first_s], mine + crossed, (), grad_down)
    last = tuple((5, k - 1, k, False) for k in range(1, 4))
    grad_down, grad_proj = finish(
        True, [*all_s, first_s, their_s], last, mine + crossed + last, grad_down
    )
    return (packed, grad_res_in, grad_res_out, grad_down, grad_proj)


def solution(mesh):
    return jax.shard_map(
        body,
        mesh=mesh,
        in_specs=(
            P(DP, None),
            P(DP),
            P(DP, None),
            P(),
            P(),
            P(None, MP),
            P(MP, None),
            P(DP, MP),
        ),
        out_specs=(P(DP, MP), P(), P(), P(None, MP), P(MP, None)),
        check_vma=False,
    )
```

```python
import functools
import jax
import jax.numpy as jnp
from jax import lax
from jax.experimental import pallas as pl
from jax.experimental.pallas import tpu as pltpu
from jax.sharding import PartitionSpec as P

STRIDE = 8
DP, MP = "dp", "mp"
LANES = 128
BF = jnp.bfloat16
F32 = jnp.float32
VMEM_LIMIT = 16 << 20


def elu(v):
    return jnp.where(v > 0, v, jnp.exp(jnp.minimum(v, 0.0)) - 1.0)


def slope(v):
    return jnp.where(v > 0, 1.0, jnp.exp(jnp.minimum(v, 0.0)))


def mm(a, b):
    return jnp.dot(a, b, preferred_element_type=F32)


def mm_nt(a, b):
    return lax.dot_general(a, b, (((1,), (1,)), ((), ())), preferred_element_type=F32)


def mm_tn(a, b):
    return lax.dot_general(a, b, (((0,), (0,)), ((), ())), preferred_element_type=F32)


def shift(v, s):
    n = v.shape[0]
    rows = lax.broadcasted_iota(jnp.int32, v.shape, 0)
    rolled = pltpu.roll(v, (-s) % n, 0)
    keep = rows < n - s if s > 0 else rows >= -s
    return jnp.where(keep, rolled, 0.0)


def spread(ref, value):
    for i in range(ref.shape[0]):
        ref[i] = value[:, i * LANES : (i + 1) * LANES]


def every(ref, start, size):
    return jnp.concatenate(
        [ref[i, pl.ds(start, size, stride=STRIDE), :] for i in range(ref.shape[0])], 1
    )


def call(kernel, outs, ins, scratch=(), flops=0, where=None, aliases=None):
    whole = pl.BlockSpec(memory_space=pltpu.VMEM)
    spaces = {i: pl.BlockSpec(memory_space=space) for i, space in (where or {}).items()}
    ins = [
        pltpu.with_memory_space_constraint(a, pltpu.HBM) if i in spaces else a
        for i, a in enumerate(ins)
    ]
    return pl.pallas_call(
        kernel,
        out_shape=[jax.ShapeDtypeStruct(s, d) for s, d in outs],
        in_specs=[spaces.get(i, whole) for i in range(len(ins))],
        out_specs=[spaces.get(len(ins) + i, whole) for i in range(len(outs))],
        scratch_shapes=list(scratch),
        input_output_aliases=aliases or {},
        compiler_params=pltpu.CompilerParams(vmem_limit_bytes=VMEM_LIMIT),
        cost_estimate=pl.CostEstimate(
            flops=flops, transcendentals=0, bytes_accessed=1 << 20
        ),
    )(*ins)


def position():
    m = lax.axis_index(MP)
    return lax.rem(m, 2), m // 2, lax.rem(lax.axis_index(DP), 2)


def masked(value, mask):
    wide = jnp.concatenate([mask[...]] * (value.shape[1] // mask.shape[1]), 1)
    return jnp.where(wide > 0, value, 0.0)


def depth():
    return lax.rem(lax.axis_index(DP) // 2, 4)


def forward_kernel(
    capacity, lengths_hbm, feat_hbm, routes_hbm, wi_hbm, wo_hbm,
    a1, sig, ys, wo_out, placing, mask, xs, lengths, feat, routes, wi, sems,
):
    frames, ch = a1.shape[1], a1.shape[2]
    c, _, _ = position()
    rows = frames * STRIDE
    parts = feat.shape[0]
    size = rows // parts
    copies = [
        pltpu.make_async_copy(
            feat_hbm.at[pl.ds(pl.multiple_of(c * rows + i * size, size), size), :],
            feat.at[i],
            sems.at[i],
        )
        for i in range(parts)
    ]
    rest = [
        pltpu.make_async_copy(src, dst, sems.at[parts + i])
        for i, (src, dst) in enumerate(((routes_hbm, routes), (wi_hbm, wi), (wo_hbm, wo_out)))
    ]
    table = pltpu.make_async_copy(lengths_hbm, lengths, sems.at[parts + len(rest)])
    table.start()
    for copy in copies + rest:
        copy.start()
    table.wait()
    length = lengths[c]
    live = lax.broadcasted_iota(jnp.int32, (frames, ch), 0) < length
    mask[...] = jnp.where(live[:, : mask.shape[1]], 1.0, 0.0)
    for i in range(parts):
        copies[i].wait()
        value = feat[i].astype(F32)
        for k in range(xs.shape[0]):
            xs[k, i * size : (i + 1) * size] = value[:, k * LANES : (k + 1) * LANES]
    for copy in rest:
        copy.wait()
    placing[...] = placing_of(routes[...], placing.shape[0], capacity)
    wcat = jnp.concatenate([wi[k * ch : (k + 1) * ch, :] for k in range(3)], 1)

    for p in range(STRIDE):
        signal = jnp.where(live, every(xs, p, frames), 0.0)
        sig[p] = signal.astype(BF)
        act = elu(signal).astype(BF)
        a1[p] = act
        ys[p] = mm(act, wcat)


def section_kernel(sig, ys, wo, mask, a2, sec, ahid, shid):
    hid = wo.shape[0]
    for p in range(STRIDE):
        left = shift(ys[(p - 1) % STRIDE, :, :hid], -1 if p > 0 else -2)
        right = shift(ys[(p + 1) % STRIDE, :, 2 * hid :], 1 if p < STRIDE - 1 else 2)
        hidden = left + ys[p, :, hid : 2 * hid] + right
        act_hid = elu(hidden).astype(BF)
        ahid[p] = act_hid
        shid[p] = slope(hidden).astype(BF)
        section = masked(sig[p].astype(F32) + mm(act_hid, wo[...]), mask).astype(BF)
        sec[p] = section
        a2[p] = elu(section.astype(F32)).astype(BF)


def down_kernel(
    mask, a2, dwa, dwb, pa, pb, adown, sdown, lat_send, lat_keep, ls,
):
    frames, ch = a2.shape[1], a2.shape[2]
    _, y, _ = position()
    half = STRIDE // 2

    def tap(k):
        return jnp.concatenate([dwa[k * ch : (k + 1) * ch, :], dwb[k * ch : (k + 1) * ch, :]], 1)

    down = jnp.zeros((frames, 2 * dwa.shape[1]), F32)
    before = jnp.zeros_like(down)
    after = jnp.zeros_like(down)
    for p in range(STRIDE):
        act = a2[p]
        down = down + mm(act, tap(p + half))
        if p < half:
            after = after + mm(act, tap(p + 3 * half))
        else:
            before = before + mm(act, tap(p - half))
    down = down + shift(before, -1) + shift(after, 1)
    act_down = elu(down).astype(BF)
    adown[...] = act_down
    sdown[...] = slope(down)
    proj = jnp.concatenate([pa[...], pb[...]], 0)
    lat = proj.shape[1]
    spread(ls, masked(mm(act_down, proj), mask))
    pieces = frames // STRIDE
    for j in range(half):
        cols = slice(j * lat, (j + 1) * lat)
        lat_send[:, cols] = every(ls, half * (1 - y) + j, pieces).astype(BF)
        lat_keep[:, cols] = every(ls, half * y + j, pieces).astype(BF)


def placing_of(targets, slots, capacity):
    pieces = targets.shape[1]
    chosen = jnp.where(targets == lax.broadcasted_iota(jnp.int32, (128, pieces), 0), 1.0, 0.0)
    upper = (
        lax.broadcasted_iota(jnp.int32, (pieces, pieces), 0)
        < lax.broadcasted_iota(jnp.int32, (pieces, pieces), 1)
    )
    earlier = mm(chosen.astype(BF), jnp.where(upper, 1.0, 0.0).astype(BF))
    rank = jnp.sum(earlier * chosen, axis=0, keepdims=True).astype(jnp.int32)
    slot = targets * capacity + rank
    ids = lax.broadcasted_iota(jnp.int32, (slots, pieces), 0)
    return jnp.where(slot == ids, 1.0, 0.0).astype(BF)


def parts_kernel(whole, *refs):
    *outs, sems = refs
    z = depth()
    copies = [
        pltpu.make_async_copy(whole.at[z ^ k], out, sems.at[k]) for k, out in enumerate(outs)
    ]
    for copy in copies:
        copy.start()
    for copy in copies:
        copy.wait()


def columns_kernel(*refs):
    *parts, send, keep = refs
    _, _, x = position()
    for k, part in enumerate(parts):
        send[k] = part[1 - x]
        keep[k] = part[x]


def assemble(keep, recv, out):
    _, _, x = position()
    z = depth()
    size = keep.shape[1]
    for k in range(keep.shape[0]):
        for part, column in ((keep, x), (recv, 1 - x)):
            at = (2 * (z ^ k) + column) * size
            out[pl.ds(pl.multiple_of(at, size), size), :] = part[k]


def pick_kernel(placing, *refs):
    *parts, own, other, rows, buf = refs
    c, _, _ = position()
    if len(parts) == 1:
        rows[...] = parts[0][...]
    else:
        assemble(*parts, rows)
    buf[...] = mm_tn(placing[...], rows[...])
    half = own.shape[0]
    own[...] = buf[pl.ds(pl.multiple_of(c * half, half), half), :].astype(BF)
    other[...] = buf[pl.ds(pl.multiple_of((1 - c) * half, half), half), :].astype(BF)


def place_kernel(placing, mine, theirs, outgoing, buf):
    c, _, _ = position()
    half = mine.shape[0]
    buf[pl.ds(pl.multiple_of(c * half, half), half), :] = mine[...].astype(F32)
    buf[pl.ds(pl.multiple_of((1 - c) * half, half), half), :] = theirs[...].astype(F32)
    outgoing[...] = mm(placing[...], buf[...].astype(BF)).astype(BF)


def place_parts_kernel(placing, mine, theirs, *refs):
    *outs, buf, rows = refs
    place_kernel(placing, mine, theirs, rows, buf)
    z = depth()
    _, columns, size, _ = (1,) + outs[0].shape
    for k, out in enumerate(outs):
        for i in range(columns):
            at = ((z ^ k) * columns + i) * size
            out[i] = rows[pl.ds(pl.multiple_of(at, size), size), :]


def packed_kernel(keep, recv, out):
    assemble(keep, recv, out)


def lat_mix_kernel(lat_keep, lat_y, mine, theirs):
    c, _, _ = position()
    total = (lat_keep[...].astype(F32) + lat_y[...].astype(F32)).astype(BF)
    cols = mine.shape[1]
    mine[...] = jnp.where(c == 0, total[:, :cols], total[:, cols:])
    theirs[...] = jnp.where(c == 0, total[:, cols:], total[:, :cols])


def section_grad(gd, gshift, wa, wb, part, j, ch):
    half = STRIDE // 2
    first = part * half + j + half
    second = jnp.where(part == 0, 3 * half + j, j)
    rows1 = pl.ds(pl.multiple_of(first * ch, ch), ch)
    rows2 = pl.ds(pl.multiple_of(second * ch, ch), ch)
    w1 = jnp.concatenate([wa[rows1, :], wb[rows1, :]], 1)
    w2 = jnp.concatenate([wa[rows2, :], wb[rows2, :]], 1)
    return mm_nt(gd, w1) + mm_nt(gshift, w2)


def moved(gd, part):
    g = gd.astype(F32)
    return jnp.where(part == 0, shift(g, -1), shift(g, 1)).astype(BF)


def latent_grad_kernel(
    mask, g_own, g_core, g_y, g_far, adown, sdown, pa, pb,
    gd_out, swap, gproj_keep, gl,
):
    frames = adown.shape[0]
    width, lat = pa.shape
    pieces = g_own.shape[0]
    c, y, _ = position()
    blocks = (
        (g_own, 2 * y + c),
        (g_core, 2 * y + 1 - c),
        (g_y, 2 * (1 - y) + c),
        (g_far, 2 * (1 - y) + 1 - c),
    )
    for block, owner in blocks:
        for j in range(2):
            for i in range(gl.shape[0]):
                at = j * lat + i * LANES
                gl[i, pl.ds(2 * owner + j, pieces, stride=STRIDE), :] = block[
                    :, at : at + LANES
                ].astype(F32)
    g_latent = masked(jnp.concatenate([gl[i] for i in range(gl.shape[0])], 1), mask).astype(BF)
    proj = jnp.concatenate([pa[...], pb[...]], 0)
    gd = (mm_nt(g_latent, proj) * sdown[...]).astype(BF)
    gd_out[...] = gd
    swap[:frames] = gd[:, width:]
    gproj = mm_tn(adown[...], g_latent)
    swap[frames : frames + width] = gproj[width:, :width].astype(BF)
    swap[frames + width :] = gproj[width:, width:].astype(BF)
    gproj_keep[:width] = gproj[:width, :width]
    gproj_keep[width:] = gproj[:width, width:]


def section_send_kernel(gd, dwa, dwb, send):
    _, y, _ = position()
    full = gd[...]
    g2 = moved(full, 1 - y)
    for j in range(STRIDE // 2):
        send[j] = section_grad(full, g2, dwa, dwb, 1 - y, j, send.shape[2]).astype(BF)


def section_keep_kernel(gd, dwa, dwb, keep):
    _, y, _ = position()
    full = gd[...]
    g2 = moved(full, y)
    for j in range(STRIDE // 2):
        keep[j] = section_grad(full, g2, dwa, dwb, y, j, keep.shape[2])


def weight_grads(a2a, a2b, ga, gb, part, j):
    half = STRIDE // 2
    p = part * half + j
    return mm_tn(a2a[p], ga) + mm_tn(a2b[p], gb)


def pair(g, part):
    return jnp.concatenate([g, moved(g, part)], 1)


def down_send_kernel(a2a, a2b, gd, swap, gproj, send_u, send_s):
    frames = gd.shape[0]
    width = swap.shape[1]
    _, _, x = position()
    ga = pair(gd[:, :width], x)
    gb = pair(swap[:frames], x)
    rows = send_s.shape[1]
    extra = send_u.shape[1] - rows
    for j in range(STRIDE // 2):
        w = weight_grads(a2a, a2b, ga, gb, x, j)
        send_u[j, :rows] = w[:, :width].astype(BF)
        send_s[j] = w[:, width:].astype(BF)
        at = pl.ds(pl.multiple_of(((1 - x) * 4 + j) * extra, extra), extra)
        send_u[j, rows:] = (gproj[at, :] + swap[pl.ds(pl.multiple_of(frames + ((1 - x) * 4 + j) * extra, extra), extra), :].astype(F32)).astype(BF)


def down_keep_kernel(a2a, a2b, gd, swap, gproj, keep_u, keep_s):
    frames = gd.shape[0]
    width = swap.shape[1]
    _, _, x = position()
    part = 1 - x
    ga = pair(gd[:, :width], part)
    gb = pair(swap[:frames], part)
    rows = keep_s.shape[1]
    extra = keep_u.shape[1] - rows
    for j in range(STRIDE // 2):
        w = weight_grads(a2a, a2b, ga, gb, part, j)
        keep_u[j, :rows] = w[:, :width]
        keep_s[j] = w[:, width:]
        at = pl.ds(pl.multiple_of((x * 4 + j) * extra, extra), extra)
        keep_u[j, rows:] = gproj[at, :] + swap[pl.ds(pl.multiple_of(frames + (x * 4 + j) * extra, extra), extra), :].astype(F32)


def residual_kernel(
    mask, keep, recv, sec, ahid, shid, wo, a1, kept, send1, send2, send3, gh, buf,
):
    half = STRIDE // 2
    ch = keep.shape[2]
    hid = wo.shape[0]
    c, y, _ = position()
    g_out = jnp.zeros((hid, ch), F32)
    for j in range(half):
        g = keep[j] + recv[j].astype(F32)
        g_branch = masked(g * slope(sec[y * half + j].astype(F32)), mask).astype(BF)
        g_out = g_out + mm_tn(ahid[y * half + j], g_branch)
        gh[j] = mm_nt(g_branch, wo[...]) * shid[y * half + j].astype(F32)
    taps = [jnp.zeros((ch, hid), F32) for _ in range(3)]
    for j in range(half):
        g = gh[j]
        p = y * half + j
        here = g.astype(BF)
        taps[1] = taps[1] + mm_tn(a1[p], here)
        down1 = shift(g, 1)
        up1 = shift(g, -1)
        if j == 0:
            down1 = jnp.where(y == 0, shift(g, 2), down1)
        if j == half - 1:
            up1 = jnp.where(y == 1, shift(g, -2), up1)
        taps[0] = taps[0] + mm_tn(a1[lax.rem(p + STRIDE - 1, STRIDE)], down1.astype(BF))
        taps[2] = taps[2] + mm_tn(a1[lax.rem(p + 1, STRIDE)], up1.astype(BF))
    for k in range(3):
        for i in range(ch // hid):
            buf[k * (ch // hid) + i] = taps[k][i * hid : (i + 1) * hid]
    for i in range(ch // hid):
        buf[3 * (ch // hid) + i] = g_out[:, i * hid : (i + 1) * hid]
    m = 2 * y + c
    n = buf.shape[0] // 4
    for i in range(n):
        at = slice(i * hid, (i + 1) * hid)
        kept[at] = buf[m * n + i]
        for k, out in enumerate((send1, send2, send3)):
            out[at] = buf[(m ^ (k + 1)) * n + i].astype(BF)


def residual_finish_kernel(r0, r1, r2, r3, out_in, out_out, buf):
    c, y, _ = position()
    m = 2 * y + c
    rows, hid = r0.shape
    for k, r in enumerate((r0, r1, r2, r3)):
        buf[m ^ k] = r[...].astype(F32)
    for q in range(3):
        out_in[q * rows : (q + 1) * rows] = buf[q]
    for i in range(rows // hid):
        out_out[:, i * hid : (i + 1) * hid] = buf[3, i * hid : (i + 1) * hid]


def sum_kernel(keep, recv, own, *sends):
    z = depth()
    own[...] = keep[z] + recv[z].astype(F32)
    for k, out in enumerate(sends):
        at = z ^ (k + 1)
        out[...] = (keep[at] + recv[at].astype(F32)).astype(BF)


def swap_bit(value, axis, bit):
    n = lax.axis_size(axis)
    return lax.ppermute(value, axis, [(i, i ^ bit) for i in range(n)])


def stages_of(n):
    found, bit = [], 2
    while bit < n:
        members = 4 if n // bit >= 4 else 2
        found.append((bit, members))
        bit *= members
    return found


def pick(stack, index):
    return lax.dynamic_index_in_dim(stack, index, 0, keepdims=False)


def fan(values, axis, bit):
    return [swap_bit(v, axis, bit * (k + 1)) for k, v in enumerate(values)]


def plus(total, received):
    for r in received:
        total = total + r.astype(F32)
    return total


def reduce_rest(kept, received, me, stages):
    shape = kept.shape[1:]
    own, *sends = call(sum_kernel, [(shape, F32)] + [(shape, BF)] * 3, [kept, received])
    received = fan(sends, DP, stages[0][0])
    for bit, members in stages[1:]:
        parts = plus(own, received).reshape(members, -1, own.shape[-1])
        place = (me // bit) % members
        sends = [pick(parts, place ^ k).astype(BF) for k in range(1, members)]
        own, received = pick(parts, place), fan(sends, DP, bit)
    return plus(own, received).astype(BF)


def gather_high(own, me, stages):
    for bit, members in reversed(stages[1:]):
        place = (me // bit) % members
        blocks = [own] + fan([own] * (members - 1), DP, bit)
        ordered = jnp.stack(blocks)
        own = jnp.concatenate([pick(ordered, place ^ k) for k in range(members)], 0)
    return own


def finish_kernel(shifted, count, written, projected, *refs):
    ins, rest = refs[:count], refs[count:]
    if projected:
        *_, out, out_proj, buf, sems = rest
    else:
        *_, out, buf, sems = rest
    _, _, x = position()
    z = depth()
    half = STRIDE // 2
    rows = buf.shape[1]

    def block(entry):
        operand, lead, k, own = entry
        ref = ins[operand]
        value = ref if lead is None else ref.at[lead]
        part, xp = (1 - x, x) if own else (x, 1 - x)
        return value, z ^ k, part, xp

    copies = []
    for n, entry in enumerate(written):
        value, j, part, _ = block(entry)
        tap = part * half + j + half
        if shifted:
            tap = jnp.where(part == 0, 3 * half + j, j)
        buf[n] = value[:rows].astype(F32)
        copy = pltpu.make_async_copy(
            buf.at[n], out.at[pl.ds(pl.multiple_of(tap * rows, rows), rows), :], sems.at[n]
        )
        copy.start()
        copies.append(copy)
    for entry in projected:
        value, j, _, xp = block(entry)
        per = out_proj.shape[0] * 2 // STRIDE
        where = pl.ds(pl.multiple_of(j * per, per), per)
        width = value.shape[1]
        extra = value[rows : rows + per].astype(F32)

        @pl.when(xp == 0)
        def _():
            out_proj[where, :width] = extra

        @pl.when(xp == 1)
        def _():
            out_proj[where, width:] = extra

    for copy in copies:
        copy.wait()


def body(
    features, lengths, routes, res_in_weight, res_out_weight, down_weight, proj_weight, cotangent
):
    utts = lengths.shape[0]
    total_rows = features.shape[0] // utts
    ch = features.shape[1]
    frames = total_rows // STRIDE
    hid = res_out_weight.shape[0]
    width = down_weight.shape[1]
    lat = proj_weight.shape[1]
    dp_count = lax.axis_size(DP)
    pieces = routes.shape[0]
    half_pieces = pieces // utts
    capacity = 2 * pieces // dp_count
    slots = dp_count * capacity
    cols = cotangent.shape[1]
    half = STRIDE // 2
    me_dp = lax.axis_index(DP)
    stages = stages_of(dp_count)
    staged = dp_count == 8
    lane_block = ((dp_count // 2, capacity, cols), BF)
    pair_block = ((2, capacity, cols), BF)

    def through_dp(parts):
        received = fan(parts[1:], DP, 2)
        send, keep = call(columns_kernel, [lane_block] * 2, [parts[0], *received])
        return keep, swap_bit(send, DP, 1)

    def all_to_all(value):
        return lax.all_to_all(
            value.reshape(dp_count, capacity, cols), DP, split_axis=0, concat_axis=0
        ).reshape(slots, cols)

    other_down = swap_bit(down_weight, MP, 1)
    other_proj = swap_bit(proj_weight, MP, 1)
    if staged:
        parts = call(
            parts_kernel,
            [pair_block] * 4,
            [cotangent.reshape(dp_count // 2, 2, capacity, cols)],
            scratch=[pltpu.SemaphoreType.DMA((4,))],
            where={0: pltpu.HBM},
        )
        returned = through_dp(parts)
    else:
        returned = [all_to_all(cotangent)]

    loads = 4
    wide = ((STRIDE, frames, ch), BF)
    narrow = ((STRIDE, frames, hid), BF)
    a1, sig, ys, wo, placing, mask = call(
        functools.partial(forward_kernel, capacity),
        [
            wide,
            wide,
            ((STRIDE, frames, 3 * hid), F32),
            (res_out_weight.shape, BF),
            ((slots, pieces), BF),
            ((frames, LANES), F32),
        ],
        [lengths, features, routes.reshape(1, pieces), res_in_weight, res_out_weight],
        scratch=[
            pltpu.VMEM((ch // LANES, total_rows, LANES), F32),
            pltpu.SMEM(lengths.shape, lengths.dtype),
            pltpu.VMEM((loads, total_rows // loads, ch), BF),
            pltpu.VMEM((1, pieces), routes.dtype),
            pltpu.VMEM(res_in_weight.shape, BF),
            pltpu.SemaphoreType.DMA((loads + 4,)),
        ],
        where={i: pltpu.HBM for i in range(5)},
        flops=1 << 30,
    )
    a2, sec, ahid, shid = call(
        section_kernel, [wide, wide, narrow, narrow], [sig, ys, wo, mask], flops=1 << 30
    )
    other_a2 = swap_bit(a2, MP, 1)
    adown, sdown, lat_send, lat_keep = call(
        down_kernel,
        [
            ((frames, 2 * width), BF),
            ((frames, 2 * width), F32),
            ((half_pieces, half * lat), BF),
            ((half_pieces, half * lat), BF),
        ],
        [mask, a2, down_weight, other_down, proj_weight, other_proj],
        scratch=[pltpu.VMEM((lat // LANES, frames, LANES), F32)],
        flops=1 << 30,
    )
    lat_y = swap_bit(lat_send, MP, 2)

    g_own, g_other = call(
        pick_kernel,
        [((half_pieces, cols), BF), ((half_pieces, cols), BF)],
        [placing, *returned],
        scratch=[pltpu.VMEM((slots, cols), BF), pltpu.VMEM((pieces, cols), F32)],
    )
    g_y = swap_bit(g_own, MP, 2)
    g_far = swap_bit(g_other, MP, 3)
    g_core = swap_bit(g_other, MP, 1)

    mine, theirs = call(
        lat_mix_kernel, [((half_pieces, cols), BF)] * 2, [lat_keep, lat_y]
    )
    theirs = swap_bit(theirs, MP, 1)

    gd, swap, gproj = call(
        latent_grad_kernel,
        [
            ((frames, 2 * width), BF),
            ((frames + 2 * width, width), BF),
            ((2 * width, lat // 2), F32),
        ],
        [mask, g_own, g_core, g_y, g_far, adown, sdown, proj_weight, other_proj],
        scratch=[pltpu.VMEM((lat // LANES, frames, LANES), F32)],
        flops=1 << 30,
    )
    got = swap_bit(swap, MP, 1)
    (g_send,) = call(
        section_send_kernel,
        [((half, frames, ch), BF)],
        [gd, down_weight, other_down],
        flops=1 << 29,
    )
    g_recv = swap_bit(g_send, MP, 2)
    extra = 2 * width // STRIDE
    send_u, send_s = call(
        down_send_kernel,
        [((half, ch + extra, width), BF), ((half, ch, width), BF)],
        [a2, other_a2, gd, got, gproj],
        flops=1 << 29,
    )
    recv_u = swap_bit(send_u, DP, 1)
    recv_s = swap_bit(send_s, DP, 1)
    keep_u, keep_s = call(
        down_keep_kernel,
        [((half, ch + extra, width), F32), ((half, ch, width), F32)],
        [a2, other_a2, gd, got, gproj],
        flops=1 << 29,
    )
    (keep_g,) = call(
        section_keep_kernel,
        [((half, frames, ch), F32)],
        [gd, down_weight, other_down],
        flops=1 << 29,
    )

    row_scratch = pltpu.VMEM((pieces, cols), F32)
    if staged:
        parts = call(
            place_parts_kernel,
            [pair_block] * 4,
            [placing, mine, theirs],
            scratch=[row_scratch, pltpu.VMEM((slots, cols), BF)],
        )
        (packed,) = call(packed_kernel, [((slots, cols), BF)], [*through_dp(parts)])
    else:
        (outgoing,) = call(
            place_kernel,
            [((slots, cols), BF)],
            [placing, mine, theirs],
            scratch=[row_scratch],
        )
        packed = all_to_all(outgoing)

    blocks = 4 * (ch // hid)
    quarter = (blocks // 4 * hid, hid)
    e_own, *e_sends = call(
        residual_kernel,
        [(quarter, F32)] + [(quarter, BF)] * 3,
        [mask, keep_g, g_recv, sec, ahid, shid, wo, a1],
        scratch=[pltpu.VMEM((half, frames, hid), F32), pltpu.VMEM((blocks, hid, hid), F32)],
        flops=1 << 30,
    )
    received = fan(e_sends, MP, 1)
    e_own = plus(e_own, received)
    sent = e_own.astype(BF)

    own_u = gather_high(reduce_rest(keep_u, recv_u, me_dp, stages), me_dp, stages)
    own_s = gather_high(reduce_rest(keep_s, recv_s, me_dp, stages), me_dp, stages)
    all_u = [own_u] + fan([own_u] * 3, DP, stages[0][0])
    both = jnp.concatenate([own_s, sent])
    first_s = swap_bit(both, DP, 1)
    all_s = [own_s] + fan([own_s] * 3, DP, stages[0][0])
    their_u = swap_bit(jnp.stack(all_u), DP, 1)
    their_s = swap_bit(jnp.stack(all_s[1:]), DP, 1)
    received = [first_s[own_s.shape[0] :]]
    for bit, members in stages:
        e_own = plus(e_own, received)
        sent = e_own.astype(BF)
        received = fan([sent] * (members - 1), DP, bit)
    sent = plus(e_own, received).astype(BF)
    grad_res_in, grad_res_out = call(
        residual_finish_kernel,
        [((3 * ch, hid), F32), ((hid, ch), F32)],
        [sent, *fan([sent] * 3, MP, 1)],
        scratch=[pltpu.VMEM((4,) + quarter, F32)],
    )

    down_out = ((2 * STRIDE * ch, width), F32)
    mine = tuple((k, None, k, True) for k in range(4))

    def finish(shifted, ins, written, projected, before=None):
        n = len(ins)
        aliased = before is not None
        return call(
            functools.partial(finish_kernel, shifted, n, written, projected),
            [down_out] + [((width, lat), F32)] * bool(projected),
            [*ins] + [before] * aliased,
            scratch=[
                pltpu.VMEM((len(written), ch, width), F32),
                pltpu.SemaphoreType.DMA((len(written),)),
            ],
            where={n: pltpu.HBM, n + aliased: pltpu.HBM},
            aliases={n: 0} if aliased else None,
        )

    first = mine + tuple((4, k, k, False) for k in range(4))
    grad_down, grad_proj = finish(False, [*all_u, their_u], first, first)
    second = mine + ((4, None, 0, False),)
    (grad_down,) = finish(True, [*all_s, first_s], second, (), grad_down)
    last = tuple((0, k - 1, k, False) for k in range(1, 4))
    (grad_down,) = finish(True, [their_s], last, (), grad_down)
    return (packed, grad_res_in, grad_res_out, grad_down, grad_proj)


def solution(mesh):
    return jax.shard_map(
        body,
        mesh=mesh,
        in_specs=(
            P(DP, None),
            P(DP),
            P(DP, None),
            P(),
            P(),
            P(None, MP),
            P(MP, None),
            P(DP, MP),
        ),
        out_specs=(P(DP, MP), P(), P(), P(None, MP), P(MP, None)),
        check_vma=False,
    )
```

```python
import functools
import jax
import jax.numpy as jnp
from jax import lax
from jax.experimental import pallas as pl
from jax.experimental.pallas import tpu as pltpu
from jax.sharding import PartitionSpec as P

STRIDE = 8
DP, MP = "dp", "mp"
LANES = 128
BF = jnp.bfloat16
F32 = jnp.float32
VMEM_LIMIT = 16 << 20


def elu(v):
    return jnp.where(v > 0, v, jnp.exp(jnp.minimum(v, 0.0)) - 1.0)


def slope(v):
    return jnp.where(v > 0, 1.0, jnp.exp(jnp.minimum(v, 0.0)))


def mm(a, b):
    return jnp.dot(a, b, preferred_element_type=F32)


def mm_nt(a, b):
    return lax.dot_general(a, b, (((1,), (1,)), ((), ())), preferred_element_type=F32)


def mm_tn(a, b):
    return lax.dot_general(a, b, (((0,), (0,)), ((), ())), preferred_element_type=F32)


def shift(v, s):
    n = v.shape[0]
    rows = lax.broadcasted_iota(jnp.int32, v.shape, 0)
    rolled = pltpu.roll(v, (-s) % n, 0)
    keep = rows < n - s if s > 0 else rows >= -s
    return jnp.where(keep, rolled, 0.0)


def spread(ref, value):
    for i in range(ref.shape[0]):
        ref[i] = value[:, i * LANES : (i + 1) * LANES]


def every(ref, start, size):
    return jnp.concatenate(
        [ref[i, pl.ds(start, size, stride=STRIDE), :] for i in range(ref.shape[0])], 1
    )


def call(kernel, outs, ins, scratch=(), flops=0, where=None, aliases=None):
    whole = pl.BlockSpec(memory_space=pltpu.VMEM)
    spaces = {i: pl.BlockSpec(memory_space=space) for i, space in (where or {}).items()}
    ins = [
        pltpu.with_memory_space_constraint(a, pltpu.HBM) if i in spaces else a
        for i, a in enumerate(ins)
    ]
    return pl.pallas_call(
        kernel,
        out_shape=[jax.ShapeDtypeStruct(s, d) for s, d in outs],
        in_specs=[spaces.get(i, whole) for i in range(len(ins))],
        out_specs=[spaces.get(len(ins) + i, whole) for i in range(len(outs))],
        scratch_shapes=list(scratch),
        input_output_aliases=aliases or {},
        compiler_params=pltpu.CompilerParams(vmem_limit_bytes=VMEM_LIMIT),
        cost_estimate=pl.CostEstimate(
            flops=flops, transcendentals=0, bytes_accessed=1 << 20
        ),
    )(*ins)


def position():
    m = lax.axis_index(MP)
    return lax.rem(m, 2), m // 2, lax.rem(lax.axis_index(DP), 2)


def masked(value, mask):
    wide = jnp.concatenate([mask[...]] * (value.shape[1] // mask.shape[1]), 1)
    return jnp.where(wide > 0, value, 0.0)


def depth():
    return lax.rem(lax.axis_index(DP) // 2, 4)


def forward_kernel(
    capacity, lengths_hbm, feat_hbm, routes_hbm, wi_hbm, wo_hbm,
    a1, a2, sec, ahid, shid, placing, mask, xs, ys, lengths, feat, routes, wi, wo, sems,
):
    frames, ch = a1.shape[1], a1.shape[2]
    hid = wo.shape[0]
    c, _, _ = position()
    rows = frames * STRIDE
    parts = feat.shape[0]
    size = rows // parts
    copies = [
        pltpu.make_async_copy(
            feat_hbm.at[pl.ds(pl.multiple_of(c * rows + i * size, size), size), :],
            feat.at[i],
            sems.at[i],
        )
        for i in range(parts)
    ]
    rest = [
        pltpu.make_async_copy(src, dst, sems.at[parts + i])
        for i, (src, dst) in enumerate(((routes_hbm, routes), (wi_hbm, wi), (wo_hbm, wo)))
    ]
    table = pltpu.make_async_copy(lengths_hbm, lengths, sems.at[parts + len(rest)])
    table.start()
    for copy in copies + rest:
        copy.start()
    table.wait()
    length = lengths[c]
    live = lax.broadcasted_iota(jnp.int32, (frames, ch), 0) < length
    mask[...] = jnp.where(live[:, : mask.shape[1]], 1.0, 0.0)
    for i in range(parts):
        copies[i].wait()
        value = feat[i].astype(F32)
        for k in range(xs.shape[0]):
            xs[k, i * size : (i + 1) * size] = value[:, k * LANES : (k + 1) * LANES]
    for copy in rest:
        copy.wait()
    placing[...] = placing_of(routes[...], placing.shape[0], capacity)
    wcat = jnp.concatenate([wi[k * ch : (k + 1) * ch, :] for k in range(3)], 1)

    def signal(p):
        return jnp.where(live, every(xs, p, frames), 0.0)

    for p in range(STRIDE):
        act = elu(signal(p)).astype(BF)
        a1[p] = act
        ys[p] = mm(act, wcat)
    for p in range(STRIDE):
        left = shift(ys[(p - 1) % STRIDE, :, :hid], -1 if p > 0 else -2)
        right = shift(ys[(p + 1) % STRIDE, :, 2 * hid :], 1 if p < STRIDE - 1 else 2)
        hidden = left + ys[p, :, hid : 2 * hid] + right
        act_hid = elu(hidden).astype(BF)
        ahid[p] = act_hid
        shid[p] = slope(hidden).astype(BF)
        section = jnp.where(live, signal(p) + mm(act_hid, wo[...]), 0.0).astype(BF)
        sec[p] = section
        a2[p] = elu(section.astype(F32)).astype(BF)


def down_kernel(
    mask, a2, dwa, dwb, pa, pb, adown, sdown, lat_send, lat_keep, ls,
):
    frames, ch = a2.shape[1], a2.shape[2]
    _, y, _ = position()
    half = STRIDE // 2

    def tap(k):
        return jnp.concatenate([dwa[k * ch : (k + 1) * ch, :], dwb[k * ch : (k + 1) * ch, :]], 1)

    down = jnp.zeros((frames, 2 * dwa.shape[1]), F32)
    before = jnp.zeros_like(down)
    after = jnp.zeros_like(down)
    for p in range(STRIDE):
        act = a2[p]
        down = down + mm(act, tap(p + half))
        if p < half:
            after = after + mm(act, tap(p + 3 * half))
        else:
            before = before + mm(act, tap(p - half))
    down = down + shift(before, -1) + shift(after, 1)
    act_down = elu(down).astype(BF)
    adown[...] = act_down
    sdown[...] = slope(down)
    proj = jnp.concatenate([pa[...], pb[...]], 0)
    lat = proj.shape[1]
    spread(ls, masked(mm(act_down, proj), mask))
    pieces = frames // STRIDE
    for j in range(half):
        cols = slice(j * lat, (j + 1) * lat)
        lat_send[:, cols] = every(ls, half * (1 - y) + j, pieces).astype(BF)
        lat_keep[:, cols] = every(ls, half * y + j, pieces).astype(BF)


def placing_of(targets, slots, capacity):
    pieces = targets.shape[1]
    chosen = jnp.where(targets == lax.broadcasted_iota(jnp.int32, (128, pieces), 0), 1.0, 0.0)
    upper = (
        lax.broadcasted_iota(jnp.int32, (pieces, pieces), 0)
        < lax.broadcasted_iota(jnp.int32, (pieces, pieces), 1)
    )
    earlier = mm(chosen.astype(BF), jnp.where(upper, 1.0, 0.0).astype(BF))
    rank = jnp.sum(earlier * chosen, axis=0, keepdims=True).astype(jnp.int32)
    slot = targets * capacity + rank
    ids = lax.broadcasted_iota(jnp.int32, (slots, pieces), 0)
    return jnp.where(slot == ids, 1.0, 0.0).astype(BF)


def parts_kernel(whole, *refs):
    *outs, sems = refs
    z = depth()
    copies = [
        pltpu.make_async_copy(whole.at[z ^ k], out, sems.at[k]) for k, out in enumerate(outs)
    ]
    for copy in copies:
        copy.start()
    for copy in copies:
        copy.wait()


def columns_kernel(*refs):
    *parts, send, keep = refs
    _, _, x = position()
    for k, part in enumerate(parts):
        send[k] = part[1 - x]
        keep[k] = part[x]


def assemble(keep, recv, out):
    _, _, x = position()
    z = depth()
    size = keep.shape[1]
    for k in range(keep.shape[0]):
        for part, column in ((keep, x), (recv, 1 - x)):
            at = (2 * (z ^ k) + column) * size
            out[pl.ds(pl.multiple_of(at, size), size), :] = part[k]


def pick_kernel(placing, *refs):
    *parts, own, other, rows, buf = refs
    c, _, _ = position()
    if len(parts) == 1:
        rows[...] = parts[0][...]
    else:
        assemble(*parts, rows)
    buf[...] = mm_tn(placing[...], rows[...])
    half = own.shape[0]
    own[...] = buf[pl.ds(pl.multiple_of(c * half, half), half), :].astype(BF)
    other[...] = buf[pl.ds(pl.multiple_of((1 - c) * half, half), half), :].astype(BF)


def place_kernel(placing, mine, theirs, outgoing, buf):
    c, _, _ = position()
    half = mine.shape[0]
    buf[pl.ds(pl.multiple_of(c * half, half), half), :] = mine[...].astype(F32)
    buf[pl.ds(pl.multiple_of((1 - c) * half, half), half), :] = theirs[...].astype(F32)
    outgoing[...] = mm(placing[...], buf[...].astype(BF)).astype(BF)


def place_parts_kernel(placing, mine, theirs, *refs):
    *outs, buf, rows = refs
    place_kernel(placing, mine, theirs, rows, buf)
    z = depth()
    _, columns, size, _ = (1,) + outs[0].shape
    for k, out in enumerate(outs):
        for i in range(columns):
            at = ((z ^ k) * columns + i) * size
            out[i] = rows[pl.ds(pl.multiple_of(at, size), size), :]


def packed_kernel(keep, recv, out):
    assemble(keep, recv, out)


def lat_mix_kernel(lat_keep, lat_y, mine, theirs):
    c, _, _ = position()
    total = (lat_keep[...].astype(F32) + lat_y[...].astype(F32)).astype(BF)
    cols = mine.shape[1]
    mine[...] = jnp.where(c == 0, total[:, :cols], total[:, cols:])
    theirs[...] = jnp.where(c == 0, total[:, cols:], total[:, :cols])


def section_grad(gd, gshift, wa, wb, part, j, ch):
    half = STRIDE // 2
    first = part * half + j + half
    second = jnp.where(part == 0, 3 * half + j, j)
    rows1 = pl.ds(pl.multiple_of(first * ch, ch), ch)
    rows2 = pl.ds(pl.multiple_of(second * ch, ch), ch)
    w1 = jnp.concatenate([wa[rows1, :], wb[rows1, :]], 1)
    w2 = jnp.concatenate([wa[rows2, :], wb[rows2, :]], 1)
    return mm_nt(gd, w1) + mm_nt(gshift, w2)


def moved(gd, part):
    g = gd.astype(F32)
    return jnp.where(part == 0, shift(g, -1), shift(g, 1)).astype(BF)


def latent_grad_kernel(
    mask, g_own, g_core, g_y, g_far, adown, sdown, pa, pb,
    gd_out, swap, gproj_keep, gl,
):
    frames = adown.shape[0]
    width, lat = pa.shape
    pieces = g_own.shape[0]
    c, y, _ = position()
    blocks = (
        (g_own, 2 * y + c),
        (g_core, 2 * y + 1 - c),
        (g_y, 2 * (1 - y) + c),
        (g_far, 2 * (1 - y) + 1 - c),
    )
    for block, owner in blocks:
        for j in range(2):
            for i in range(gl.shape[0]):
                at = j * lat + i * LANES
                gl[i, pl.ds(2 * owner + j, pieces, stride=STRIDE), :] = block[
                    :, at : at + LANES
                ].astype(F32)
    g_latent = masked(jnp.concatenate([gl[i] for i in range(gl.shape[0])], 1), mask).astype(BF)
    proj = jnp.concatenate([pa[...], pb[...]], 0)
    gd = (mm_nt(g_latent, proj) * sdown[...]).astype(BF)
    gd_out[...] = gd
    swap[:frames] = gd[:, width:]
    gproj = mm_tn(adown[...], g_latent)
    swap[frames : frames + width] = gproj[width:, :width].astype(BF)
    swap[frames + width :] = gproj[width:, width:].astype(BF)
    gproj_keep[:width] = gproj[:width, :width]
    gproj_keep[width:] = gproj[:width, width:]


def section_send_kernel(gd, dwa, dwb, send):
    _, y, _ = position()
    full = gd[...]
    g2 = moved(full, 1 - y)
    for j in range(STRIDE // 2):
        send[j] = section_grad(full, g2, dwa, dwb, 1 - y, j, send.shape[2]).astype(BF)


def section_keep_kernel(gd, dwa, dwb, keep):
    _, y, _ = position()
    full = gd[...]
    g2 = moved(full, y)
    for j in range(STRIDE // 2):
        keep[j] = section_grad(full, g2, dwa, dwb, y, j, keep.shape[2])


def weight_grads(a2a, a2b, ga, gb, part, j):
    half = STRIDE // 2
    p = part * half + j
    return mm_tn(a2a[p], ga) + mm_tn(a2b[p], gb)


def pair(g, part):
    return jnp.concatenate([g, moved(g, part)], 1)


def down_send_kernel(a2a, a2b, gd, swap, gproj, send_u, send_s):
    frames = gd.shape[0]
    width = swap.shape[1]
    _, _, x = position()
    ga = pair(gd[:, :width], x)
    gb = pair(swap[:frames], x)
    extra = send_s.shape[1] - send_u.shape[1]
    rows = send_u.shape[1]
    for j in range(STRIDE // 2):
        w = weight_grads(a2a, a2b, ga, gb, x, j)
        send_u[j] = w[:, :width].astype(BF)
        send_s[j, :rows] = w[:, width:].astype(BF)
        at = pl.ds(pl.multiple_of(((1 - x) * 4 + j) * extra, extra), extra)
        send_s[j, rows:] = (gproj[at, :] + swap[pl.ds(pl.multiple_of(frames + ((1 - x) * 4 + j) * extra, extra), extra), :].astype(F32)).astype(BF)


def down_keep_kernel(a2a, a2b, gd, swap, gproj, keep_u, keep_s):
    frames = gd.shape[0]
    width = swap.shape[1]
    _, _, x = position()
    part = 1 - x
    ga = pair(gd[:, :width], part)
    gb = pair(swap[:frames], part)
    extra = keep_s.shape[1] - keep_u.shape[1]
    rows = keep_u.shape[1]
    for j in range(STRIDE // 2):
        w = weight_grads(a2a, a2b, ga, gb, part, j)
        keep_u[j] = w[:, :width]
        keep_s[j, :rows] = w[:, width:]
        at = pl.ds(pl.multiple_of((x * 4 + j) * extra, extra), extra)
        keep_s[j, rows:] = gproj[at, :] + swap[pl.ds(pl.multiple_of(frames + (x * 4 + j) * extra, extra), extra), :].astype(F32)


def residual_kernel(
    mask, keep, recv, sec, ahid, shid, wo, a1, kept, send1, send2, send3, gh, buf,
):
    half = STRIDE // 2
    ch = keep.shape[2]
    hid = wo.shape[0]
    c, y, _ = position()
    g_out = jnp.zeros((hid, ch), F32)
    for j in range(half):
        g = keep[j] + recv[j].astype(F32)
        g_branch = masked(g * slope(sec[y * half + j].astype(F32)), mask).astype(BF)
        g_out = g_out + mm_tn(ahid[y * half + j], g_branch)
        gh[j] = mm_nt(g_branch, wo[...]) * shid[y * half + j].astype(F32)
    taps = [jnp.zeros((ch, hid), F32) for _ in range(3)]
    for j in range(half):
        g = gh[j]
        p = y * half + j
        here = g.astype(BF)
        taps[1] = taps[1] + mm_tn(a1[p], here)
        down1 = shift(g, 1)
        up1 = shift(g, -1)
        if j == 0:
            down1 = jnp.where(y == 0, shift(g, 2), down1)
        if j == half - 1:
            up1 = jnp.where(y == 1, shift(g, -2), up1)
        taps[0] = taps[0] + mm_tn(a1[lax.rem(p + STRIDE - 1, STRIDE)], down1.astype(BF))
        taps[2] = taps[2] + mm_tn(a1[lax.rem(p + 1, STRIDE)], up1.astype(BF))
    for k in range(3):
        for i in range(ch // hid):
            buf[k * (ch // hid) + i] = taps[k][i * hid : (i + 1) * hid]
    for i in range(ch // hid):
        buf[3 * (ch // hid) + i] = g_out[:, i * hid : (i + 1) * hid]
    m = 2 * y + c
    n = buf.shape[0] // 4
    for i in range(n):
        at = slice(i * hid, (i + 1) * hid)
        kept[at] = buf[m * n + i]
        for k, out in enumerate((send1, send2, send3)):
            out[at] = buf[(m ^ (k + 1)) * n + i].astype(BF)


def residual_finish_kernel(r0, r1, r2, r3, out_in, out_out, buf, sems):
    c, y, _ = position()
    m = 2 * y + c
    rows, hid = r0.shape
    for k, r in enumerate((r0, r1, r2, r3)):
        buf[m ^ k] = r[...].astype(F32)
    copies = [
        pltpu.make_async_copy(buf.at[q], out_in.at[pl.ds(q * rows, rows), :], sems.at[q])
        for q in range(3)
    ] + [
        pltpu.make_async_copy(
            buf.at[3, pl.ds(i * hid, hid), :], out_out.at[:, pl.ds(i * hid, hid)], sems.at[4 + i]
        )
        for i in range(rows // hid)
    ]
    for copy in copies:
        copy.start()
    for copy in copies:
        copy.wait()


def sum_kernel(keep, recv, own, *sends):
    z = depth()
    own[...] = keep[z] + recv[z].astype(F32)
    for k, out in enumerate(sends):
        at = z ^ (k + 1)
        out[...] = (keep[at] + recv[at].astype(F32)).astype(BF)


def swap_bit(value, axis, bit):
    n = lax.axis_size(axis)
    return lax.ppermute(value, axis, [(i, i ^ bit) for i in range(n)])


def stages_of(n):
    found, bit = [], 2
    while bit < n:
        members = 4 if n // bit >= 4 else 2
        found.append((bit, members))
        bit *= members
    return found


def pick(stack, index):
    return lax.dynamic_index_in_dim(stack, index, 0, keepdims=False)


def fan(values, axis, bit):
    return [swap_bit(v, axis, bit * (k + 1)) for k, v in enumerate(values)]


def plus(total, received):
    for r in received:
        total = total + r.astype(F32)
    return total


def reduce_rest(kept, received, me, stages):
    shape = kept.shape[1:]
    own, *sends = call(sum_kernel, [(shape, F32)] + [(shape, BF)] * 3, [kept, received])
    received = fan(sends, DP, stages[0][0])
    for bit, members in stages[1:]:
        parts = plus(own, received).reshape(members, -1, own.shape[-1])
        place = (me // bit) % members
        sends = [pick(parts, place ^ k).astype(BF) for k in range(1, members)]
        own, received = pick(parts, place), fan(sends, DP, bit)
    return plus(own, received).astype(BF)


def gather_high(own, me, stages):
    for bit, members in reversed(stages[1:]):
        place = (me // bit) % members
        blocks = [own] + fan([own] * (members - 1), DP, bit)
        ordered = jnp.stack(blocks)
        own = jnp.concatenate([pick(ordered, place ^ k) for k in range(members)], 0)
    return own


def finish_kernel(shifted, count, written, projected, *refs):
    ins, rest = refs[:count], refs[count:]
    if projected:
        *_, out, out_proj, buf, sems = rest
    else:
        *_, out, buf, sems = rest
    _, _, x = position()
    z = depth()
    half = STRIDE // 2
    rows = buf.shape[1]

    def block(entry):
        operand, lead, k, own = entry
        ref = ins[operand]
        value = ref if lead is None else ref.at[lead]
        part, xp = (1 - x, x) if own else (x, 1 - x)
        return value, z ^ k, part, xp

    copies = []
    for n, entry in enumerate(written):
        value, j, part, _ = block(entry)
        tap = part * half + j + half
        if shifted:
            tap = jnp.where(part == 0, 3 * half + j, j)
        buf[n] = value[:rows].astype(F32)
        copy = pltpu.make_async_copy(
            buf.at[n], out.at[pl.ds(pl.multiple_of(tap * rows, rows), rows), :], sems.at[n]
        )
        copy.start()
        copies.append(copy)
    for entry in projected:
        value, j, _, xp = block(entry)
        per = out_proj.shape[0] * 2 // STRIDE
        where = pl.ds(pl.multiple_of(j * per, per), per)
        width = value.shape[1]
        extra = value[rows : rows + per].astype(F32)

        @pl.when(xp == 0)
        def _():
            out_proj[where, :width] = extra

        @pl.when(xp == 1)
        def _():
            out_proj[where, width:] = extra

    for copy in copies:
        copy.wait()


def body(
    features, lengths, routes, res_in_weight, res_out_weight, down_weight, proj_weight, cotangent
):
    utts = lengths.shape[0]
    total_rows = features.shape[0] // utts
    ch = features.shape[1]
    frames = total_rows // STRIDE
    hid = res_out_weight.shape[0]
    width = down_weight.shape[1]
    lat = proj_weight.shape[1]
    dp_count = lax.axis_size(DP)
    pieces = routes.shape[0]
    half_pieces = pieces // utts
    capacity = 2 * pieces // dp_count
    slots = dp_count * capacity
    cols = cotangent.shape[1]
    half = STRIDE // 2
    me_dp = lax.axis_index(DP)
    stages = stages_of(dp_count)
    staged = dp_count == 8
    lane_block = ((dp_count // 2, capacity, cols), BF)
    pair_block = ((2, capacity, cols), BF)

    def through_dp(parts):
        received = fan(parts[1:], DP, 2)
        send, keep = call(columns_kernel, [lane_block] * 2, [parts[0], *received])
        return keep, swap_bit(send, DP, 1)

    def all_to_all(value):
        return lax.all_to_all(
            value.reshape(dp_count, capacity, cols), DP, split_axis=0, concat_axis=0
        ).reshape(slots, cols)

    other_down = swap_bit(down_weight, MP, 1)
    other_proj = swap_bit(proj_weight, MP, 1)
    if staged:
        parts = call(
            parts_kernel,
            [pair_block] * 4,
            [cotangent.reshape(dp_count // 2, 2, capacity, cols)],
            scratch=[pltpu.SemaphoreType.DMA((4,))],
            where={0: pltpu.HBM},
        )
        returned = through_dp(parts)
    else:
        returned = [all_to_all(cotangent)]

    loads = 4
    a1, a2, sec, ahid, shid, placing, mask = call(
        functools.partial(forward_kernel, capacity),
        [
            ((STRIDE, frames, ch), BF),
            ((STRIDE, frames, ch), BF),
            ((STRIDE, frames, ch), BF),
            ((STRIDE, frames, hid), BF),
            ((STRIDE, frames, hid), BF),
            ((slots, pieces), BF),
            ((frames, LANES), F32),
        ],
        [lengths, features, routes.reshape(1, pieces), res_in_weight, res_out_weight],
        scratch=[
            pltpu.VMEM((ch // LANES, total_rows, LANES), F32),
            pltpu.VMEM((STRIDE, frames, 3 * hid), F32),
            pltpu.SMEM(lengths.shape, lengths.dtype),
            pltpu.VMEM((loads, total_rows // loads, ch), BF),
            pltpu.VMEM((1, pieces), routes.dtype),
            pltpu.VMEM(res_in_weight.shape, BF),
            pltpu.VMEM(res_out_weight.shape, BF),
            pltpu.SemaphoreType.DMA((loads + 4,)),
        ],
        where={i: pltpu.HBM for i in range(5)},
        flops=4 << 30,
    )
    other_a2 = swap_bit(a2, MP, 1)
    adown, sdown, lat_send, lat_keep = call(
        down_kernel,
        [
            ((frames, 2 * width), BF),
            ((frames, 2 * width), F32),
            ((half_pieces, half * lat), BF),
            ((half_pieces, half * lat), BF),
        ],
        [mask, a2, down_weight, other_down, proj_weight, other_proj],
        scratch=[pltpu.VMEM((lat // LANES, frames, LANES), F32)],
        flops=1 << 30,
    )
    lat_y = swap_bit(lat_send, MP, 2)

    g_own, g_other = call(
        pick_kernel,
        [((half_pieces, cols), BF), ((half_pieces, cols), BF)],
        [placing, *returned],
        scratch=[pltpu.VMEM((slots, cols), BF), pltpu.VMEM((pieces, cols), F32)],
    )
    g_y = swap_bit(g_own, MP, 2)
    g_far = swap_bit(g_other, MP, 3)
    g_core = swap_bit(g_other, MP, 1)

    mine, theirs = call(
        lat_mix_kernel, [((half_pieces, cols), BF)] * 2, [lat_keep, lat_y]
    )
    theirs = swap_bit(theirs, MP, 1)

    gd, swap, gproj = call(
        latent_grad_kernel,
        [
            ((frames, 2 * width), BF),
            ((frames + 2 * width, width), BF),
            ((2 * width, lat // 2), F32),
        ],
        [mask, g_own, g_core, g_y, g_far, adown, sdown, proj_weight, other_proj],
        scratch=[pltpu.VMEM((lat // LANES, frames, LANES), F32)],
        flops=1 << 30,
    )
    got = swap_bit(swap, MP, 1)
    (g_send,) = call(
        section_send_kernel,
        [((half, frames, ch), BF)],
        [gd, down_weight, other_down],
        flops=1 << 29,
    )
    g_recv = swap_bit(g_send, MP, 2)
    extra = 2 * width // STRIDE
    send_u, send_s = call(
        down_send_kernel,
        [((half, ch, width), BF), ((half, ch + extra, width), BF)],
        [a2, other_a2, gd, got, gproj],
        flops=1 << 29,
    )
    recv_u = swap_bit(send_u, DP, 1)
    recv_s = swap_bit(send_s, DP, 1)
    keep_u, keep_s = call(
        down_keep_kernel,
        [((half, ch, width), F32), ((half, ch + extra, width), F32)],
        [a2, other_a2, gd, got, gproj],
        flops=1 << 29,
    )
    (keep_g,) = call(
        section_keep_kernel,
        [((half, frames, ch), F32)],
        [gd, down_weight, other_down],
        flops=1 << 29,
    )

    row_scratch = pltpu.VMEM((pieces, cols), F32)
    if staged:
        parts = call(
            place_parts_kernel,
            [pair_block] * 4,
            [placing, mine, theirs],
            scratch=[row_scratch, pltpu.VMEM((slots, cols), BF)],
        )
        (packed,) = call(packed_kernel, [((slots, cols), BF)], [*through_dp(parts)])
    else:
        (outgoing,) = call(
            place_kernel,
            [((slots, cols), BF)],
            [placing, mine, theirs],
            scratch=[row_scratch],
        )
        packed = all_to_all(outgoing)

    blocks = 4 * (ch // hid)
    quarter = (blocks // 4 * hid, hid)
    e_own, *e_sends = call(
        residual_kernel,
        [(quarter, F32)] + [(quarter, BF)] * 3,
        [mask, keep_g, g_recv, sec, ahid, shid, res_out_weight, a1],
        scratch=[pltpu.VMEM((half, frames, hid), F32), pltpu.VMEM((blocks, hid, hid), F32)],
        flops=1 << 30,
    )
    received = fan(e_sends, MP, 1)
    e_own = plus(e_own, received)
    sent = e_own.astype(BF)

    own_u = gather_high(reduce_rest(keep_u, recv_u, me_dp, stages), me_dp, stages)
    own_s = gather_high(reduce_rest(keep_s, recv_s, me_dp, stages), me_dp, stages)
    all_u = [own_u] + fan([own_u] * 3, DP, stages[0][0])
    both = jnp.concatenate([own_s, sent])
    first_s = swap_bit(both, DP, 1)
    all_s = [own_s] + fan([own_s] * 3, DP, stages[0][0])
    their_u = swap_bit(jnp.stack(all_u), DP, 1)
    their_s = swap_bit(jnp.stack(all_s[1:]), DP, 1)
    received = [first_s[own_s.shape[0] :]]
    for bit, members in stages:
        e_own = plus(e_own, received)
        sent = e_own.astype(BF)
        received = fan([sent] * (members - 1), DP, bit)
    sent = plus(e_own, received).astype(BF)
    far = swap_bit(sent, MP, 2)
    grad_res_in, grad_res_out = call(
        residual_finish_kernel,
        [((3 * ch, hid), F32), ((hid, ch), F32)],
        [sent, swap_bit(sent, MP, 1), far, swap_bit(far, MP, 1)],
        scratch=[pltpu.VMEM((4,) + quarter, F32), pltpu.SemaphoreType.DMA((4 + ch // hid,))],
        where={4: pltpu.HBM, 5: pltpu.HBM},
    )

    down_out = ((2 * STRIDE * ch, width), F32)
    mine = tuple((k, None, k, True) for k in range(4))

    def finish(shifted, ins, written, projected, before=None):
        n = len(ins)
        aliased = before is not None
        return call(
            functools.partial(finish_kernel, shifted, n, written, projected),
            [down_out] + [((width, lat), F32)] * bool(projected),
            [*ins] + [before] * aliased,
            scratch=[
                pltpu.VMEM((len(written), ch, width), F32),
                pltpu.SemaphoreType.DMA((len(written),)),
            ],
            where={n: pltpu.HBM, n + aliased: pltpu.HBM},
            aliases={n: 0} if aliased else None,
        )

    (grad_down,) = finish(
        False, [*all_u, their_u], mine + tuple((4, k, k, False) for k in range(4)), ()
    )
    crossed = ((4, None, 0, False),)
    (grad_down,) = finish(True, [*all_s, first_s], mine + crossed, (), grad_down)
    last = tuple((5, k - 1, k, False) for k in range(1, 4))
    grad_down, grad_proj = finish(
        True, [*all_s, first_s, their_s], last, mine + crossed + last, grad_down
    )
    return (packed, grad_res_in, grad_res_out, grad_down, grad_proj)


def solution(mesh):
    return jax.shard_map(
        body,
        mesh=mesh,
        in_specs=(
            P(DP, None),
            P(DP),
            P(DP, None),
            P(),
            P(),
            P(None, MP),
            P(MP, None),
            P(DP, MP),
        ),
        out_specs=(P(DP, MP), P(), P(), P(None, MP), P(MP, None)),
        check_vma=False,
    )
```

```python
import functools
import jax
import jax.numpy as jnp
from jax import lax
from jax.experimental import pallas as pl
from jax.experimental.pallas import tpu as pltpu
from jax.sharding import PartitionSpec as P

STRIDE = 8
DP, MP = "dp", "mp"
LANES = 128
BF = jnp.bfloat16
F32 = jnp.float32
VMEM_LIMIT = 16 << 20


def elu(v):
    return jnp.where(v > 0, v, jnp.exp(jnp.minimum(v, 0.0)) - 1.0)


def slope(v):
    return jnp.where(v > 0, 1.0, jnp.exp(jnp.minimum(v, 0.0)))


def mm(a, b):
    return jnp.dot(a, b, preferred_element_type=F32)


def mm_nt(a, b):
    return lax.dot_general(a, b, (((1,), (1,)), ((), ())), preferred_element_type=F32)


def mm_tn(a, b):
    return lax.dot_general(a, b, (((0,), (0,)), ((), ())), preferred_element_type=F32)


def shift(v, s):
    n = v.shape[0]
    rows = lax.broadcasted_iota(jnp.int32, v.shape, 0)
    rolled = pltpu.roll(v, (-s) % n, 0)
    keep = rows < n - s if s > 0 else rows >= -s
    return jnp.where(keep, rolled, 0.0)


def spread(ref, value):
    for i in range(ref.shape[0]):
        ref[i] = value[:, i * LANES : (i + 1) * LANES]


def every(ref, start, size):
    return jnp.concatenate(
        [ref[i, pl.ds(start, size, stride=STRIDE), :] for i in range(ref.shape[0])], 1
    )


def call(kernel, outs, ins, scratch=(), flops=0, where=None, aliases=None):
    whole = pl.BlockSpec(memory_space=pltpu.VMEM)
    spaces = {i: pl.BlockSpec(memory_space=space) for i, space in (where or {}).items()}
    ins = [
        pltpu.with_memory_space_constraint(a, pltpu.HBM) if i in spaces else a
        for i, a in enumerate(ins)
    ]
    return pl.pallas_call(
        kernel,
        out_shape=[jax.ShapeDtypeStruct(s, d) for s, d in outs],
        in_specs=[spaces.get(i, whole) for i in range(len(ins))],
        out_specs=[spaces.get(len(ins) + i, whole) for i in range(len(outs))],
        scratch_shapes=list(scratch),
        input_output_aliases=aliases or {},
        compiler_params=pltpu.CompilerParams(vmem_limit_bytes=VMEM_LIMIT),
        cost_estimate=pl.CostEstimate(
            flops=flops, transcendentals=0, bytes_accessed=1 << 20
        ),
    )(*ins)


def position():
    m = lax.axis_index(MP)
    return lax.rem(m, 2), m // 2, lax.rem(lax.axis_index(DP), 2)


def masked(value, mask):
    wide = jnp.concatenate([mask[...]] * (value.shape[1] // mask.shape[1]), 1)
    return jnp.where(wide > 0, value, 0.0)


def depth():
    return lax.rem(lax.axis_index(DP) // 2, 4)


def forward_kernel(
    capacity, lengths_hbm, feat_hbm, routes_hbm, wi_hbm, wo_hbm,
    a1, a2, sec, ahid, shid, placing, mask, xs, ys, lengths, feat, routes, wi, wo, sems,
):
    frames, ch = a1.shape[1], a1.shape[2]
    hid = wo.shape[0]
    c, _, _ = position()
    rows = frames * STRIDE
    parts = feat.shape[0]
    size = rows // parts
    copies = [
        pltpu.make_async_copy(
            feat_hbm.at[pl.ds(pl.multiple_of(c * rows + i * size, size), size), :],
            feat.at[i],
            sems.at[i],
        )
        for i in range(parts)
    ]
    rest = [
        pltpu.make_async_copy(src, dst, sems.at[parts + i])
        for i, (src, dst) in enumerate(((routes_hbm, routes), (wi_hbm, wi), (wo_hbm, wo)))
    ]
    table = pltpu.make_async_copy(lengths_hbm, lengths, sems.at[parts + len(rest)])
    table.start()
    for copy in copies + rest:
        copy.start()
    table.wait()
    length = lengths[c]
    live = lax.broadcasted_iota(jnp.int32, (frames, ch), 0) < length
    mask[...] = jnp.where(live[:, : mask.shape[1]], 1.0, 0.0)
    for i in range(parts):
        copies[i].wait()
        value = feat[i].astype(F32)
        for k in range(xs.shape[0]):
            xs[k, i * size : (i + 1) * size] = value[:, k * LANES : (k + 1) * LANES]
    for copy in rest:
        copy.wait()
    placing[...] = placing_of(routes[...], placing.shape[0], capacity)
    wcat = jnp.concatenate([wi[k * ch : (k + 1) * ch, :] for k in range(3)], 1)

    def signal(p):
        return jnp.where(live, every(xs, p, frames), 0.0)

    for p in range(STRIDE):
        act = elu(signal(p)).astype(BF)
        a1[p] = act
        ys[p] = mm(act, wcat)
    for p in range(STRIDE):
        left = shift(ys[(p - 1) % STRIDE, :, :hid], -1 if p > 0 else -2)
        right = shift(ys[(p + 1) % STRIDE, :, 2 * hid :], 1 if p < STRIDE - 1 else 2)
        hidden = left + ys[p, :, hid : 2 * hid] + right
        act_hid = elu(hidden).astype(BF)
        ahid[p] = act_hid
        shid[p] = slope(hidden).astype(BF)
        section = jnp.where(live, signal(p) + mm(act_hid, wo[...]), 0.0).astype(BF)
        sec[p] = section
        a2[p] = elu(section.astype(F32)).astype(BF)


def down_kernel(
    mask, a2, dwa, dwb, pa, pb, adown, sdown, lat_send, lat_keep, ls,
):
    frames, ch = a2.shape[1], a2.shape[2]
    _, y, _ = position()
    half = STRIDE // 2

    def tap(k):
        return jnp.concatenate([dwa[k * ch : (k + 1) * ch, :], dwb[k * ch : (k + 1) * ch, :]], 1)

    down = jnp.zeros((frames, 2 * dwa.shape[1]), F32)
    before = jnp.zeros_like(down)
    after = jnp.zeros_like(down)
    for p in range(STRIDE):
        act = a2[p]
        down = down + mm(act, tap(p + half))
        if p < half:
            after = after + mm(act, tap(p + 3 * half))
        else:
            before = before + mm(act, tap(p - half))
    down = down + shift(before, -1) + shift(after, 1)
    act_down = elu(down).astype(BF)
    adown[...] = act_down
    sdown[...] = slope(down)
    proj = jnp.concatenate([pa[...], pb[...]], 0)
    lat = proj.shape[1]
    spread(ls, masked(mm(act_down, proj), mask))
    pieces = frames // STRIDE
    for j in range(half):
        cols = slice(j * lat, (j + 1) * lat)
        lat_send[:, cols] = every(ls, half * (1 - y) + j, pieces).astype(BF)
        lat_keep[:, cols] = every(ls, half * y + j, pieces).astype(BF)


def placing_of(targets, slots, capacity):
    pieces = targets.shape[1]
    chosen = jnp.where(targets == lax.broadcasted_iota(jnp.int32, (128, pieces), 0), 1.0, 0.0)
    upper = (
        lax.broadcasted_iota(jnp.int32, (pieces, pieces), 0)
        < lax.broadcasted_iota(jnp.int32, (pieces, pieces), 1)
    )
    earlier = mm(chosen.astype(BF), jnp.where(upper, 1.0, 0.0).astype(BF))
    rank = jnp.sum(earlier * chosen, axis=0, keepdims=True).astype(jnp.int32)
    slot = targets * capacity + rank
    ids = lax.broadcasted_iota(jnp.int32, (slots, pieces), 0)
    return jnp.where(slot == ids, 1.0, 0.0).astype(BF)


def parts_kernel(whole, *refs):
    *outs, sems = refs
    z = depth()
    copies = [
        pltpu.make_async_copy(whole.at[z ^ k], out, sems.at[k]) for k, out in enumerate(outs)
    ]
    for copy in copies:
        copy.start()
    for copy in copies:
        copy.wait()


def columns_kernel(*refs):
    *parts, send, keep = refs
    _, _, x = position()
    for k, part in enumerate(parts):
        send[k] = part[1 - x]
        keep[k] = part[x]


def assemble(keep, recv, out):
    _, _, x = position()
    z = depth()
    size = keep.shape[1]
    for k in range(keep.shape[0]):
        for part, column in ((keep, x), (recv, 1 - x)):
            at = (2 * (z ^ k) + column) * size
            out[pl.ds(pl.multiple_of(at, size), size), :] = part[k]


def pick_kernel(placing, *refs):
    *parts, own, other, rows, buf = refs
    c, _, _ = position()
    cols = parts[0].shape[-1]
    for i in range(2):
        if len(parts) == 2:
            rows[...] = parts[i][...]
        else:
            assemble(parts[2 * i], parts[2 * i + 1], rows)
        buf[:, i * cols : (i + 1) * cols] = mm_tn(placing[...], rows[...])
    half = own.shape[0]
    own[...] = buf[pl.ds(pl.multiple_of(c * half, half), half), :].astype(BF)
    other[...] = buf[pl.ds(pl.multiple_of((1 - c) * half, half), half), :].astype(BF)


def place_kernel(placing, mine, theirs, outgoing, buf):
    c, _, _ = position()
    half = mine.shape[0]
    buf[pl.ds(pl.multiple_of(c * half, half), half), :] = mine[...].astype(F32)
    buf[pl.ds(pl.multiple_of((1 - c) * half, half), half), :] = theirs[...].astype(F32)
    outgoing[...] = mm(placing[...], buf[...].astype(BF)).astype(BF)


def place_parts_kernel(placing, mine, theirs, *refs):
    *outs, buf, rows = refs
    place_kernel(placing, mine, theirs, rows, buf)
    z = depth()
    _, columns, size, _ = (1,) + outs[0].shape
    for k, out in enumerate(outs):
        for i in range(columns):
            at = ((z ^ k) * columns + i) * size
            out[i] = rows[pl.ds(pl.multiple_of(at, size), size), :]


def packed_kernel(keep, recv, out):
    assemble(keep, recv, out)


def lat_mix_kernel(lat_keep, lat_y, mine, theirs):
    c, _, _ = position()
    total = (lat_keep[...].astype(F32) + lat_y[...].astype(F32)).astype(BF)
    cols = mine.shape[1]
    mine[...] = jnp.where(c == 0, total[:, :cols], total[:, cols:])
    theirs[...] = jnp.where(c == 0, total[:, cols:], total[:, :cols])


def section_grad(gd, gshift, wa, wb, part, j, ch):
    half = STRIDE // 2
    first = part * half + j + half
    second = jnp.where(part == 0, 3 * half + j, j)
    rows1 = pl.ds(pl.multiple_of(first * ch, ch), ch)
    rows2 = pl.ds(pl.multiple_of(second * ch, ch), ch)
    w1 = jnp.concatenate([wa[rows1, :], wb[rows1, :]], 1)
    w2 = jnp.concatenate([wa[rows2, :], wb[rows2, :]], 1)
    return mm_nt(gd, w1) + mm_nt(gshift, w2)


def moved(gd, part):
    g = gd.astype(F32)
    return jnp.where(part == 0, shift(g, -1), shift(g, 1)).astype(BF)


def latent_grad_kernel(
    mask, g_own, g_core, adown, sdown, pa, pb,
    gd_out, swap, gproj_keep, gl,
):
    frames = adown.shape[0]
    width, lat = pa.shape
    pieces = g_own.shape[0]
    c, y, _ = position()
    side = 2 * lat
    blocks = (
        (g_own.at[:, :side], 2 * y + c),
        (g_own.at[:, side:], 2 * (1 - y) + c),
        (g_core.at[:, :side], 2 * y + 1 - c),
        (g_core.at[:, side:], 2 * (1 - y) + 1 - c),
    )
    for block, owner in blocks:
        for j in range(2):
            for i in range(gl.shape[0]):
                at = j * lat + i * LANES
                gl[i, pl.ds(2 * owner + j, pieces, stride=STRIDE), :] = block[
                    :, at : at + LANES
                ].astype(F32)
    g_latent = masked(jnp.concatenate([gl[i] for i in range(gl.shape[0])], 1), mask).astype(BF)
    proj = jnp.concatenate([pa[...], pb[...]], 0)
    gd = (mm_nt(g_latent, proj) * sdown[...]).astype(BF)
    gd_out[...] = gd
    swap[:frames] = gd[:, width:]
    gproj = mm_tn(adown[...], g_latent)
    swap[frames : frames + width] = gproj[width:, :width].astype(BF)
    swap[frames + width :] = gproj[width:, width:].astype(BF)
    gproj_keep[:width] = gproj[:width, :width]
    gproj_keep[width:] = gproj[:width, width:]


def section_send_kernel(gd, dwa, dwb, send):
    _, y, _ = position()
    full = gd[...]
    g2 = moved(full, 1 - y)
    for j in range(STRIDE // 2):
        send[j] = section_grad(full, g2, dwa, dwb, 1 - y, j, send.shape[2]).astype(BF)


def section_keep_kernel(gd, dwa, dwb, keep):
    _, y, _ = position()
    full = gd[...]
    g2 = moved(full, y)
    for j in range(STRIDE // 2):
        keep[j] = section_grad(full, g2, dwa, dwb, y, j, keep.shape[2])


def weight_grads(a2a, a2b, ga, gb, part, j):
    half = STRIDE // 2
    p = part * half + j
    return mm_tn(a2a[p], ga) + mm_tn(a2b[p], gb)


def pair(g, part):
    return jnp.concatenate([g, moved(g, part)], 1)


def down_send_kernel(a2a, a2b, gd, swap, gproj, send_u, send_s):
    frames = gd.shape[0]
    width = swap.shape[1]
    _, _, x = position()
    ga = pair(gd[:, :width], x)
    gb = pair(swap[:frames], x)
    extra = send_s.shape[1] - send_u.shape[1]
    rows = send_u.shape[1]
    for j in range(STRIDE // 2):
        w = weight_grads(a2a, a2b, ga, gb, x, j)
        send_u[j] = w[:, :width].astype(BF)
        send_s[j, :rows] = w[:, width:].astype(BF)
        at = pl.ds(pl.multiple_of(((1 - x) * 4 + j) * extra, extra), extra)
        send_s[j, rows:] = (gproj[at, :] + swap[pl.ds(pl.multiple_of(frames + ((1 - x) * 4 + j) * extra, extra), extra), :].astype(F32)).astype(BF)


def down_keep_kernel(a2a, a2b, gd, swap, gproj, keep_u, keep_s):
    frames = gd.shape[0]
    width = swap.shape[1]
    _, _, x = position()
    part = 1 - x
    ga = pair(gd[:, :width], part)
    gb = pair(swap[:frames], part)
    extra = keep_s.shape[1] - keep_u.shape[1]
    rows = keep_u.shape[1]
    for j in range(STRIDE // 2):
        w = weight_grads(a2a, a2b, ga, gb, part, j)
        keep_u[j] = w[:, :width]
        keep_s[j, :rows] = w[:, width:]
        at = pl.ds(pl.multiple_of((x * 4 + j) * extra, extra), extra)
        keep_s[j, rows:] = gproj[at, :] + swap[pl.ds(pl.multiple_of(frames + (x * 4 + j) * extra, extra), extra), :].astype(F32)


def residual_kernel(
    mask, keep, recv, sec, ahid, shid, wo, a1, kept, send1, send2, send3, gh, buf,
):
    half = STRIDE // 2
    ch = keep.shape[2]
    hid = wo.shape[0]
    c, y, _ = position()
    g_out = jnp.zeros((hid, ch), F32)
    for j in range(half):
        g = keep[j] + recv[j].astype(F32)
        g_branch = masked(g * slope(sec[y * half + j].astype(F32)), mask).astype(BF)
        g_out = g_out + mm_tn(ahid[y * half + j], g_branch)
        gh[j] = mm_nt(g_branch, wo[...]) * shid[y * half + j].astype(F32)
    taps = [jnp.zeros((ch, hid), F32) for _ in range(3)]
    for j in range(half):
        g = gh[j]
        p = y * half + j
        here = g.astype(BF)
        taps[1] = taps[1] + mm_tn(a1[p], here)
        down1 = shift(g, 1)
        up1 = shift(g, -1)
        if j == 0:
            down1 = jnp.where(y == 0, shift(g, 2), down1)
        if j == half - 1:
            up1 = jnp.where(y == 1, shift(g, -2), up1)
        taps[0] = taps[0] + mm_tn(a1[lax.rem(p + STRIDE - 1, STRIDE)], down1.astype(BF))
        taps[2] = taps[2] + mm_tn(a1[lax.rem(p + 1, STRIDE)], up1.astype(BF))
    for k in range(3):
        for i in range(ch // hid):
            buf[k * (ch // hid) + i] = taps[k][i * hid : (i + 1) * hid]
    for i in range(ch // hid):
        buf[3 * (ch // hid) + i] = g_out[:, i * hid : (i + 1) * hid]
    m = 2 * y + c
    n = buf.shape[0] // 4
    for i in range(n):
        at = slice(i * hid, (i + 1) * hid)
        kept[at] = buf[m * n + i]
        for k, out in enumerate((send1, send2, send3)):
            out[at] = buf[(m ^ (k + 1)) * n + i].astype(BF)


def residual_finish_kernel(r0, r1, r2, r3, out_in, out_out, buf):
    c, y, _ = position()
    m = 2 * y + c
    rows, hid = r0.shape
    for k, r in enumerate((r0, r1, r2, r3)):
        buf[m ^ k] = r[...].astype(F32)
    for q in range(3):
        out_in[q * rows : (q + 1) * rows] = buf[q]
    for i in range(rows // hid):
        out_out[:, i * hid : (i + 1) * hid] = buf[3, i * hid : (i + 1) * hid]


def sum_kernel(keep, recv, own, *sends):
    z = depth()
    own[...] = keep[z] + recv[z].astype(F32)
    for k, out in enumerate(sends):
        at = z ^ (k + 1)
        out[...] = (keep[at] + recv[at].astype(F32)).astype(BF)


def swap_bit(value, axis, bit):
    n = lax.axis_size(axis)
    return lax.ppermute(value, axis, [(i, i ^ bit) for i in range(n)])


def stages_of(n):
    found, bit = [], 2
    while bit < n:
        members = 4 if n // bit >= 4 else 2
        found.append((bit, members))
        bit *= members
    return found


def pick(stack, index):
    return lax.dynamic_index_in_dim(stack, index, 0, keepdims=False)


def fan(values, axis, bit):
    return [swap_bit(v, axis, bit * (k + 1)) for k, v in enumerate(values)]


def plus(total, received):
    for r in received:
        total = total + r.astype(F32)
    return total


def reduce_rest(kept, received, me, stages):
    shape = kept.shape[1:]
    own, *sends = call(sum_kernel, [(shape, F32)] + [(shape, BF)] * 3, [kept, received])
    received = fan(sends, DP, stages[0][0])
    for bit, members in stages[1:]:
        parts = plus(own, received).reshape(members, -1, own.shape[-1])
        place = (me // bit) % members
        sends = [pick(parts, place ^ k).astype(BF) for k in range(1, members)]
        own, received = pick(parts, place), fan(sends, DP, bit)
    return plus(own, received).astype(BF)


def gather_high(own, me, stages):
    for bit, members in reversed(stages[1:]):
        place = (me // bit) % members
        blocks = [own] + fan([own] * (members - 1), DP, bit)
        ordered = jnp.stack(blocks)
        own = jnp.concatenate([pick(ordered, place ^ k) for k in range(members)], 0)
    return own


def finish_kernel(shifted, count, written, projected, *refs):
    ins, rest = refs[:count], refs[count:]
    if projected:
        *_, out, out_proj, buf, sems = rest
    else:
        *_, out, buf, sems = rest
    _, _, x = position()
    z = depth()
    half = STRIDE // 2
    rows = buf.shape[1]

    def block(entry):
        operand, lead, k, own = entry
        ref = ins[operand]
        value = ref if lead is None else ref.at[lead]
        part, xp = (1 - x, x) if own else (x, 1 - x)
        return value, z ^ k, part, xp

    copies = []
    for n, entry in enumerate(written):
        value, j, part, _ = block(entry)
        tap = part * half + j + half
        if shifted:
            tap = jnp.where(part == 0, 3 * half + j, j)
        buf[n] = value[:rows].astype(F32)
        copy = pltpu.make_async_copy(
            buf.at[n], out.at[pl.ds(pl.multiple_of(tap * rows, rows), rows), :], sems.at[n]
        )
        copy.start()
        copies.append(copy)
    for entry in projected:
        value, j, _, xp = block(entry)
        per = out_proj.shape[0] * 2 // STRIDE
        where = pl.ds(pl.multiple_of(j * per, per), per)
        width = value.shape[1]
        extra = value[rows : rows + per].astype(F32)

        @pl.when(xp == 0)
        def _():
            out_proj[where, :width] = extra

        @pl.when(xp == 1)
        def _():
            out_proj[where, width:] = extra

    for copy in copies:
        copy.wait()


def body(
    features, lengths, routes, res_in_weight, res_out_weight, down_weight, proj_weight, cotangent
):
    utts = lengths.shape[0]
    total_rows = features.shape[0] // utts
    ch = features.shape[1]
    frames = total_rows // STRIDE
    hid = res_out_weight.shape[0]
    width = down_weight.shape[1]
    lat = proj_weight.shape[1]
    dp_count, mp_count = lax.axis_size(DP), lax.axis_size(MP)
    pieces = routes.shape[0]
    half_pieces = pieces // utts
    capacity = 2 * pieces // dp_count
    slots = dp_count * capacity
    cols = cotangent.shape[1]
    half = STRIDE // 2
    me_dp = lax.axis_index(DP)
    stages = stages_of(dp_count)
    staged = dp_count == 8
    lane_block = ((dp_count // 2, capacity, cols), BF)
    pair_block = ((2, capacity, cols), BF)

    def columns(parts):
        received = fan(parts[1:], DP, 2)
        return call(columns_kernel, [lane_block] * 2, [parts[0], *received])

    def all_to_all(value):
        return lax.all_to_all(
            value.reshape(dp_count, capacity, cols), DP, split_axis=0, concat_axis=0
        ).reshape(slots, cols)

    other_down = swap_bit(down_weight, MP, 1)
    other_proj = swap_bit(proj_weight, MP, 1)
    if staged:
        parts = call(
            parts_kernel,
            [pair_block] * 4,
            [cotangent.reshape(dp_count // 2, 2, capacity, cols)],
            scratch=[pltpu.SemaphoreType.DMA((4,))],
            where={0: pltpu.HBM},
        )
        send, keep = columns(parts)
        both_axes = [(i, i ^ (mp_count + 2)) for i in range(dp_count * mp_count)]
        far = lax.ppermute(send, (DP, MP), both_axes)
        across = swap_bit(send, DP, 1)
        returned = [keep, across, swap_bit(keep, MP, 2), far]
    else:
        direct = all_to_all(cotangent)
        returned = [direct, swap_bit(direct, MP, 2)]

    loads = 4
    a1, a2, sec, ahid, shid, placing, mask = call(
        functools.partial(forward_kernel, capacity),
        [
            ((STRIDE, frames, ch), BF),
            ((STRIDE, frames, ch), BF),
            ((STRIDE, frames, ch), BF),
            ((STRIDE, frames, hid), BF),
            ((STRIDE, frames, hid), BF),
            ((slots, pieces), BF),
            ((frames, LANES), F32),
        ],
        [lengths, features, routes.reshape(1, pieces), res_in_weight, res_out_weight],
        scratch=[
            pltpu.VMEM((ch // LANES, total_rows, LANES), F32),
            pltpu.VMEM((STRIDE, frames, 3 * hid), F32),
            pltpu.SMEM(lengths.shape, lengths.dtype),
            pltpu.VMEM((loads, total_rows // loads, ch), BF),
            pltpu.VMEM((1, pieces), routes.dtype),
            pltpu.VMEM(res_in_weight.shape, BF),
            pltpu.VMEM(res_out_weight.shape, BF),
            pltpu.SemaphoreType.DMA((loads + 4,)),
        ],
        where={i: pltpu.HBM for i in range(5)},
        flops=4 << 30,
    )
    other_a2 = swap_bit(a2, MP, 1)
    adown, sdown, lat_send, lat_keep = call(
        down_kernel,
        [
            ((frames, 2 * width), BF),
            ((frames, 2 * width), F32),
            ((half_pieces, half * lat), BF),
            ((half_pieces, half * lat), BF),
        ],
        [mask, a2, down_weight, other_down, proj_weight, other_proj],
        scratch=[pltpu.VMEM((lat // LANES, frames, LANES), F32)],
        flops=1 << 30,
    )
    lat_y = swap_bit(lat_send, MP, 2)

    g_own, g_other = call(
        pick_kernel,
        [((half_pieces, 2 * cols), BF)] * 2,
        [placing, *returned],
        scratch=[pltpu.VMEM((slots, cols), BF), pltpu.VMEM((pieces, 2 * cols), F32)],
    )
    g_core = swap_bit(g_other, MP, 1)

    mine, theirs = call(
        lat_mix_kernel, [((half_pieces, cols), BF)] * 2, [lat_keep, lat_y]
    )
    theirs = swap_bit(theirs, MP, 1)

    gd, swap, gproj = call(
        latent_grad_kernel,
        [
            ((frames, 2 * width), BF),
            ((frames + 2 * width, width), BF),
            ((2 * width, lat // 2), F32),
        ],
        [mask, g_own, g_core, adown, sdown, proj_weight, other_proj],
        scratch=[pltpu.VMEM((lat // LANES, frames, LANES), F32)],
        flops=1 << 30,
    )
    got = swap_bit(swap, MP, 1)
    (g_send,) = call(
        section_send_kernel,
        [((half, frames, ch), BF)],
        [gd, down_weight, other_down],
        flops=1 << 29,
    )
    g_recv = swap_bit(g_send, MP, 2)
    extra = 2 * width // STRIDE
    send_u, send_s = call(
        down_send_kernel,
        [((half, ch, width), BF), ((half, ch + extra, width), BF)],
        [a2, other_a2, gd, got, gproj],
        flops=1 << 29,
    )
    recv_u = swap_bit(send_u, DP, 1)
    recv_s = swap_bit(send_s, DP, 1)
    keep_u, keep_s = call(
        down_keep_kernel,
        [((half, ch, width), F32), ((half, ch + extra, width), F32)],
        [a2, other_a2, gd, got, gproj],
        flops=1 << 29,
    )
    (keep_g,) = call(
        section_keep_kernel,
        [((half, frames, ch), F32)],
        [gd, down_weight, other_down],
        flops=1 << 29,
    )

    row_scratch = pltpu.VMEM((pieces, cols), F32)
    if staged:
        parts = call(
            place_parts_kernel,
            [pair_block] * 4,
            [placing, mine, theirs],
            scratch=[row_scratch, pltpu.VMEM((slots, cols), BF)],
        )
        send, keep = columns(parts)
        (packed,) = call(packed_kernel, [((slots, cols), BF)], [keep, swap_bit(send, DP, 1)])
    else:
        (outgoing,) = call(
            place_kernel,
            [((slots, cols), BF)],
            [placing, mine, theirs],
            scratch=[row_scratch],
        )
        packed = all_to_all(outgoing)

    blocks = 4 * (ch // hid)
    quarter = (blocks // 4 * hid, hid)
    e_own, *e_sends = call(
        residual_kernel,
        [(quarter, F32)] + [(quarter, BF)] * 3,
        [mask, keep_g, g_recv, sec, ahid, shid, res_out_weight, a1],
        scratch=[pltpu.VMEM((half, frames, hid), F32), pltpu.VMEM((blocks, hid, hid), F32)],
        flops=1 << 30,
    )
    received = fan(e_sends, MP, 1)
    e_own = plus(e_own, received)
    sent = e_own.astype(BF)

    own_u = gather_high(reduce_rest(keep_u, recv_u, me_dp, stages), me_dp, stages)
    own_s = gather_high(reduce_rest(keep_s, recv_s, me_dp, stages), me_dp, stages)
    all_u = [own_u] + fan([own_u] * 3, DP, stages[0][0])
    both = jnp.concatenate([own_s, sent])
    first_s = swap_bit(both, DP, 1)
    all_s = [own_s] + fan([own_s] * 3, DP, stages[0][0])
    their_u = swap_bit(jnp.stack(all_u), DP, 1)
    their_s = swap_bit(jnp.stack(all_s[1:]), DP, 1)
    received = [first_s[own_s.shape[0] :]]
    for bit, members in stages:
        e_own = plus(e_own, received)
        sent = e_own.astype(BF)
        received = fan([sent] * (members - 1), DP, bit)
    sent = plus(e_own, received).astype(BF)
    grad_res_in, grad_res_out = call(
        residual_finish_kernel,
        [((3 * ch, hid), F32), ((hid, ch), F32)],
        [sent, *fan([sent] * 3, MP, 1)],
        scratch=[pltpu.VMEM((4,) + quarter, F32)],
    )

    down_out = ((2 * STRIDE * ch, width), F32)
    mine = tuple((k, None, k, True) for k in range(4))

    def finish(shifted, ins, written, projected, before=None):
        n = len(ins)
        aliased = before is not None
        return call(
            functools.partial(finish_kernel, shifted, n, written, projected),
            [down_out] + [((width, lat), F32)] * bool(projected),
            [*ins] + [before] * aliased,
            scratch=[
                pltpu.VMEM((len(written), ch, width), F32),
                pltpu.SemaphoreType.DMA((len(written),)),
            ],
            where={n: pltpu.HBM, n + aliased: pltpu.HBM},
            aliases={n: 0} if aliased else None,
        )

    (grad_down,) = finish(
        False, [*all_u, their_u], mine + tuple((4, k, k, False) for k in range(4)), ()
    )
    crossed = ((4, None, 0, False),)
    (grad_down,) = finish(True, [*all_s, first_s], mine + crossed, (), grad_down)
    last = tuple((5, k - 1, k, False) for k in range(1, 4))
    grad_down, grad_proj = finish(
        True, [*all_s, first_s, their_s], last, mine + crossed + last, grad_down
    )
    return (packed, grad_res_in, grad_res_out, grad_down, grad_proj)


def solution(mesh):
    return jax.shard_map(
        body,
        mesh=mesh,
        in_specs=(
            P(DP, None),
            P(DP),
            P(DP, None),
            P(),
            P(),
            P(None, MP),
            P(MP, None),
            P(DP, MP),
        ),
        out_specs=(P(DP, MP), P(), P(), P(None, MP), P(MP, None)),
        check_vma=False,
    )
```

```python
import functools
import jax
import jax.numpy as jnp
from jax import lax
from jax.experimental import pallas as pl
from jax.experimental.pallas import tpu as pltpu
from jax.sharding import PartitionSpec as P

STRIDE = 8
DP, MP = "dp", "mp"
LANES = 128
BF = jnp.bfloat16
F32 = jnp.float32
VMEM_LIMIT = 16 << 20


def elu(v):
    return jnp.where(v > 0, v, jnp.exp(jnp.minimum(v, 0.0)) - 1.0)


def slope(v):
    return jnp.where(v > 0, 1.0, jnp.exp(jnp.minimum(v, 0.0)))


def mm(a, b):
    return jnp.dot(a, b, preferred_element_type=F32)


def mm_nt(a, b):
    return lax.dot_general(a, b, (((1,), (1,)), ((), ())), preferred_element_type=F32)


def mm_tn(a, b):
    return lax.dot_general(a, b, (((0,), (0,)), ((), ())), preferred_element_type=F32)


def shift(v, s):
    n = v.shape[0]
    rows = lax.broadcasted_iota(jnp.int32, v.shape, 0)
    rolled = pltpu.roll(v, (-s) % n, 0)
    keep = rows < n - s if s > 0 else rows >= -s
    return jnp.where(keep, rolled, 0.0)


def spread(ref, value):
    for i in range(ref.shape[0]):
        ref[i] = value[:, i * LANES : (i + 1) * LANES]


def every(ref, start, size):
    return jnp.concatenate(
        [ref[i, pl.ds(start, size, stride=STRIDE), :] for i in range(ref.shape[0])], 1
    )


def call(kernel, outs, ins, scratch=(), flops=0, where=None, aliases=None):
    whole = pl.BlockSpec(memory_space=pltpu.VMEM)
    spaces = {i: pl.BlockSpec(memory_space=space) for i, space in (where or {}).items()}
    ins = [
        pltpu.with_memory_space_constraint(a, pltpu.HBM) if i in spaces else a
        for i, a in enumerate(ins)
    ]
    return pl.pallas_call(
        kernel,
        out_shape=[jax.ShapeDtypeStruct(s, d) for s, d in outs],
        in_specs=[spaces.get(i, whole) for i in range(len(ins))],
        out_specs=[spaces.get(len(ins) + i, whole) for i in range(len(outs))],
        scratch_shapes=list(scratch),
        input_output_aliases=aliases or {},
        compiler_params=pltpu.CompilerParams(vmem_limit_bytes=VMEM_LIMIT),
        cost_estimate=pl.CostEstimate(
            flops=flops, transcendentals=0, bytes_accessed=1 << 20
        ),
    )(*ins)


def position():
    m = lax.axis_index(MP)
    return lax.rem(m, 2), m // 2, lax.rem(lax.axis_index(DP), 2)


def masked(value, mask):
    wide = jnp.concatenate([mask[...]] * (value.shape[1] // mask.shape[1]), 1)
    return jnp.where(wide > 0, value, 0.0)


def depth():
    return lax.rem(lax.axis_index(DP) // 2, 4)


def forward_kernel(
    capacity, lengths_hbm, feat_hbm, routes_hbm, wi_hbm, wo_hbm,
    a1, a2, sec, ahid, shid, placing, mask, xs, ys, lengths, feat, routes, wi, wo, sems,
):
    frames, ch = a1.shape[1], a1.shape[2]
    hid = wo.shape[0]
    c, _, _ = position()
    rows = frames * STRIDE
    parts = feat.shape[0]
    size = rows // parts
    copies = [
        pltpu.make_async_copy(
            feat_hbm.at[pl.ds(pl.multiple_of(c * rows + i * size, size), size), :],
            feat.at[i],
            sems.at[i],
        )
        for i in range(parts)
    ]
    rest = [
        pltpu.make_async_copy(src, dst, sems.at[parts + i])
        for i, (src, dst) in enumerate(((routes_hbm, routes), (wi_hbm, wi), (wo_hbm, wo)))
    ]
    table = pltpu.make_async_copy(lengths_hbm, lengths, sems.at[parts + len(rest)])
    table.start()
    for copy in copies + rest:
        copy.start()
    table.wait()
    length = lengths[c]
    live = lax.broadcasted_iota(jnp.int32, (frames, ch), 0) < length
    mask[...] = jnp.where(live[:, : mask.shape[1]], 1.0, 0.0)
    for i in range(parts):
        copies[i].wait()
        value = feat[i].astype(F32)
        for k in range(xs.shape[0]):
            xs[k, i * size : (i + 1) * size] = value[:, k * LANES : (k + 1) * LANES]
    for copy in rest:
        copy.wait()
    placing[...] = placing_of(routes[...], placing.shape[0], capacity)
    wcat = jnp.concatenate([wi[k * ch : (k + 1) * ch, :] for k in range(3)], 1)

    def signal(p):
        return jnp.where(live, every(xs, p, frames), 0.0)

    for p in range(STRIDE):
        act = elu(signal(p)).astype(BF)
        a1[p] = act
        ys[p] = mm(act, wcat)
    for p in range(STRIDE):
        left = shift(ys[(p - 1) % STRIDE, :, :hid], -1 if p > 0 else -2)
        right = shift(ys[(p + 1) % STRIDE, :, 2 * hid :], 1 if p < STRIDE - 1 else 2)
        hidden = left + ys[p, :, hid : 2 * hid] + right
        act_hid = elu(hidden).astype(BF)
        ahid[p] = act_hid
        shid[p] = slope(hidden).astype(BF)
        section = jnp.where(live, signal(p) + mm(act_hid, wo[...]), 0.0).astype(BF)
        sec[p] = section
        a2[p] = elu(section.astype(F32)).astype(BF)


def down_kernel(
    mask, a2, dwa, dwb, pa, pb, adown, sdown, lat_send, lat_keep, ls,
):
    frames, ch = a2.shape[1], a2.shape[2]
    _, y, _ = position()
    half = STRIDE // 2

    def tap(k):
        return jnp.concatenate([dwa[k * ch : (k + 1) * ch, :], dwb[k * ch : (k + 1) * ch, :]], 1)

    down = jnp.zeros((frames, 2 * dwa.shape[1]), F32)
    before = jnp.zeros_like(down)
    after = jnp.zeros_like(down)
    for p in range(STRIDE):
        act = a2[p]
        down = down + mm(act, tap(p + half))
        if p < half:
            after = after + mm(act, tap(p + 3 * half))
        else:
            before = before + mm(act, tap(p - half))
    down = down + shift(before, -1) + shift(after, 1)
    act_down = elu(down).astype(BF)
    adown[...] = act_down
    sdown[...] = slope(down)
    proj = jnp.concatenate([pa[...], pb[...]], 0)
    lat = proj.shape[1]
    spread(ls, masked(mm(act_down, proj), mask))
    pieces = frames // STRIDE
    for j in range(half):
        cols = slice(j * lat, (j + 1) * lat)
        lat_send[:, cols] = every(ls, half * (1 - y) + j, pieces).astype(BF)
        lat_keep[:, cols] = every(ls, half * y + j, pieces).astype(BF)


def placing_of(targets, slots, capacity):
    pieces = targets.shape[1]
    chosen = jnp.where(targets == lax.broadcasted_iota(jnp.int32, (128, pieces), 0), 1.0, 0.0)
    upper = (
        lax.broadcasted_iota(jnp.int32, (pieces, pieces), 0)
        < lax.broadcasted_iota(jnp.int32, (pieces, pieces), 1)
    )
    earlier = mm(chosen.astype(BF), jnp.where(upper, 1.0, 0.0).astype(BF))
    rank = jnp.sum(earlier * chosen, axis=0, keepdims=True).astype(jnp.int32)
    slot = targets * capacity + rank
    ids = lax.broadcasted_iota(jnp.int32, (slots, pieces), 0)
    return jnp.where(slot == ids, 1.0, 0.0).astype(BF)


def parts_kernel(whole, *refs):
    *outs, sems = refs
    z = depth()
    copies = [
        pltpu.make_async_copy(whole.at[z ^ k], out, sems.at[k]) for k, out in enumerate(outs)
    ]
    for copy in copies:
        copy.start()
    for copy in copies:
        copy.wait()


def columns_kernel(*refs):
    *parts, send, keep = refs
    _, _, x = position()
    for k, part in enumerate(parts):
        send[k] = part[1 - x]
        keep[k] = part[x]


def assemble(keep, recv, out):
    _, _, x = position()
    z = depth()
    size = keep.shape[1]
    for k in range(keep.shape[0]):
        for part, column in ((keep, x), (recv, 1 - x)):
            at = (2 * (z ^ k) + column) * size
            out[pl.ds(pl.multiple_of(at, size), size), :] = part[k]


def pick_kernel(placing, *refs):
    *parts, own, other, rows, buf = refs
    c, _, _ = position()
    cols = parts[0].shape[-1]
    for i in range(2):
        if len(parts) == 2:
            rows[...] = parts[i][...]
        else:
            assemble(parts[2 * i], parts[2 * i + 1], rows)
        buf[:, i * cols : (i + 1) * cols] = mm_tn(placing[...], rows[...])
    half = own.shape[0]
    own[...] = buf[pl.ds(pl.multiple_of(c * half, half), half), :].astype(BF)
    other[...] = buf[pl.ds(pl.multiple_of((1 - c) * half, half), half), :].astype(BF)


def place_kernel(placing, mine, theirs, outgoing, buf):
    c, _, _ = position()
    half = mine.shape[0]
    buf[pl.ds(pl.multiple_of(c * half, half), half), :] = mine[...].astype(F32)
    buf[pl.ds(pl.multiple_of((1 - c) * half, half), half), :] = theirs[...].astype(F32)
    outgoing[...] = mm(placing[...], buf[...].astype(BF)).astype(BF)


def place_parts_kernel(placing, mine, theirs, *refs):
    *outs, buf, rows = refs
    place_kernel(placing, mine, theirs, rows, buf)
    z = depth()
    _, columns, size, _ = (1,) + outs[0].shape
    for k, out in enumerate(outs):
        for i in range(columns):
            at = ((z ^ k) * columns + i) * size
            out[i] = rows[pl.ds(pl.multiple_of(at, size), size), :]


def flat_columns_kernel(*refs):
    *parts, send, keep = refs
    _, _, x = position()
    size, cols = keep.shape[1:]
    groups = cols // LANES
    for k, part in enumerate(parts):
        value = part[1 - x]
        for q in range(groups):
            at = (k * groups + q) * size
            send[at : at + size] = value[:, q * LANES : (q + 1) * LANES]
        keep[k] = part[x]


def packed_kernel(base, keep, recv, out):
    _, _, x = position()
    z = depth()
    members, size, cols = keep.shape
    groups = cols // LANES
    for k in range(members):
        own = pl.ds(pl.multiple_of((2 * (z ^ k) + x) * size, size), size)
        other = pl.ds(pl.multiple_of((2 * (z ^ k) + 1 - x) * size, size), size)
        out[own, :] = keep[k]
        for q in range(groups):
            at = base + (k * groups + q) * size
            out[other, q * LANES : (q + 1) * LANES] = recv[at : at + size]


def lat_mix_kernel(lat_keep, lat_y, mine, theirs):
    c, _, _ = position()
    total = (lat_keep[...].astype(F32) + lat_y[...].astype(F32)).astype(BF)
    cols = mine.shape[1]
    mine[...] = jnp.where(c == 0, total[:, :cols], total[:, cols:])
    theirs[...] = jnp.where(c == 0, total[:, cols:], total[:, :cols])


def section_grad(gd, gshift, wa, wb, part, j, ch):
    half = STRIDE // 2
    first = part * half + j + half
    second = jnp.where(part == 0, 3 * half + j, j)
    rows1 = pl.ds(pl.multiple_of(first * ch, ch), ch)
    rows2 = pl.ds(pl.multiple_of(second * ch, ch), ch)
    w1 = jnp.concatenate([wa[rows1, :], wb[rows1, :]], 1)
    w2 = jnp.concatenate([wa[rows2, :], wb[rows2, :]], 1)
    return mm_nt(gd, w1) + mm_nt(gshift, w2)


def moved(gd, part):
    g = gd.astype(F32)
    return jnp.where(part == 0, shift(g, -1), shift(g, 1)).astype(BF)


def latent_grad_kernel(
    mask, g_own, g_core, adown, sdown, pa, pb,
    gd_out, swap, gproj_keep, gl,
):
    frames = adown.shape[0]
    width, lat = pa.shape
    pieces = g_own.shape[0]
    c, y, _ = position()
    side = 2 * lat
    blocks = (
        (g_own.at[:, :side], 2 * y + c),
        (g_own.at[:, side:], 2 * (1 - y) + c),
        (g_core.at[:, :side], 2 * y + 1 - c),
        (g_core.at[:, side:], 2 * (1 - y) + 1 - c),
    )
    for block, owner in blocks:
        for j in range(2):
            for i in range(gl.shape[0]):
                at = j * lat + i * LANES
                gl[i, pl.ds(2 * owner + j, pieces, stride=STRIDE), :] = block[
                    :, at : at + LANES
                ].astype(F32)
    g_latent = masked(jnp.concatenate([gl[i] for i in range(gl.shape[0])], 1), mask).astype(BF)
    proj = jnp.concatenate([pa[...], pb[...]], 0)
    gd = (mm_nt(g_latent, proj) * sdown[...]).astype(BF)
    gd_out[...] = gd
    swap[:frames] = gd[:, width:]
    gproj = mm_tn(adown[...], g_latent)
    swap[frames : frames + width] = gproj[width:, :width].astype(BF)
    swap[frames + width :] = gproj[width:, width:].astype(BF)
    gproj_keep[:width] = gproj[:width, :width]
    gproj_keep[width:] = gproj[:width, width:]


def section_send_kernel(gd, dwa, dwb, send):
    _, y, _ = position()
    full = gd[...]
    g2 = moved(full, 1 - y)
    for j in range(STRIDE // 2):
        send[j] = section_grad(full, g2, dwa, dwb, 1 - y, j, send.shape[2]).astype(BF)


def section_keep_kernel(gd, dwa, dwb, keep):
    _, y, _ = position()
    full = gd[...]
    g2 = moved(full, y)
    for j in range(STRIDE // 2):
        keep[j] = section_grad(full, g2, dwa, dwb, y, j, keep.shape[2])


def weight_grads(a2a, a2b, ga, gb, part, j):
    half = STRIDE // 2
    p = part * half + j
    return mm_tn(a2a[p], ga) + mm_tn(a2b[p], gb)


def pair(g, part):
    return jnp.concatenate([g, moved(g, part)], 1)


def down_send_kernel(a2a, a2b, gd, swap, gproj, send_u, send_s):
    frames = gd.shape[0]
    width = swap.shape[1]
    _, _, x = position()
    ga = pair(gd[:, :width], x)
    gb = pair(swap[:frames], x)
    extra = send_s.shape[1] - send_u.shape[1]
    rows = send_u.shape[1]
    for j in range(STRIDE // 2):
        w = weight_grads(a2a, a2b, ga, gb, x, j)
        send_u[j] = w[:, :width].astype(BF)
        send_s[j, :rows] = w[:, width:].astype(BF)
        at = pl.ds(pl.multiple_of(((1 - x) * 4 + j) * extra, extra), extra)
        send_s[j, rows:] = (gproj[at, :] + swap[pl.ds(pl.multiple_of(frames + ((1 - x) * 4 + j) * extra, extra), extra), :].astype(F32)).astype(BF)


def down_keep_kernel(a2a, a2b, gd, swap, gproj, keep_u, keep_s):
    frames = gd.shape[0]
    width = swap.shape[1]
    _, _, x = position()
    part = 1 - x
    ga = pair(gd[:, :width], part)
    gb = pair(swap[:frames], part)
    extra = keep_s.shape[1] - keep_u.shape[1]
    rows = keep_u.shape[1]
    for j in range(STRIDE // 2):
        w = weight_grads(a2a, a2b, ga, gb, part, j)
        keep_u[j] = w[:, :width]
        keep_s[j, :rows] = w[:, width:]
        at = pl.ds(pl.multiple_of((x * 4 + j) * extra, extra), extra)
        keep_s[j, rows:] = gproj[at, :] + swap[pl.ds(pl.multiple_of(frames + (x * 4 + j) * extra, extra), extra), :].astype(F32)


def residual_kernel(
    mask, keep, recv, sec, ahid, shid, wo, a1, kept, send1, send2, send3, gh, buf,
):
    half = STRIDE // 2
    ch = keep.shape[2]
    hid = wo.shape[0]
    c, y, _ = position()
    g_out = jnp.zeros((hid, ch), F32)
    for j in range(half):
        g = keep[j] + recv[j].astype(F32)
        g_branch = masked(g * slope(sec[y * half + j].astype(F32)), mask).astype(BF)
        g_out = g_out + mm_tn(ahid[y * half + j], g_branch)
        gh[j] = mm_nt(g_branch, wo[...]) * shid[y * half + j].astype(F32)
    taps = [jnp.zeros((ch, hid), F32) for _ in range(3)]
    for j in range(half):
        g = gh[j]
        p = y * half + j
        here = g.astype(BF)
        taps[1] = taps[1] + mm_tn(a1[p], here)
        down1 = shift(g, 1)
        up1 = shift(g, -1)
        if j == 0:
            down1 = jnp.where(y == 0, shift(g, 2), down1)
        if j == half - 1:
            up1 = jnp.where(y == 1, shift(g, -2), up1)
        taps[0] = taps[0] + mm_tn(a1[lax.rem(p + STRIDE - 1, STRIDE)], down1.astype(BF))
        taps[2] = taps[2] + mm_tn(a1[lax.rem(p + 1, STRIDE)], up1.astype(BF))
    for k in range(3):
        for i in range(ch // hid):
            buf[k * (ch // hid) + i] = taps[k][i * hid : (i + 1) * hid]
    for i in range(ch // hid):
        buf[3 * (ch // hid) + i] = g_out[:, i * hid : (i + 1) * hid]
    m = 2 * y + c
    n = buf.shape[0] // 4
    for i in range(n):
        at = slice(i * hid, (i + 1) * hid)
        kept[at] = buf[m * n + i]
        for k, out in enumerate((send1, send2, send3)):
            out[at] = buf[(m ^ (k + 1)) * n + i].astype(BF)


def residual_finish_kernel(r0, r1, r2, r3, out_in, out_out, buf):
    c, y, _ = position()
    m = 2 * y + c
    rows, hid = r0.shape
    for k, r in enumerate((r0, r1, r2, r3)):
        buf[m ^ k] = r[...].astype(F32)
    for q in range(3):
        out_in[q * rows : (q + 1) * rows] = buf[q]
    for i in range(rows // hid):
        out_out[:, i * hid : (i + 1) * hid] = buf[3, i * hid : (i + 1) * hid]


def sum_kernel(keep, recv, own, *sends):
    z = depth()
    own[...] = keep[z] + recv[z].astype(F32)
    for k, out in enumerate(sends):
        at = z ^ (k + 1)
        out[...] = (keep[at] + recv[at].astype(F32)).astype(BF)


def swap_bit(value, axis, bit):
    n = lax.axis_size(axis)
    return lax.ppermute(value, axis, [(i, i ^ bit) for i in range(n)])


def stages_of(n):
    found, bit = [], 2
    while bit < n:
        members = 4 if n // bit >= 4 else 2
        found.append((bit, members))
        bit *= members
    return found


def pick(stack, index):
    return lax.dynamic_index_in_dim(stack, index, 0, keepdims=False)


def fan(values, axis, bit):
    return [swap_bit(v, axis, bit * (k + 1)) for k, v in enumerate(values)]


def plus(total, received):
    for r in received:
        total = total + r.astype(F32)
    return total


def reduce_rest(kept, received, me, stages):
    shape = kept.shape[1:]
    own, *sends = call(sum_kernel, [(shape, F32)] + [(shape, BF)] * 3, [kept, received])
    received = fan(sends, DP, stages[0][0])
    for bit, members in stages[1:]:
        parts = plus(own, received).reshape(members, -1, own.shape[-1])
        place = (me // bit) % members
        sends = [pick(parts, place ^ k).astype(BF) for k in range(1, members)]
        own, received = pick(parts, place), fan(sends, DP, bit)
    return lax.optimization_barrier(plus(own, received).astype(BF))


def gather_high(own, me, stages):
    for bit, members in reversed(stages[1:]):
        place = (me // bit) % members
        blocks = [own] + fan([own] * (members - 1), DP, bit)
        ordered = jnp.stack(blocks)
        own = jnp.concatenate([pick(ordered, place ^ k) for k in range(members)], 0)
    return own


def finish_kernel(shifted, count, written, projected, *refs):
    ins, rest = refs[:count], refs[count:]
    if projected:
        *_, out, out_proj, buf, sems, pbuf, psems = rest
    else:
        *_, out, buf, sems = rest
    _, _, x = position()
    z = depth()
    half = STRIDE // 2
    rows = buf.shape[1]

    def block(entry):
        operand, lead, k, own = entry
        ref = ins[operand]
        value = ref.at[pl.ds(lead, ref.shape[0] - lead), :]
        part, xp = (1 - x, x) if own else (x, 1 - x)
        return value, z ^ k, part, xp

    copies = []
    for n, entry in enumerate(written):
        value, j, part, _ = block(entry)
        tap = part * half + j + half
        if shifted:
            tap = jnp.where(part == 0, 3 * half + j, j)
        buf[n] = value[:rows].astype(F32)
        copy = pltpu.make_async_copy(
            buf.at[n], out.at[pl.ds(pl.multiple_of(tap * rows, rows), rows), :], sems.at[n]
        )
        copy.start()
        copies.append(copy)
    for n, entry in enumerate(projected):
        value, j, _, xp = block(entry)
        per, width = pbuf.shape[1:]
        pbuf[n] = value[rows : rows + per].astype(F32)
        copy = pltpu.make_async_copy(
            pbuf.at[n],
            out_proj.at[
                pl.ds(pl.multiple_of(j * per, per), per),
                pl.ds(pl.multiple_of(xp * width, width), width),
            ],
            psems.at[n],
        )
        copy.start()
        copies.append(copy)
    for copy in copies:
        copy.wait()


def body(
    features, lengths, routes, res_in_weight, res_out_weight, down_weight, proj_weight, cotangent
):
    utts = lengths.shape[0]
    total_rows = features.shape[0] // utts
    ch = features.shape[1]
    frames = total_rows // STRIDE
    hid = res_out_weight.shape[0]
    width = down_weight.shape[1]
    lat = proj_weight.shape[1]
    dp_count, mp_count = lax.axis_size(DP), lax.axis_size(MP)
    pieces = routes.shape[0]
    half_pieces = pieces // utts
    capacity = 2 * pieces // dp_count
    slots = dp_count * capacity
    cols = cotangent.shape[1]
    half = STRIDE // 2
    me_dp = lax.axis_index(DP)
    stages = stages_of(dp_count)
    staged = dp_count == 8
    lane_block = ((dp_count // 2, capacity, cols), BF)
    pair_block = ((2, capacity, cols), BF)

    def columns(parts):
        received = fan(parts[1:], DP, 2)
        return call(columns_kernel, [lane_block] * 2, [parts[0], *received])

    def all_to_all(value):
        return lax.all_to_all(
            value.reshape(dp_count, capacity, cols), DP, split_axis=0, concat_axis=0
        ).reshape(slots, cols)

    other_down = swap_bit(down_weight, MP, 1)
    other_proj = swap_bit(proj_weight, MP, 1)
    if staged:
        parts = call(
            parts_kernel,
            [pair_block] * 4,
            [cotangent.reshape(dp_count // 2, 2, capacity, cols)],
            scratch=[pltpu.SemaphoreType.DMA((4,))],
            where={0: pltpu.HBM},
        )
        send, keep = columns(parts)
        both_axes = [(i, i ^ (mp_count + 2)) for i in range(dp_count * mp_count)]
        far = lax.ppermute(send, (DP, MP), both_axes)
        across = swap_bit(send, DP, 1)
        returned = [keep, across, swap_bit(keep, MP, 2), far]
    else:
        direct = all_to_all(cotangent)
        returned = [direct, swap_bit(direct, MP, 2)]

    loads = 4
    a1, a2, sec, ahid, shid, placing, mask = call(
        functools.partial(forward_kernel, capacity),
        [
            ((STRIDE, frames, ch), BF),
            ((STRIDE, frames, ch), BF),
            ((STRIDE, frames, ch), BF),
            ((STRIDE, frames, hid), BF),
            ((STRIDE, frames, hid), BF),
            ((slots, pieces), BF),
            ((frames, LANES), F32),
        ],
        [lengths, features, routes.reshape(1, pieces), res_in_weight, res_out_weight],
        scratch=[
            pltpu.VMEM((ch // LANES, total_rows, LANES), F32),
            pltpu.VMEM((STRIDE, frames, 3 * hid), F32),
            pltpu.SMEM(lengths.shape, lengths.dtype),
            pltpu.VMEM((loads, total_rows // loads, ch), BF),
            pltpu.VMEM((1, pieces), routes.dtype),
            pltpu.VMEM(res_in_weight.shape, BF),
            pltpu.VMEM(res_out_weight.shape, BF),
            pltpu.SemaphoreType.DMA((loads + 4,)),
        ],
        where={i: pltpu.HBM for i in range(5)},
        flops=4 << 30,
    )
    other_a2 = swap_bit(a2, MP, 1)
    adown, sdown, lat_send, lat_keep = call(
        down_kernel,
        [
            ((frames, 2 * width), BF),
            ((frames, 2 * width), F32),
            ((half_pieces, half * lat), BF),
            ((half_pieces, half * lat), BF),
        ],
        [mask, a2, down_weight, other_down, proj_weight, other_proj],
        scratch=[pltpu.VMEM((lat // LANES, frames, LANES), F32)],
        flops=1 << 30,
    )
    lat_y = swap_bit(lat_send, MP, 2)

    g_own, g_other = call(
        pick_kernel,
        [((half_pieces, 2 * cols), BF)] * 2,
        [placing, *returned],
        scratch=[pltpu.VMEM((slots, cols), BF), pltpu.VMEM((pieces, 2 * cols), F32)],
    )
    g_core = swap_bit(g_other, MP, 1)

    mine, theirs = call(
        lat_mix_kernel, [((half_pieces, cols), BF)] * 2, [lat_keep, lat_y]
    )
    theirs = swap_bit(theirs, MP, 1)

    gd, swap, gproj = call(
        latent_grad_kernel,
        [
            ((frames, 2 * width), BF),
            ((frames + 2 * width, width), BF),
            ((2 * width, lat // 2), F32),
        ],
        [mask, g_own, g_core, adown, sdown, proj_weight, other_proj],
        scratch=[pltpu.VMEM((lat // LANES, frames, LANES), F32)],
        flops=1 << 30,
    )
    got = swap_bit(swap, MP, 1)
    (g_send,) = call(
        section_send_kernel,
        [((half, frames, ch), BF)],
        [gd, down_weight, other_down],
        flops=1 << 29,
    )
    g_recv = swap_bit(g_send, MP, 2)
    extra = 2 * width // STRIDE
    send_u, send_s = call(
        down_send_kernel,
        [((half, ch, width), BF), ((half, ch + extra, width), BF)],
        [a2, other_a2, gd, got, gproj],
        flops=1 << 29,
    )
    recv_u = swap_bit(send_u, DP, 1)
    recv_s = swap_bit(send_s, DP, 1)
    keep_u, keep_s = call(
        down_keep_kernel,
        [((half, ch, width), F32), ((half, ch + extra, width), F32)],
        [a2, other_a2, gd, got, gproj],
        flops=1 << 29,
    )
    (keep_g,) = call(
        section_keep_kernel,
        [((half, frames, ch), F32)],
        [gd, down_weight, other_down],
        flops=1 << 29,
    )

    row_scratch = pltpu.VMEM((pieces, cols), F32)
    if staged:
        parts = call(
            place_parts_kernel,
            [pair_block] * 4,
            [placing, mine, theirs],
            scratch=[row_scratch, pltpu.VMEM((slots, cols), BF)],
        )
        received = fan(parts[1:], DP, 2)
        flat_block = ((dp_count // 2 * capacity * cols // LANES, LANES), BF)
        send_o, keep_o = call(flat_columns_kernel, [flat_block, lane_block], [parts[0], *received])
        crossing = [send_o]
    else:
        (outgoing,) = call(
            place_kernel,
            [((slots, cols), BF)],
            [placing, mine, theirs],
            scratch=[row_scratch],
        )
        packed = all_to_all(outgoing)
        crossing = []

    blocks = 4 * (ch // hid)
    quarter = (blocks // 4 * hid, hid)
    e_own, *e_sends = call(
        residual_kernel,
        [(quarter, F32)] + [(quarter, BF)] * 3,
        [mask, keep_g, g_recv, sec, ahid, shid, res_out_weight, a1],
        scratch=[pltpu.VMEM((half, frames, hid), F32), pltpu.VMEM((blocks, hid, hid), F32)],
        flops=1 << 30,
    )
    received = fan(e_sends, MP, 1)
    e_own = plus(e_own, received)
    sent = e_own.astype(BF)

    own_u = gather_high(reduce_rest(keep_u, recv_u, me_dp, stages), me_dp, stages)
    own_s = gather_high(reduce_rest(keep_s, recv_s, me_dp, stages), me_dp, stages)
    all_u = [own_u] + fan([own_u] * 3, DP, stages[0][0])
    both = jnp.concatenate([own_s, sent])
    first_s = swap_bit(both, DP, 1)
    all_s = [own_s] + fan([own_s] * 3, DP, stages[0][0])
    their_u = swap_bit(jnp.concatenate(all_u + crossing), DP, 1)
    their_s = swap_bit(jnp.concatenate(all_s[1:]), DP, 1)
    received = [first_s[own_s.shape[0] :]]
    for bit, members in stages:
        e_own = plus(e_own, received)
        sent = e_own.astype(BF)
        received = fan([sent] * (members - 1), DP, bit)
    sent = plus(e_own, received).astype(BF)
    grad_res_in, grad_res_out = call(
        residual_finish_kernel,
        [((3 * ch, hid), F32), ((hid, ch), F32)],
        [sent, *fan([sent] * 3, MP, 1)],
        scratch=[pltpu.VMEM((4,) + quarter, F32)],
    )

    down_out = ((2 * STRIDE * ch, width), F32)
    proj_out = ((width, lat), F32)
    mine = tuple((k, 0, k, True) for k in range(4))

    def finish(shifted, ins, written, projected, before=()):
        n, m = len(ins), len(before)
        outs = [down_out] + [proj_out] * bool(projected)
        scratch = [
            pltpu.VMEM((len(written), ch, width), F32),
            pltpu.SemaphoreType.DMA((len(written),)),
        ]
        if projected:
            scratch += [
                pltpu.VMEM((len(projected), extra, width), F32),
                pltpu.SemaphoreType.DMA((len(projected),)),
            ]
        return call(
            functools.partial(finish_kernel, shifted, n, written, projected),
            outs,
            [*ins, *before],
            scratch=scratch,
            where={n + i: pltpu.HBM for i in range(m + len(outs))},
            aliases={n + i: i for i in range(m)},
        )

    size_u, size_s = own_u.shape[0], own_s.shape[0]
    first = mine + tuple((4, k * size_u, k, False) for k in range(4))
    (grad_down,) = finish(False, [*all_u, their_u], first, ())
    second = mine + ((4, 0, 0, False),)
    done = finish(True, [*all_s, first_s], second, second, [grad_down])
    last = tuple((0, (k - 1) * size_s, k, False) for k in range(1, 4))
    grad_down, grad_proj = finish(True, [their_s], last, last, done)
    if staged:
        (packed,) = call(
            functools.partial(packed_kernel, 4 * size_u),
            [((slots, cols), BF)],
            [keep_o, their_u],
        )
    return (packed, grad_res_in, grad_res_out, grad_down, grad_proj)


def solution(mesh):
    return jax.shard_map(
        body,
        mesh=mesh,
        in_specs=(
            P(DP, None),
            P(DP),
            P(DP, None),
            P(),
            P(),
            P(None, MP),
            P(MP, None),
            P(DP, MP),
        ),
        out_specs=(P(DP, MP), P(), P(), P(None, MP), P(MP, None)),
        check_vma=False,
    )
```

```python
import functools
import jax
import jax.numpy as jnp
from jax import lax
from jax.experimental import pallas as pl
from jax.experimental.pallas import tpu as pltpu
from jax.sharding import PartitionSpec as P

STRIDE = 8
DP, MP = "dp", "mp"
LANES = 128
BF = jnp.bfloat16
F32 = jnp.float32
VMEM_LIMIT = 16 << 20


def elu(v):
    return jnp.where(v > 0, v, jnp.exp(jnp.minimum(v, 0.0)) - 1.0)


def slope(v):
    return jnp.where(v > 0, 1.0, jnp.exp(jnp.minimum(v, 0.0)))


def mm(a, b):
    return jnp.dot(a, b, preferred_element_type=F32)


def mm_nt(a, b):
    return lax.dot_general(a, b, (((1,), (1,)), ((), ())), preferred_element_type=F32)


def mm_tn(a, b):
    return lax.dot_general(a, b, (((0,), (0,)), ((), ())), preferred_element_type=F32)


def shift(v, s):
    n = v.shape[0]
    rows = lax.broadcasted_iota(jnp.int32, v.shape, 0)
    rolled = pltpu.roll(v, (-s) % n, 0)
    keep = rows < n - s if s > 0 else rows >= -s
    return jnp.where(keep, rolled, 0.0)


def spread(ref, value):
    for i in range(ref.shape[0]):
        ref[i] = value[:, i * LANES : (i + 1) * LANES]


def every(ref, start, size):
    return jnp.concatenate(
        [ref[i, pl.ds(start, size, stride=STRIDE), :] for i in range(ref.shape[0])], 1
    )


def call(kernel, outs, ins, scratch=(), flops=0, where=None, aliases=None):
    whole = pl.BlockSpec(memory_space=pltpu.VMEM)
    spaces = {i: pl.BlockSpec(memory_space=space) for i, space in (where or {}).items()}
    ins = [
        pltpu.with_memory_space_constraint(a, pltpu.HBM) if i in spaces else a
        for i, a in enumerate(ins)
    ]
    return pl.pallas_call(
        kernel,
        out_shape=[jax.ShapeDtypeStruct(s, d) for s, d in outs],
        in_specs=[spaces.get(i, whole) for i in range(len(ins))],
        out_specs=[spaces.get(len(ins) + i, whole) for i in range(len(outs))],
        scratch_shapes=list(scratch),
        input_output_aliases=aliases or {},
        compiler_params=pltpu.CompilerParams(vmem_limit_bytes=VMEM_LIMIT),
        cost_estimate=pl.CostEstimate(
            flops=flops, transcendentals=0, bytes_accessed=1 << 20
        ),
    )(*ins)


def position():
    m = lax.axis_index(MP)
    return lax.rem(m, 2), m // 2, lax.rem(lax.axis_index(DP), 2)


def masked(value, mask):
    wide = jnp.concatenate([mask[...]] * (value.shape[1] // mask.shape[1]), 1)
    return jnp.where(wide > 0, value, 0.0)


def depth():
    return lax.rem(lax.axis_index(DP) // 2, 4)


def forward_kernel(
    capacity, lengths_hbm, feat_hbm, routes_hbm, wi_hbm, wo_hbm,
    a1, a2, sec, ahid, shid, placing, mask, xs, ys, lengths, feat, routes, wi, wo, sems,
):
    frames, ch = a1.shape[1], a1.shape[2]
    hid = wo.shape[0]
    c, _, _ = position()
    rows = frames * STRIDE
    parts = feat.shape[0]
    size = rows // parts
    copies = [
        pltpu.make_async_copy(
            feat_hbm.at[pl.ds(pl.multiple_of(c * rows + i * size, size), size), :],
            feat.at[i],
            sems.at[i],
        )
        for i in range(parts)
    ]
    rest = [
        pltpu.make_async_copy(src, dst, sems.at[parts + i])
        for i, (src, dst) in enumerate(((routes_hbm, routes), (wi_hbm, wi), (wo_hbm, wo)))
    ]
    table = pltpu.make_async_copy(lengths_hbm, lengths, sems.at[parts + len(rest)])
    table.start()
    for copy in copies + rest:
        copy.start()
    table.wait()
    length = lengths[c]
    live = lax.broadcasted_iota(jnp.int32, (frames, ch), 0) < length
    mask[...] = jnp.where(live[:, : mask.shape[1]], 1.0, 0.0)
    for i in range(parts):
        copies[i].wait()
        value = feat[i].astype(F32)
        for k in range(xs.shape[0]):
            xs[k, i * size : (i + 1) * size] = value[:, k * LANES : (k + 1) * LANES]
    for copy in rest:
        copy.wait()
    placing[...] = placing_of(routes[...], placing.shape[0], capacity)
    wcat = jnp.concatenate([wi[k * ch : (k + 1) * ch, :] for k in range(3)], 1)

    def signal(p):
        return jnp.where(live, every(xs, p, frames), 0.0)

    for p in range(STRIDE):
        act = elu(signal(p)).astype(BF)
        a1[p] = act
        ys[p] = mm(act, wcat)
    for p in range(STRIDE):
        left = shift(ys[(p - 1) % STRIDE, :, :hid], -1 if p > 0 else -2)
        right = shift(ys[(p + 1) % STRIDE, :, 2 * hid :], 1 if p < STRIDE - 1 else 2)
        hidden = left + ys[p, :, hid : 2 * hid] + right
        act_hid = elu(hidden).astype(BF)
        ahid[p] = act_hid
        shid[p] = slope(hidden).astype(BF)
        section = jnp.where(live, signal(p) + mm(act_hid, wo[...]), 0.0).astype(BF)
        sec[p] = section
        a2[p] = elu(section.astype(F32)).astype(BF)


def down_kernel(
    mask, a2, dwa, dwb, pa, pb, adown, sdown, lat_send, lat_keep, ls,
):
    frames, ch = a2.shape[1], a2.shape[2]
    _, y, _ = position()
    half = STRIDE // 2

    def tap(k):
        return jnp.concatenate([dwa[k * ch : (k + 1) * ch, :], dwb[k * ch : (k + 1) * ch, :]], 1)

    down = jnp.zeros((frames, 2 * dwa.shape[1]), F32)
    before = jnp.zeros_like(down)
    after = jnp.zeros_like(down)
    for p in range(STRIDE):
        act = a2[p]
        down = down + mm(act, tap(p + half))
        if p < half:
            after = after + mm(act, tap(p + 3 * half))
        else:
            before = before + mm(act, tap(p - half))
    down = down + shift(before, -1) + shift(after, 1)
    act_down = elu(down).astype(BF)
    adown[...] = act_down
    sdown[...] = slope(down)
    proj = jnp.concatenate([pa[...], pb[...]], 0)
    lat = proj.shape[1]
    spread(ls, masked(mm(act_down, proj), mask))
    pieces = frames // STRIDE
    for j in range(half):
        cols = slice(j * lat, (j + 1) * lat)
        lat_send[:, cols] = every(ls, half * (1 - y) + j, pieces).astype(BF)
        lat_keep[:, cols] = every(ls, half * y + j, pieces).astype(BF)


def placing_of(targets, slots, capacity):
    pieces = targets.shape[1]
    chosen = jnp.where(targets == lax.broadcasted_iota(jnp.int32, (128, pieces), 0), 1.0, 0.0)
    upper = (
        lax.broadcasted_iota(jnp.int32, (pieces, pieces), 0)
        < lax.broadcasted_iota(jnp.int32, (pieces, pieces), 1)
    )
    earlier = mm(chosen.astype(BF), jnp.where(upper, 1.0, 0.0).astype(BF))
    rank = jnp.sum(earlier * chosen, axis=0, keepdims=True).astype(jnp.int32)
    slot = targets * capacity + rank
    ids = lax.broadcasted_iota(jnp.int32, (slots, pieces), 0)
    return jnp.where(slot == ids, 1.0, 0.0).astype(BF)


def parts_kernel(whole, *refs):
    *outs, sems = refs
    z = depth()
    copies = [
        pltpu.make_async_copy(whole.at[z ^ k], out, sems.at[k]) for k, out in enumerate(outs)
    ]
    for copy in copies:
        copy.start()
    for copy in copies:
        copy.wait()


def columns_kernel(*refs):
    *parts, send, keep = refs
    _, _, x = position()
    for k, part in enumerate(parts):
        send[k] = part[1 - x]
        keep[k] = part[x]


def assemble(keep, recv, out):
    _, _, x = position()
    z = depth()
    size = keep.shape[1]
    for k in range(keep.shape[0]):
        for part, column in ((keep, x), (recv, 1 - x)):
            at = (2 * (z ^ k) + column) * size
            out[pl.ds(pl.multiple_of(at, size), size), :] = part[k]


def pick_kernel(placing, *refs):
    *parts, own, other, rows, buf = refs
    c, _, _ = position()
    cols = parts[0].shape[-1]
    for i in range(2):
        if len(parts) == 2:
            rows[...] = parts[i][...]
        else:
            assemble(parts[2 * i], parts[2 * i + 1], rows)
        buf[:, i * cols : (i + 1) * cols] = mm_tn(placing[...], rows[...])
    half = own.shape[0]
    own[...] = buf[pl.ds(pl.multiple_of(c * half, half), half), :].astype(BF)
    other[...] = buf[pl.ds(pl.multiple_of((1 - c) * half, half), half), :].astype(BF)


def place_kernel(placing, mine, theirs, outgoing, buf):
    c, _, _ = position()
    half = mine.shape[0]
    buf[pl.ds(pl.multiple_of(c * half, half), half), :] = mine[...].astype(F32)
    buf[pl.ds(pl.multiple_of((1 - c) * half, half), half), :] = theirs[...].astype(F32)
    outgoing[...] = mm(placing[...], buf[...].astype(BF)).astype(BF)


def place_parts_kernel(placing, mine, theirs, *refs):
    *outs, buf, rows = refs
    place_kernel(placing, mine, theirs, rows, buf)
    z = depth()
    _, columns, size, _ = (1,) + outs[0].shape
    for k, out in enumerate(outs):
        for i in range(columns):
            at = ((z ^ k) * columns + i) * size
            out[i] = rows[pl.ds(pl.multiple_of(at, size), size), :]


def flat_columns_kernel(*refs):
    *parts, send, keep = refs
    _, _, x = position()
    size, cols = keep.shape[1:]
    groups = cols // LANES
    for k, part in enumerate(parts):
        value = part[1 - x]
        for q in range(groups):
            at = (k * groups + q) * size
            send[at : at + size] = value[:, q * LANES : (q + 1) * LANES]
        keep[k] = part[x]


def packed_kernel(base, keep, recv, out):
    _, _, x = position()
    z = depth()
    members, size, cols = keep.shape
    groups = cols // LANES
    for k in range(members):
        own = pl.ds(pl.multiple_of((2 * (z ^ k) + x) * size, size), size)
        other = pl.ds(pl.multiple_of((2 * (z ^ k) + 1 - x) * size, size), size)
        out[own, :] = keep[k]
        for q in range(groups):
            at = base + (k * groups + q) * size
            out[other, q * LANES : (q + 1) * LANES] = recv[at : at + size]


def lat_mix_kernel(lat_keep, lat_y, mine, theirs):
    c, _, _ = position()
    total = (lat_keep[...].astype(F32) + lat_y[...].astype(F32)).astype(BF)
    cols = mine.shape[1]
    mine[...] = jnp.where(c == 0, total[:, :cols], total[:, cols:])
    theirs[...] = jnp.where(c == 0, total[:, cols:], total[:, :cols])


def section_grad(gd, gshift, wa, wb, part, j, ch):
    half = STRIDE // 2
    first = part * half + j + half
    second = jnp.where(part == 0, 3 * half + j, j)
    rows1 = pl.ds(pl.multiple_of(first * ch, ch), ch)
    rows2 = pl.ds(pl.multiple_of(second * ch, ch), ch)
    w1 = jnp.concatenate([wa[rows1, :], wb[rows1, :]], 1)
    w2 = jnp.concatenate([wa[rows2, :], wb[rows2, :]], 1)
    return mm_nt(gd, w1) + mm_nt(gshift, w2)


def moved(gd, part):
    g = gd.astype(F32)
    return jnp.where(part == 0, shift(g, -1), shift(g, 1)).astype(BF)


def latent_grad_kernel(
    mask, g_own, g_core, adown, sdown, pa, pb,
    gd_out, swap, gproj_keep, gl,
):
    frames = adown.shape[0]
    width, lat = pa.shape
    pieces = g_own.shape[0]
    c, y, _ = position()
    side = 2 * lat
    blocks = (
        (g_own.at[:, :side], 2 * y + c),
        (g_own.at[:, side:], 2 * (1 - y) + c),
        (g_core.at[:, :side], 2 * y + 1 - c),
        (g_core.at[:, side:], 2 * (1 - y) + 1 - c),
    )
    for block, owner in blocks:
        for j in range(2):
            for i in range(gl.shape[0]):
                at = j * lat + i * LANES
                gl[i, pl.ds(2 * owner + j, pieces, stride=STRIDE), :] = block[
                    :, at : at + LANES
                ].astype(F32)
    g_latent = masked(jnp.concatenate([gl[i] for i in range(gl.shape[0])], 1), mask).astype(BF)
    proj = jnp.concatenate([pa[...], pb[...]], 0)
    gd = (mm_nt(g_latent, proj) * sdown[...]).astype(BF)
    gd_out[...] = gd
    swap[:frames] = gd[:, width:]
    gproj = mm_tn(adown[...], g_latent)
    swap[frames : frames + width] = gproj[width:, :width].astype(BF)
    swap[frames + width :] = gproj[width:, width:].astype(BF)
    gproj_keep[:width] = gproj[:width, :width]
    gproj_keep[width:] = gproj[:width, width:]


def section_send_kernel(gd, dwa, dwb, send):
    _, y, _ = position()
    full = gd[...]
    g2 = moved(full, 1 - y)
    for j in range(STRIDE // 2):
        send[j] = section_grad(full, g2, dwa, dwb, 1 - y, j, send.shape[2]).astype(BF)


def section_keep_kernel(gd, dwa, dwb, keep):
    _, y, _ = position()
    full = gd[...]
    g2 = moved(full, y)
    for j in range(STRIDE // 2):
        keep[j] = section_grad(full, g2, dwa, dwb, y, j, keep.shape[2])


def weight_grads(a2a, a2b, ga, gb, part, j):
    half = STRIDE // 2
    p = part * half + j
    return mm_tn(a2a[p], ga) + mm_tn(a2b[p], gb)


def pair(g, part):
    return jnp.concatenate([g, moved(g, part)], 1)


def down_send_kernel(a2a, a2b, gd, swap, gproj, send_u, send_s):
    frames = gd.shape[0]
    width = swap.shape[1]
    _, _, x = position()
    ga = pair(gd[:, :width], x)
    gb = pair(swap[:frames], x)
    extra = send_s.shape[1] - send_u.shape[1]
    rows = send_u.shape[1]
    for j in range(STRIDE // 2):
        w = weight_grads(a2a, a2b, ga, gb, x, j)
        send_u[j] = w[:, :width].astype(BF)
        send_s[j, :rows] = w[:, width:].astype(BF)
        at = pl.ds(pl.multiple_of(((1 - x) * 4 + j) * extra, extra), extra)
        send_s[j, rows:] = (gproj[at, :] + swap[pl.ds(pl.multiple_of(frames + ((1 - x) * 4 + j) * extra, extra), extra), :].astype(F32)).astype(BF)


def down_keep_kernel(a2a, a2b, gd, swap, gproj, keep_u, keep_s):
    frames = gd.shape[0]
    width = swap.shape[1]
    _, _, x = position()
    part = 1 - x
    ga = pair(gd[:, :width], part)
    gb = pair(swap[:frames], part)
    extra = keep_s.shape[1] - keep_u.shape[1]
    rows = keep_u.shape[1]
    for j in range(STRIDE // 2):
        w = weight_grads(a2a, a2b, ga, gb, part, j)
        keep_u[j] = w[:, :width]
        keep_s[j, :rows] = w[:, width:]
        at = pl.ds(pl.multiple_of((x * 4 + j) * extra, extra), extra)
        keep_s[j, rows:] = gproj[at, :] + swap[pl.ds(pl.multiple_of(frames + (x * 4 + j) * extra, extra), extra), :].astype(F32)


def residual_kernel(
    mask, keep, recv, sec, ahid, shid, wo, a1, kept, send1, send2, send3, gh, buf,
):
    half = STRIDE // 2
    ch = keep.shape[2]
    hid = wo.shape[0]
    c, y, _ = position()
    g_out = jnp.zeros((hid, ch), F32)
    for j in range(half):
        g = keep[j] + recv[j].astype(F32)
        g_branch = masked(g * slope(sec[y * half + j].astype(F32)), mask).astype(BF)
        g_out = g_out + mm_tn(ahid[y * half + j], g_branch)
        gh[j] = mm_nt(g_branch, wo[...]) * shid[y * half + j].astype(F32)
    taps = [jnp.zeros((ch, hid), F32) for _ in range(3)]
    for j in range(half):
        g = gh[j]
        p = y * half + j
        here = g.astype(BF)
        taps[1] = taps[1] + mm_tn(a1[p], here)
        down1 = shift(g, 1)
        up1 = shift(g, -1)
        if j == 0:
            down1 = jnp.where(y == 0, shift(g, 2), down1)
        if j == half - 1:
            up1 = jnp.where(y == 1, shift(g, -2), up1)
        taps[0] = taps[0] + mm_tn(a1[lax.rem(p + STRIDE - 1, STRIDE)], down1.astype(BF))
        taps[2] = taps[2] + mm_tn(a1[lax.rem(p + 1, STRIDE)], up1.astype(BF))
    for k in range(3):
        for i in range(ch // hid):
            buf[k * (ch // hid) + i] = taps[k][i * hid : (i + 1) * hid]
    for i in range(ch // hid):
        buf[3 * (ch // hid) + i] = g_out[:, i * hid : (i + 1) * hid]
    m = 2 * y + c
    n = buf.shape[0] // 4
    for i in range(n):
        at = slice(i * hid, (i + 1) * hid)
        kept[at] = buf[m * n + i]
        for k, out in enumerate((send1, send2, send3)):
            out[at] = buf[(m ^ (k + 1)) * n + i].astype(BF)


def residual_finish_kernel(r0, r1, r2, r3, out_in, out_out, buf):
    c, y, _ = position()
    m = 2 * y + c
    rows, hid = r0.shape
    for k, r in enumerate((r0, r1, r2, r3)):
        buf[m ^ k] = r[...].astype(F32)
    for q in range(3):
        out_in[q * rows : (q + 1) * rows] = buf[q]
    for i in range(rows // hid):
        out_out[:, i * hid : (i + 1) * hid] = buf[3, i * hid : (i + 1) * hid]


def sum_kernel(keep, recv, own, *sends):
    z = depth()
    own[...] = keep[z] + recv[z].astype(F32)
    for k, out in enumerate(sends):
        at = z ^ (k + 1)
        out[...] = (keep[at] + recv[at].astype(F32)).astype(BF)


def swap_bit(value, axis, bit):
    n = lax.axis_size(axis)
    return lax.ppermute(value, axis, [(i, i ^ bit) for i in range(n)])


def stages_of(n):
    found, bit = [], 2
    while bit < n:
        members = 4 if n // bit >= 4 else 2
        found.append((bit, members))
        bit *= members
    return found


def pick(stack, index):
    return lax.dynamic_index_in_dim(stack, index, 0, keepdims=False)


def fan(values, axis, bit):
    return [swap_bit(v, axis, bit * (k + 1)) for k, v in enumerate(values)]


def plus(total, received):
    for r in received:
        total = total + r.astype(F32)
    return total


def reduce_rest(kept, received, me, stages):
    shape = kept.shape[1:]
    own, *sends = call(sum_kernel, [(shape, F32)] + [(shape, BF)] * 3, [kept, received])
    received = fan(sends, DP, stages[0][0])
    for bit, members in stages[1:]:
        parts = plus(own, received).reshape(members, -1, own.shape[-1])
        place = (me // bit) % members
        sends = [pick(parts, place ^ k).astype(BF) for k in range(1, members)]
        own, received = pick(parts, place), fan(sends, DP, bit)
    return lax.optimization_barrier(plus(own, received).astype(BF))


def gather_high(own, me, stages):
    for bit, members in reversed(stages[1:]):
        place = (me // bit) % members
        blocks = [own] + fan([own] * (members - 1), DP, bit)
        ordered = jnp.stack(blocks)
        own = jnp.concatenate([pick(ordered, place ^ k) for k in range(members)], 0)
    return own


def finish_kernel(shifted, count, written, projected, *refs):
    ins, rest = refs[:count], refs[count:]
    if projected:
        *_, out, out_proj, buf, sems, pbuf, psems = rest
    else:
        *_, out, buf, sems = rest
    _, _, x = position()
    z = depth()
    half = STRIDE // 2
    rows = buf.shape[1]

    def block(entry):
        operand, lead, k, own = entry
        ref = ins[operand]
        value = ref.at[pl.ds(lead, ref.shape[0] - lead), :]
        part, xp = (1 - x, x) if own else (x, 1 - x)
        return value, z ^ k, part, xp

    copies = []
    for n, entry in enumerate(written):
        value, j, part, _ = block(entry)
        tap = part * half + j + half
        if shifted:
            tap = jnp.where(part == 0, 3 * half + j, j)
        buf[n] = value[:rows].astype(F32)
        copy = pltpu.make_async_copy(
            buf.at[n], out.at[pl.ds(pl.multiple_of(tap * rows, rows), rows), :], sems.at[n]
        )
        copy.start()
        copies.append(copy)
    for n, entry in enumerate(projected):
        value, j, _, xp = block(entry)
        per, width = pbuf.shape[1:]
        pbuf[n] = value[rows : rows + per].astype(F32)
        copy = pltpu.make_async_copy(
            pbuf.at[n],
            out_proj.at[
                pl.ds(pl.multiple_of(j * per, per), per),
                pl.ds(pl.multiple_of(xp * width, width), width),
            ],
            psems.at[n],
        )
        copy.start()
        copies.append(copy)
    for copy in copies:
        copy.wait()


def body(
    features, lengths, routes, res_in_weight, res_out_weight, down_weight, proj_weight, cotangent
):
    utts = lengths.shape[0]
    total_rows = features.shape[0] // utts
    ch = features.shape[1]
    frames = total_rows // STRIDE
    hid = res_out_weight.shape[0]
    width = down_weight.shape[1]
    lat = proj_weight.shape[1]
    dp_count, mp_count = lax.axis_size(DP), lax.axis_size(MP)
    pieces = routes.shape[0]
    half_pieces = pieces // utts
    capacity = 2 * pieces // dp_count
    slots = dp_count * capacity
    cols = cotangent.shape[1]
    half = STRIDE // 2
    me_dp = lax.axis_index(DP)
    stages = stages_of(dp_count)
    staged = dp_count == 8
    lane_block = ((dp_count // 2, capacity, cols), BF)
    pair_block = ((2, capacity, cols), BF)

    def columns(parts):
        received = fan(parts[1:], DP, 2)
        return call(columns_kernel, [lane_block] * 2, [parts[0], *received])

    def all_to_all(value):
        return lax.all_to_all(
            value.reshape(dp_count, capacity, cols), DP, split_axis=0, concat_axis=0
        ).reshape(slots, cols)

    other_down = swap_bit(down_weight, MP, 1)
    other_proj = swap_bit(proj_weight, MP, 1)
    if staged:
        parts = call(
            parts_kernel,
            [pair_block] * 4,
            [cotangent.reshape(dp_count // 2, 2, capacity, cols)],
            scratch=[pltpu.SemaphoreType.DMA((4,))],
            where={0: pltpu.HBM},
        )
        send, keep = columns(parts)
        both_axes = [(i, i ^ (mp_count + 2)) for i in range(dp_count * mp_count)]
        far = lax.ppermute(send, (DP, MP), both_axes)
        across = swap_bit(send, DP, 1)
        returned = [keep, across, swap_bit(keep, MP, 2), far]
    else:
        direct = all_to_all(cotangent)
        returned = [direct, swap_bit(direct, MP, 2)]

    loads = 4
    a1, a2, sec, ahid, shid, placing, mask = call(
        functools.partial(forward_kernel, capacity),
        [
            ((STRIDE, frames, ch), BF),
            ((STRIDE, frames, ch), BF),
            ((STRIDE, frames, ch), BF),
            ((STRIDE, frames, hid), BF),
            ((STRIDE, frames, hid), BF),
            ((slots, pieces), BF),
            ((frames, LANES), F32),
        ],
        [lengths, features, routes.reshape(1, pieces), res_in_weight, res_out_weight],
        scratch=[
            pltpu.VMEM((ch // LANES, total_rows, LANES), F32),
            pltpu.VMEM((STRIDE, frames, 3 * hid), F32),
            pltpu.SMEM(lengths.shape, lengths.dtype),
            pltpu.VMEM((loads, total_rows // loads, ch), BF),
            pltpu.VMEM((1, pieces), routes.dtype),
            pltpu.VMEM(res_in_weight.shape, BF),
            pltpu.VMEM(res_out_weight.shape, BF),
            pltpu.SemaphoreType.DMA((loads + 4,)),
        ],
        where={i: pltpu.HBM for i in range(5)},
        flops=4 << 30,
    )
    other_a2 = swap_bit(a2, MP, 1)
    adown, sdown, lat_send, lat_keep = call(
        down_kernel,
        [
            ((frames, 2 * width), BF),
            ((frames, 2 * width), F32),
            ((half_pieces, half * lat), BF),
            ((half_pieces, half * lat), BF),
        ],
        [mask, a2, down_weight, other_down, proj_weight, other_proj],
        scratch=[pltpu.VMEM((lat // LANES, frames, LANES), F32)],
        flops=1 << 30,
    )
    lat_y = swap_bit(lat_send, MP, 2)

    g_own, g_other = call(
        pick_kernel,
        [((half_pieces, 2 * cols), BF)] * 2,
        [placing, *returned],
        scratch=[pltpu.VMEM((slots, cols), BF), pltpu.VMEM((pieces, 2 * cols), F32)],
    )
    g_core = swap_bit(g_other, MP, 1)

    mine, theirs = call(
        lat_mix_kernel, [((half_pieces, cols), BF)] * 2, [lat_keep, lat_y]
    )
    theirs = swap_bit(theirs, MP, 1)

    gd, swap, gproj = call(
        latent_grad_kernel,
        [
            ((frames, 2 * width), BF),
            ((frames + 2 * width, width), BF),
            ((2 * width, lat // 2), F32),
        ],
        [mask, g_own, g_core, adown, sdown, proj_weight, other_proj],
        scratch=[pltpu.VMEM((lat // LANES, frames, LANES), F32)],
        flops=1 << 30,
    )
    got = swap_bit(swap, MP, 1)
    (g_send,) = call(
        section_send_kernel,
        [((half, frames, ch), BF)],
        [gd, down_weight, other_down],
        flops=1 << 29,
    )
    g_recv = swap_bit(g_send, MP, 2)
    extra = 2 * width // STRIDE
    send_u, send_s = call(
        down_send_kernel,
        [((half, ch, width), BF), ((half, ch + extra, width), BF)],
        [a2, other_a2, gd, got, gproj],
        flops=1 << 29,
    )
    recv_u = swap_bit(send_u, DP, 1)
    recv_s = swap_bit(send_s, DP, 1)
    keep_u, keep_s = call(
        down_keep_kernel,
        [((half, ch, width), F32), ((half, ch + extra, width), F32)],
        [a2, other_a2, gd, got, gproj],
        flops=1 << 29,
    )
    (keep_g,) = call(
        section_keep_kernel,
        [((half, frames, ch), F32)],
        [gd, down_weight, other_down],
        flops=1 << 29,
    )

    row_scratch = pltpu.VMEM((pieces, cols), F32)
    if staged:
        parts = call(
            place_parts_kernel,
            [pair_block] * 4,
            [placing, mine, theirs],
            scratch=[row_scratch, pltpu.VMEM((slots, cols), BF)],
        )
        received = fan(parts[1:], DP, 2)
        flat_block = ((dp_count // 2 * capacity * cols // LANES, LANES), BF)
        send_o, keep_o = call(flat_columns_kernel, [flat_block, lane_block], [parts[0], *received])
        crossing = [send_o]
    else:
        (outgoing,) = call(
            place_kernel,
            [((slots, cols), BF)],
            [placing, mine, theirs],
            scratch=[row_scratch],
        )
        packed = all_to_all(outgoing)
        crossing = []

    blocks = 4 * (ch // hid)
    quarter = (blocks // 4 * hid, hid)
    e_own, *e_sends = call(
        residual_kernel,
        [(quarter, F32)] + [(quarter, BF)] * 3,
        [mask, keep_g, g_recv, sec, ahid, shid, res_out_weight, a1],
        scratch=[pltpu.VMEM((half, frames, hid), F32), pltpu.VMEM((blocks, hid, hid), F32)],
        flops=1 << 30,
    )
    received = fan(e_sends, MP, 1)
    e_own = plus(e_own, received)
    sent = e_own.astype(BF)

    own_u = gather_high(reduce_rest(keep_u, recv_u, me_dp, stages), me_dp, stages)
    own_s = gather_high(reduce_rest(keep_s, recv_s, me_dp, stages), me_dp, stages)
    all_u = [own_u] + fan([own_u] * 3, DP, stages[0][0])
    early = jnp.concatenate([own_u, own_s, sent])
    crossed = swap_bit(early, DP, 1)
    all_s = [own_s] + fan([own_s] * 3, DP, stages[0][0])
    their_u = swap_bit(jnp.concatenate(all_u[1:] + crossing), DP, 1)
    their_s = swap_bit(jnp.concatenate(all_s[1:]), DP, 1)
    size_u, size_s = own_u.shape[0], own_s.shape[0]
    received = [crossed[size_u + size_s :]]
    for bit, members in stages:
        e_own = plus(e_own, received)
        sent = e_own.astype(BF)
        received = fan([sent] * (members - 1), DP, bit)
    sent = plus(e_own, received).astype(BF)
    grad_res_in, grad_res_out = call(
        residual_finish_kernel,
        [((3 * ch, hid), F32), ((hid, ch), F32)],
        [sent, *fan([sent] * 3, MP, 1)],
        scratch=[pltpu.VMEM((4,) + quarter, F32)],
    )

    down_out = ((2 * STRIDE * ch, width), F32)
    proj_out = ((width, lat), F32)
    mine = tuple((k, 0, k, True) for k in range(4))

    def finish(shifted, ins, written, projected, before=()):
        n, m = len(ins), len(before)
        outs = [down_out] + [proj_out] * bool(projected)
        scratch = [
            pltpu.VMEM((len(written), ch, width), F32),
            pltpu.SemaphoreType.DMA((len(written),)),
        ]
        if projected:
            scratch += [
                pltpu.VMEM((len(projected), extra, width), F32),
                pltpu.SemaphoreType.DMA((len(projected),)),
            ]
        return call(
            functools.partial(finish_kernel, shifted, n, written, projected),
            outs,
            [*ins, *before],
            scratch=scratch,
            where={n + i: pltpu.HBM for i in range(m + len(outs))},
            aliases={n + i: i for i in range(m)},
        )

    far = range(1, 4)
    first = mine + ((4, size_u, 0, False),)
    grad_down, part = finish(True, [*all_s, crossed], first, first)
    second = mine + ((4, 0, 0, False),) + tuple((5, (k - 1) * size_u, k, False) for k in far)
    (grad_down,) = finish(False, [*all_u, crossed, their_u], second, (), [grad_down])
    last = tuple((0, (k - 1) * size_s, k, False) for k in far)
    grad_down, grad_proj = finish(True, [their_s], last, last, [grad_down, part])
    if staged:
        (packed,) = call(
            functools.partial(packed_kernel, 3 * size_u),
            [((slots, cols), BF)],
            [keep_o, their_u],
        )
    return (packed, grad_res_in, grad_res_out, grad_down, grad_proj)


def solution(mesh):
    return jax.shard_map(
        body,
        mesh=mesh,
        in_specs=(
            P(DP, None),
            P(DP),
            P(DP, None),
            P(),
            P(),
            P(None, MP),
            P(MP, None),
            P(DP, MP),
        ),
        out_specs=(P(DP, MP), P(), P(), P(None, MP), P(MP, None)),
        check_vma=False,
    )
```
